32 devices in a mesh: rows: 8 (over z, x), tm: 4 (over y, core).
Axes of the slice: x: 2, y: 2, z: 4, core: 2. Of those that a mesh axis runs over, the one named last changes fastest.
Arguments:
- features: bfloat16 [8, 1536, 1024], P('rows', 'tm'), may hold values from -6 to 6
- lengths: int32 [8], P('rows'), may hold values from 50 to 1536, as said below
- buckets: int32 [3071], replicated, may hold values from 0 to 63
- gain_first: float32 [1024], replicated, may hold values from 0.25 to 1.75
- first_in: bfloat16 [1024, 4096], replicated, may hold values from -0.1875 to 0.1875
- first_out: bfloat16 [4096, 1024], replicated, may hold values from -0.1875 to 0.1875
- gain_attend: float32 [1024], replicated, may hold values from 0.25 to 1.75
- query_weight: bfloat16 [1024, 1024], replicated, may hold values from -0.1875 to 0.1875
- key_weight: bfloat16 [1024, 1024], replicated, may hold values from -0.1875 to 0.1875
- value_weight: bfloat16 [1024, 1024], replicated, may hold values from -0.1875 to 0.1875
- output_weight: bfloat16 [1024, 1024], replicated, may hold values from -1 to 1
- bias_table: float32 [8, 64], replicated, may hold values from -4 to 4
- gain_conv: float32 [1024], replicated, may hold values from 0.25 to 1.75
- point_in: bfloat16 [1024, 2048], replicated, may hold values from -0.1875 to 0.1875
- depth_weight: float32 [5, 1024], replicated, may hold values from -2.5 to 2.5
- batch_scale: float32 [1024], replicated, may hold values from 0.25 to 1.75
- batch_shift: float32 [1024], replicated, may hold values from -3 to 3
- point_out: bfloat16 [1024, 1024], replicated, may hold values from -0.1875 to 0.1875
- gain_second: float32 [1024], replicated, may hold values from 0.25 to 1.75
- second_in: bfloat16 [1024, 4096], replicated, may hold values from -0.1875 to 0.1875
- second_out: bfloat16 [4096, 1024], replicated, may hold values from -0.1875 to 0.1875
- gain_final: float32 [1024], replicated, may hold values from 0.25 to 1.75
- cotangent: bfloat16 [8, 1536, 1024], P('rows', 'tm'), may hold values from -6 to 6
Outputs:
- output: bfloat16 [8, 1536, 1024], P('rows', 'tm')
- grad_features: bfloat16 [8, 1536, 1024], P('rows', 'tm')
- grad_gain_first: float32 [1024], P('rows')
- grad_first_in: float32 [1024, 4096], P('rows')
- grad_first_out: float32 [4096, 1024], P('rows')
- grad_gain_attend: float32 [1024], P('rows')
- grad_query: float32 [1024, 1024], P('rows')
- grad_key: float32 [1024, 1024], P('rows')
- grad_value: float32 [1024, 1024], P('rows')
- grad_output: float32 [1024, 1024], P('rows')
- grad_table: float32 [8, 64], replicated
- grad_gain_conv: float32 [1024], P('rows')
- grad_point_in: float32 [1024, 2048], P('rows')
- grad_depth: float32 [5, 1024], replicated
- grad_batch_scale: float32 [1024], replicated
- grad_batch_shift: float32 [1024], replicated
- grad_point_out: float32 [1024, 1024], P('rows')
- grad_gain_second: float32 [1024], P('rows')
- grad_second_in: float32 [1024, 4096], P('rows')
- grad_second_out: float32 [4096, 1024], P('rows')
- grad_gain_final: float32 [1024], P('rows')
The draws below stay inside these ranges and needn't reach their ends.
Inputs may be any that keep to these rules, and one draw needn't show every extreme that they name: `lengths`: in each aligned pair of rows (rows 2k and 2k + 1) one row, drawn from the seed, holds all 1536 frames.
All inputs are finite; a program needn't handle non-finite values.
Results may differ from the reference program's by a relative error of at most 0.02.
Values may be sent and summed in bfloat16 or wider, within the bound.
No kernel may reach another device: no remote copies, remote signals or barrier semaphores. Data moves between devices by JAX's collectives and lax.ppermute only.
A program may use at most 448 MiB of HBM per device.

```python
import jax
import jax.numpy as jnp
from jax import lax

D = 1024
FF = 4096
HEADS = 8
KW = 5
NB = 64
MIN_LEN = 50
FRAMES = 1536
BATCH = 8


def draw_lengths(key, part):
    first = jax.random.fold_in(key, 101)
    second = jax.random.fold_in(key, 202)
    ragged = jax.random.randint(first, (BATCH,), MIN_LEN, FRAMES + 1)
    chosen = jax.random.randint(second, (BATCH // 2, 1), 0, 2)
    slots = jnp.arange(2)[None, :]
    full = (slots == chosen).reshape(BATCH)
    return jnp.where(full, FRAMES, ragged).astype(jnp.int32)


def with_ends(drawn, rng, smallest, largest):
    index_at = [jax.random.randint(jax.random.fold_in(rng, axis), (), 0, length) for axis, length in enumerate(drawn.shape)]
    main_axis = drawn.shape.index(max(drawn.shape))
    neighbour = index_at[:main_axis] + [(index_at[main_axis] + 1) % drawn.shape[main_axis]] + index_at[main_axis + 1:]
    return drawn.at[tuple(index_at)].set(smallest).at[tuple(neighbour)].set(largest)


def strengthened(drawn, own_key, source, target, blocks, factor):
    owner, partner = [(jnp.arange(drawn.shape[dim]) // (drawn.shape[dim] // blocks)).reshape([-1 if axis == dim else 1 for axis in range(drawn.ndim)]) for dim in (source, target)]
    chosen = jax.random.permutation(own_key, blocks)[partner]
    strong = (owner == chosen) | (owner == (partner + blocks // 2) % blocks)
    return jnp.where(strong, factor * drawn, drawn)


def levels(stream_key, extent, split, low, top_value):
    def one(position, shards_of):
        heights = jax.random.uniform(jax.random.fold_in(jax.random.fold_in(stream_key, 6), position), (shards_of,), jnp.float32, low / len(split), top_value / len(split))
        return jnp.repeat(jnp.exp(heights), extent[position] // shards_of).reshape((-1,) + (1,) * (len(extent) - position - 1))

    factor_of = one(*split[0])
    for cut in split[1:]:
        factor_of = factor_of * one(*cut)
    return factor_of


def gaussian(rng, dims, deviation, limit, shards=(), kind=jnp.bfloat16):
    entries = deviation * jax.random.normal(rng, dims, jnp.float32)
    if shards:
        entries = entries * levels(rng, dims, shards, -0.22, 0.18)
    return jnp.clip(entries, -limit, limit).astype(kind)


def heavy_noise(own_key, shape, deviation, limit, split, heavy, kind=jnp.bfloat16):
    values = deviation * jax.random.normal(own_key, shape, jnp.float32)
    if split:
        values = values * levels(own_key, shape, split, -0.22, 0.18)
    return jnp.clip(strengthened(values, jax.random.fold_in(own_key, 3), *heavy), -limit, limit).astype(kind)


def setup_inputs(seed: int = 0) -> dict:
    streams_of = jax.random.split(jax.random.key(seed), 24)
    return {
        "features": gaussian(streams_of[0], (BATCH, FRAMES, D), 1.0, 6.0, ((0, 8), (1, 4))),
        "lengths": draw_lengths(jax.random.fold_in(streams_of[23], 71), 0),
        "buckets": with_ends(jax.random.randint(streams_of[2], (2 * FRAMES - 1,), 0, NB), jax.random.fold_in(streams_of[2], 1), 0, NB - 1).astype(jnp.int32),
        "gain_first": jnp.clip(1.0 + 0.15 * jax.random.normal(streams_of[3], (D,), jnp.float32), 0.25, 1.75),
        "first_in": gaussian(streams_of[4], (D, FF), D ** -0.5, 0.1875),
        "first_out": gaussian(streams_of[5], (FF, D), (FF // 4) ** -0.5, 0.1875),
        "gain_attend": jnp.clip(1.0 + 0.15 * jax.random.normal(streams_of[6], (D,), jnp.float32), 0.25, 1.75),
        "query_weight": gaussian(streams_of[7], (D, D), D ** -0.5, 0.1875),
        "key_weight": gaussian(streams_of[8], (D, D), D ** -0.5, 0.1875),
        "value_weight": gaussian(streams_of[9], (D, D), D ** -0.5, 0.1875),
        "output_weight": gaussian(streams_of[10], (D, D), (D // 32) ** -0.5, 1.0),
        "bias_table": gaussian(streams_of[11], (HEADS, NB), 1.0, 4.0, (), jnp.float32),
        "gain_conv": jnp.clip(1.0 + 0.15 * jax.random.normal(streams_of[12], (D,), jnp.float32), 0.25, 1.75),
        "point_in": gaussian(streams_of[13], (D, 2 * D), D ** -0.5, 0.1875),
        "depth_weight": gaussian(streams_of[14], (KW, D), KW ** -0.5, 2.5, (), jnp.float32),
        "batch_scale": jnp.clip(1.0 + 0.15 * jax.random.normal(streams_of[15], (D,), jnp.float32), 0.25, 1.75),
        "batch_shift": gaussian(streams_of[16], (D,), 0.5, 3.0, (), jnp.float32),
        "point_out": gaussian(streams_of[17], (D, D), D ** -0.5, 0.1875),
        "gain_second": jnp.clip(1.0 + 0.15 * jax.random.normal(streams_of[18], (D,), jnp.float32), 0.25, 1.75),
        "second_in": gaussian(streams_of[19], (D, FF), D ** -0.5, 0.1875),
        "second_out": gaussian(streams_of[20], (FF, D), (FF // 4) ** -0.5, 0.1875),
        "gain_final": jnp.clip(1.0 + 0.15 * jax.random.normal(streams_of[21], (D,), jnp.float32), 0.25, 1.75),
        "cotangent": heavy_noise(streams_of[22], (BATCH, FRAMES, D), 1.0, 6.0, ((0, 8), (1, 4)), (0, 2, 8, 2.0)),
    }


EPS = 1e-05
NEGATIVE = -1e+30

@jax.custom_vjp
def low(v):
    return lax.optimization_barrier(v.astype(jnp.bfloat16)).astype(jnp.float32)

@jax.custom_vjp
def low_back(v):
    return v

def low_keep(v):
    return (low(v), None)

def low_pass(kept, grad):
    return (grad,)

def back_keep(v):
    return (v, None)

def back_low(kept, grad):
    return (low(grad),)
low.defvjp(low_keep, low_pass)
low_back.defvjp(back_keep, back_low)

def matmul(left, right):
    return jnp.dot(left, right, precision=lax.Precision.HIGHEST)

def layer_norm(values, gain):
    mean = lax.optimization_barrier(jnp.mean(values, axis=-1, keepdims=True))
    centered = values - mean
    return centered * lax.rsqrt(lax.optimization_barrier(jnp.mean(centered * centered, axis=-1, keepdims=True)) + EPS) * gain

def feed_forward(values, gain, weight_in, weight_out):
    normed = low(layer_norm(values, gain))
    hidden = low_back(matmul(normed, weight_in))
    branch = low_back(matmul(low(jax.nn.silu(hidden)), weight_out))
    return values + 0.5 * branch

def attention(values, gain, query_weight, key_weight, value_weight, output_weight, bias, live):
    head_dim = D // HEADS
    normed = low(layer_norm(values, gain))

    def split_heads(weight):
        projected = low(low_back(matmul(normed, weight)))
        return projected.reshape(FRAMES, HEADS, head_dim)
    query = split_heads(query_weight)
    key = split_heads(key_weight)
    value = split_heads(value_weight)
    scores = jnp.einsum('qhd,khd->hqk', query, key, precision=lax.Precision.HIGHEST) * head_dim ** (-0.5) + bias
    scores = low_back(scores)
    masked = jnp.where(live, scores, NEGATIVE)
    top = lax.optimization_barrier(jnp.max(masked, axis=-1, keepdims=True))
    weights = jnp.where(live, jnp.exp(masked - top), 0.0)
    probs = weights / lax.optimization_barrier(jnp.sum(weights, axis=-1, keepdims=True))
    mixed = jnp.einsum('hqk,khd->qhd', low(probs), value, precision=lax.Precision.HIGHEST).reshape(FRAMES, D)
    mixed = low(low_back(mixed))
    return low_back(matmul(mixed, output_weight))

def depthwise(gated, depth_weight):
    half = KW // 2
    padded = jnp.pad(gated, ((half, half), (0, 0)))
    filtered = jnp.zeros_like(gated)
    for tap in range(KW):
        filtered = filtered + depth_weight[tap] * padded[tap:tap + FRAMES]
    return filtered

def forward(params, features, lengths, buckets):
    gain_first, first_in, first_out, gain_attend, query_weight, key_weight, value_weight, output_weight, bias_table, gain_conv, point_in, depth_weight, batch_scale, batch_shift, point_out, gain_second, second_in, second_out, gain_final = params
    offsets = jnp.arange(FRAMES)[None, :] - jnp.arange(FRAMES)[:, None] + FRAMES - 1
    bias = bias_table[:, buckets[offsets]]

    def first_part(row):
        values, length = row
        live_keys = jnp.arange(FRAMES) < length
        values = feed_forward(values, gain_first, first_in, first_out)
        values = values + attention(values, gain_attend, query_weight, key_weight, value_weight, output_weight, bias, live_keys[None, None, :])
        valid = live_keys.astype(jnp.float32)[:, None]
        normed = low(layer_norm(values, gain_conv))
        joined = low_back(matmul(normed, point_in))
        gated = joined[:, :D] * jax.nn.sigmoid(joined[:, D:]) * valid
        return (values, depthwise(gated, depth_weight))
    middles, filtered = lax.map(jax.checkpoint(first_part), (features, lengths))
    valid = (jnp.arange(FRAMES)[None, :] < lengths[:, None]).astype(jnp.float32)[:, :, None]
    count = jnp.sum(valid)
    batch_mean = lax.optimization_barrier(jnp.sum(filtered * valid, axis=(0, 1))) / count
    centered = (filtered - batch_mean) * valid
    batch_var = lax.optimization_barrier(jnp.sum(centered * centered, axis=(0, 1))) / count
    rstd = lax.rsqrt(batch_var + EPS)

    def second_part(row):
        values, conv_out, length = row
        row_valid = (jnp.arange(FRAMES) < length).astype(jnp.float32)[:, None]
        normalized = (conv_out - batch_mean) * rstd * batch_scale + batch_shift
        branch = low_back(matmul(low(jax.nn.silu(normalized)), point_out))
        values = feed_forward(values + branch, gain_second, second_in, second_out)
        return layer_norm(values, gain_final) * row_valid
    return lax.map(jax.checkpoint(second_part), (middles, filtered, lengths))

def reference(features, lengths, buckets, gain_first, first_in, first_out, gain_attend, query_weight, key_weight, value_weight, output_weight, bias_table, gain_conv, point_in, depth_weight, batch_scale, batch_shift, point_out, gain_second, second_in, second_out, gain_final, cotangent):
    params = (gain_first, first_in, first_out, gain_attend, query_weight, key_weight, value_weight, output_weight, bias_table, gain_conv, point_in, depth_weight, batch_scale, batch_shift, point_out, gain_second, second_in, second_out, gain_final)
    params = tuple((item.astype(jnp.float32) for item in params))

    def run(weights, inputs):
        return forward(weights, inputs, lengths, buckets)
    result, pullback = jax.vjp(run, params, features.astype(jnp.float32))
    grads, grad_inputs = pullback(cotangent.astype(jnp.float32))
    grad_gain_first, grad_first_in, grad_first_out, grad_gain_attend, grad_query, grad_key, grad_value, grad_output, grad_table, grad_gain_conv, grad_point_in, grad_depth, grad_batch_scale, grad_batch_shift, grad_point_out, grad_gain_second, grad_second_in, grad_second_out, grad_gain_final = grads
    return (result.astype(jnp.bfloat16), grad_inputs.astype(jnp.bfloat16), grad_gain_first, grad_first_in, grad_first_out, grad_gain_attend, grad_query, grad_key, grad_value, grad_output, grad_table, grad_gain_conv, grad_point_in, grad_depth, grad_batch_scale, grad_batch_shift, grad_point_out, grad_gain_second, grad_second_in, grad_second_out, grad_gain_final)
```

```python
import functools

import jax
import jax.numpy as jnp
from jax import lax
from jax.experimental import pallas as pl
from jax.experimental.pallas import tpu as pltpu
from jax.sharding import PartitionSpec as P

EPS = 1e-05
NEGATIVE = -1e30
LANES = 128
QUERY_TILE = 256
VMEM_LIMIT = 56 * 1024 * 1024


def swap(value, axis, bit):
    count = lax.axis_size(axis)
    return lax.ppermute(value, axis, [(i, i ^ bit) for i in range(count)])


def matmul(left, right):
    return jnp.dot(left, right, preferred_element_type=jnp.float32)


def back_prop(grad, weight):
    return lax.dot_general(
        grad, weight, (((1,), (1,)), ((), ())), preferred_element_type=jnp.float32
    )


def weight_grad(inputs, grad):
    return lax.dot_general(
        inputs, grad, (((0,), (0,)), ((), ())), preferred_element_type=jnp.float32
    ).astype(jnp.bfloat16)


def norm_forward(values, gain):
    mean = jnp.mean(values, axis=-1, keepdims=True)
    centered = values - mean
    rstd = lax.rsqrt(jnp.mean(centered * centered, axis=-1, keepdims=True) + EPS)
    scaled = centered * rstd
    return (scaled * gain, scaled, rstd)


def norm_backward(grad, scaled, rstd, gain):
    weighted = grad * gain
    inner = weighted - jnp.mean(weighted, axis=-1, keepdims=True)
    inner = inner - scaled * jnp.mean(weighted * scaled, axis=-1, keepdims=True)
    return (rstd * inner, jnp.sum(grad * scaled, axis=0))


def silu_slope(hidden):
    sigma = jax.nn.sigmoid(hidden)
    return sigma * (1.0 + hidden * (1.0 - sigma))


def ordered(first_is_lower, mine, other):
    low = jnp.where(first_is_lower, mine, other)
    high = jnp.where(first_is_lower, other, mine)
    return jnp.concatenate([low, high], axis=0)


def mesh_sum(value):
    for axis in ("tm", "rows"):
        bit = 1
        while bit < lax.axis_size(axis):
            value = value + swap(value, axis, bit)
            bit *= 2
    return value


def mesh_moments(count, mean, spread):
    for axis in ("tm", "rows"):
        bit = 1
        while bit < lax.axis_size(axis):
            sent = jnp.concatenate([mean[None], spread[None], jnp.broadcast_to(count, (1, mean.shape[0]))])
            got = swap(sent, axis, bit)
            other_mean, other_spread, other_count = got[0], got[1], got[2]
            total = count + other_count
            safe = jnp.maximum(total, 1.0)
            gap = other_mean - mean
            spread = spread + other_spread + gap * gap * (count * other_count / safe)
            mean = (count * mean + other_count * other_mean) / safe
            count = total
            bit *= 2
    return (count, mean, spread)


def reduce_rows(partial):
    size = lax.axis_size("rows")
    place = lax.axis_index("rows")
    left = partial.reshape(size, partial.shape[0] // size, partial.shape[1])
    bit = 1
    while left.shape[0] > 1:
        pairs = left.reshape(left.shape[0] // 2, 2, left.shape[1], left.shape[2])
        mine = (place // bit) % 2
        keep = lax.dynamic_index_in_dim(pairs, mine, 1, keepdims=False)
        send = lax.dynamic_index_in_dim(pairs, 1 - mine, 1, keepdims=False)
        got = swap(send, "rows", bit)
        left = (keep.astype(jnp.float32) + got.astype(jnp.float32)).astype(jnp.bfloat16)
        bit *= 2
    return left[0]


def spread_tm(piece):
    near = swap(piece, "tm", 1)
    far = swap(piece, "tm", 2)
    return [piece, near, far, swap(far, "tm", 1)]


def take_kernel(place, source, target):
    target[...] = source[...]


def take_columns(weight, groups, place, parts):
    model, total = weight.shape
    block = total // groups // parts
    if block % LANES:
        cut = weight.reshape(model, groups, parts, block)
        return lax.dynamic_index_in_dim(cut, place, 2, keepdims=False).reshape(model, -1)
    return pl.pallas_call(
        take_kernel,
        out_shape=jax.ShapeDtypeStruct((model, total // parts), weight.dtype),
        grid_spec=pltpu.PrefetchScalarGridSpec(
            num_scalar_prefetch=1,
            grid=(groups,),
            in_specs=[pl.BlockSpec((model, block), lambda g, at: (0, g * parts + at[0]))],
            out_specs=pl.BlockSpec((model, block), lambda g, at: (0, g)),
        ),
        name="take_columns",
    )(place.reshape(1), weight)


def take_rows(weight, groups, place, parts):
    total, model = weight.shape
    cut = weight.reshape(groups, parts, total // groups // parts, model)
    return lax.dynamic_index_in_dim(cut, place, 1, keepdims=False).reshape(-1, model)


def lay_kernel(widths, groups, places, *refs):
    parts = 4
    pieces, targets = refs[:parts], refs[parts:]
    for k in range(parts):
        begin = 0
        for width, target in zip(widths, targets, strict=True):
            block = width // groups
            for g in range(groups):
                at = pl.multiple_of((g * parts + places[k]) * block, LANES)
                source = pieces[k][:, begin + g * block : begin + (g + 1) * block]
                target[:, pl.ds(at, block)] = source.astype(jnp.float32)
            begin += width


def lay_columns(pieces, widths, groups, places):
    rows = pieces[0].shape[0]
    parts = len(pieces)
    if any((width // groups) % LANES for width in widths):
        outs, begin = [], 0
        stacked = jnp.zeros((parts, *pieces[0].shape), pieces[0].dtype)
        for k in range(parts):
            stacked = lax.dynamic_update_index_in_dim(stacked, pieces[k], places[k], 0)
        for width in widths:
            cut = stacked[:, :, begin : begin + width].reshape(parts, rows, groups, width // groups)
            outs.append(cut.transpose(1, 2, 0, 3).reshape(rows, parts * width).astype(jnp.float32))
            begin += width
        return outs
    return pl.pallas_call(
        functools.partial(lay_kernel, widths, groups),
        out_shape=[jax.ShapeDtypeStruct((rows, parts * width), jnp.float32) for width in widths],
        grid_spec=pltpu.PrefetchScalarGridSpec(
            num_scalar_prefetch=1,
            grid=(1,),
            in_specs=[pl.BlockSpec(p.shape, lambda i, at: (0, 0)) for p in pieces],
            out_specs=[pl.BlockSpec((rows, parts * width), lambda i, at: (0, 0)) for width in widths],
        ),
        compiler_params=pltpu.CompilerParams(vmem_limit_bytes=VMEM_LIMIT),
        name="lay_columns",
    )(places, *pieces)


def skew_kernel(line, out):
    length = line.shape[-1]
    width = out.shape[-1]
    spread = jnp.broadcast_to(line[0], (LANES, length))
    rolled = pltpu.roll(spread, length - (LANES - 1), 1, stride=1, stride_axis=0)
    out[0] = rolled[:, :width]


def skewed(lines):
    heads, _, length = lines.shape
    width = length - LANES
    return pl.pallas_call(
        skew_kernel,
        out_shape=jax.ShapeDtypeStruct((heads, LANES, width), jnp.float32),
        grid=(heads,),
        in_specs=[pl.BlockSpec((1, 1, length), lambda h: (h, 0, 0))],
        out_specs=pl.BlockSpec((1, LANES, width), lambda h: (h, 0, 0)),
        name="bias_rows",
    )(lines)


def attend_kernel(scale, at, q_ref, k_ref, v_ref, bias_ref, out_ref, lse_ref, vt_ref, s_ref, p_ref):
    tile = q_ref.shape[0]
    blocks = k_ref.shape[0] // LANES
    length = at[blocks * 2]

    @pl.when(pl.program_id(1) == 0)
    def _():
        vt_ref[...] = v_ref[...].T

    begin = pl.program_id(1) * tile
    s_ref[...] = lax.dot_general(
        k_ref[...], q_ref[...], (((1,), (1,)), ((), ())), preferred_element_type=jnp.float32
    )
    frame = lax.broadcasted_iota(jnp.int32, (LANES, tile), 0)
    top = jnp.full((1, tile), NEGATIVE, jnp.float32)
    for b in range(blocks):
        lanes = pl.ds(pl.multiple_of(at[b] + begin, LANES), tile)
        s = s_ref[b * LANES : (b + 1) * LANES] * scale + bias_ref[0, :, lanes]
        s = jnp.where(frame < length - at[blocks + b], s, NEGATIVE)
        s_ref[b * LANES : (b + 1) * LANES] = s
        top = jnp.maximum(top, jnp.max(s, axis=0, keepdims=True))
    total = jnp.zeros((1, tile), jnp.float32)
    for b in range(blocks):
        p = jnp.exp(s_ref[b * LANES : (b + 1) * LANES] - top)
        total = total + jnp.sum(p, axis=0, keepdims=True)
        p_ref[b * LANES : (b + 1) * LANES] = p.astype(jnp.bfloat16)
    mixed = jnp.dot(vt_ref[...], p_ref[...], preferred_element_type=jnp.float32) / total
    out_ref[...] = mixed.T.astype(jnp.bfloat16)
    lse_ref[0] = top + jnp.log(total)


def attend(at, query, keyval, bias, heads, head_dim):
    queries, keys = query.shape[0], keyval.shape[0]
    tile = QUERY_TILE
    width = bias.shape[-1]
    grid_spec = pltpu.PrefetchScalarGridSpec(
        num_scalar_prefetch=1,
        grid=(heads, queries // tile),
        in_specs=[
            pl.BlockSpec((tile, head_dim), lambda h, i, at: (i, h)),
            pl.BlockSpec((keys, head_dim), lambda h, i, at: (0, h)),
            pl.BlockSpec((keys, head_dim), lambda h, i, at: (0, heads + h)),
            pl.BlockSpec((1, LANES, width), lambda h, i, at: (h, 0, 0)),
        ],
        out_specs=[
            pl.BlockSpec((tile, head_dim), lambda h, i, at: (i, h)),
            pl.BlockSpec((1, 1, tile), lambda h, i, at: (h, 0, i)),
        ],
        scratch_shapes=[
            pltpu.VMEM((head_dim, keys), jnp.bfloat16),
            pltpu.VMEM((keys, tile), jnp.float32),
            pltpu.VMEM((keys, tile), jnp.bfloat16),
        ],
    )
    return pl.pallas_call(
        functools.partial(attend_kernel, head_dim ** (-0.5)),
        out_shape=[
            jax.ShapeDtypeStruct((queries, heads * head_dim), jnp.bfloat16),
            jax.ShapeDtypeStruct((heads, 1, queries), jnp.float32),
        ],
        grid_spec=grid_spec,
        compiler_params=pltpu.CompilerParams(vmem_limit_bytes=VMEM_LIMIT),
        cost_estimate=pl.CostEstimate(
            flops=4 * heads * queries * keys * head_dim,
            transcendentals=heads * queries * keys,
            bytes_accessed=4 * heads * LANES * width + 4 * heads * head_dim * (queries + keys),
        ),
        name="attend",
    )(at, query, keyval, keyval, bias)


def attend_back_kernel(
    scale, at, q_ref, k_ref, v_ref, do_ref, lse_ref, bias_ref,
    dq_ref, dk_ref, dv_ref, line_ref,
    kt_ref, s_ref, dp_ref, p_ref, ds_ref, dk_sum, dv_sum, skew_ref,
):
    tile = q_ref.shape[0]
    blocks = k_ref.shape[0] // LANES
    length = at[blocks * 2]

    @pl.when(pl.program_id(1) == 0)
    def _():
        kt_ref[...] = k_ref[...].T
        dk_sum[...] = jnp.zeros_like(dk_sum)
        dv_sum[...] = jnp.zeros_like(dv_sum)
        skew_ref[...] = jnp.zeros_like(skew_ref)

    begin = pl.program_id(1) * tile
    s_ref[...] = lax.dot_general(
        k_ref[...], q_ref[...], (((1,), (1,)), ((), ())), preferred_element_type=jnp.float32
    )
    dp_ref[...] = lax.dot_general(
        v_ref[...], do_ref[...], (((1,), (1,)), ((), ())), preferred_element_type=jnp.float32
    )
    frame = lax.broadcasted_iota(jnp.int32, (LANES, tile), 0)
    lse = lse_ref[0]
    delta = jnp.zeros((1, tile), jnp.float32)
    for b in range(blocks):
        rows = slice(b * LANES, (b + 1) * LANES)
        lanes = pl.ds(pl.multiple_of(at[b] + begin, LANES), tile)
        s = s_ref[rows] * scale + bias_ref[0, :, lanes]
        s = jnp.where(frame < length - at[blocks + b], s, NEGATIVE)
        p = jnp.exp(s - lse)
        s_ref[rows] = p
        p_ref[rows] = p.astype(jnp.bfloat16)
        delta = delta + jnp.sum(p * dp_ref[rows], axis=0, keepdims=True)
    for b in range(blocks):
        rows = slice(b * LANES, (b + 1) * LANES)
        lanes = pl.ds(pl.multiple_of(at[b] + begin, LANES), tile)
        ds = (s_ref[rows] * (dp_ref[rows] - delta)).astype(jnp.bfloat16)
        ds_ref[rows] = ds
        skew_ref[:, lanes] += ds.astype(jnp.float32)
    dv_sum[...] += jnp.dot(p_ref[...], do_ref[...], preferred_element_type=jnp.float32)
    dk_sum[...] += jnp.dot(ds_ref[...], q_ref[...], preferred_element_type=jnp.float32)
    dq = jnp.dot(kt_ref[...], ds_ref[...], preferred_element_type=jnp.float32) * scale
    dq_ref[...] = dq.T.astype(jnp.bfloat16)

    @pl.when(pl.program_id(1) == pl.num_programs(1) - 1)
    def _():
        dk_ref[...] = (dk_sum[...] * scale).astype(jnp.bfloat16)
        dv_ref[...] = dv_sum[...].astype(jnp.bfloat16)
        lines = jnp.concatenate([skew_ref[...], jnp.zeros((LANES, LANES), jnp.float32)], axis=1)
        count = LANES // 2
        while count >= 8:
            lines = lines[count:] + pltpu.roll(lines[:count], count, 1)
            count //= 2
        line_ref[0] = lines


def attend_back(at, query, keyval, grad, lse, bias, heads, head_dim):
    queries, keys = query.shape[0], keyval.shape[0]
    tile = QUERY_TILE
    width = bias.shape[-1]
    grid_spec = pltpu.PrefetchScalarGridSpec(
        num_scalar_prefetch=1,
        grid=(heads, queries // tile),
        in_specs=[
            pl.BlockSpec((tile, head_dim), lambda h, i, at: (i, h)),
            pl.BlockSpec((keys, head_dim), lambda h, i, at: (0, h)),
            pl.BlockSpec((keys, head_dim), lambda h, i, at: (0, heads + h)),
            pl.BlockSpec((tile, head_dim), lambda h, i, at: (i, h)),
            pl.BlockSpec((1, 1, tile), lambda h, i, at: (h, 0, i)),
            pl.BlockSpec((1, LANES, width), lambda h, i, at: (h, 0, 0)),
        ],
        out_specs=[
            pl.BlockSpec((tile, head_dim), lambda h, i, at: (i, h)),
            pl.BlockSpec((keys, head_dim), lambda h, i, at: (0, h)),
            pl.BlockSpec((keys, head_dim), lambda h, i, at: (0, h)),
            pl.BlockSpec((1, 8, width + LANES), lambda h, i, at: (h, 0, 0)),
        ],
        scratch_shapes=[
            pltpu.VMEM((head_dim, keys), jnp.bfloat16),
            pltpu.VMEM((keys, tile), jnp.float32),
            pltpu.VMEM((keys, tile), jnp.float32),
            pltpu.VMEM((keys, tile), jnp.bfloat16),
            pltpu.VMEM((keys, tile), jnp.bfloat16),
            pltpu.VMEM((keys, head_dim), jnp.float32),
            pltpu.VMEM((keys, head_dim), jnp.float32),
            pltpu.VMEM((LANES, width), jnp.float32),
        ],
    )
    return pl.pallas_call(
        functools.partial(attend_back_kernel, head_dim ** (-0.5)),
        out_shape=[
            jax.ShapeDtypeStruct((queries, heads * head_dim), jnp.bfloat16),
            jax.ShapeDtypeStruct((keys, heads * head_dim), jnp.bfloat16),
            jax.ShapeDtypeStruct((keys, heads * head_dim), jnp.bfloat16),
            jax.ShapeDtypeStruct((heads, 8, width + LANES), jnp.float32),
        ],
        grid_spec=grid_spec,
        compiler_params=pltpu.CompilerParams(vmem_limit_bytes=VMEM_LIMIT),
        cost_estimate=pl.CostEstimate(
            flops=10 * heads * queries * keys * head_dim,
            transcendentals=heads * queries * keys,
            bytes_accessed=4 * heads * LANES * width + 8 * heads * head_dim * (queries + keys),
        ),
        name="attend_back",
    )(at, query, keyval, keyval, grad, lse, bias)


def ffn_forward(values, gain, weight_in, weight_out):
    normed, scaled, rstd = norm_forward(values, gain)
    act_in = normed.astype(jnp.bfloat16)
    hidden = matmul(act_in, weight_in)
    act_mid = jax.nn.silu(hidden).astype(jnp.bfloat16)
    slope = silu_slope(hidden).astype(jnp.bfloat16)
    return (values + 0.5 * matmul(act_mid, weight_out), (act_in, slope, scaled, rstd))


def ffn_backward(grad, kept, gain, weight_in, weight_out):
    act_in, slope, scaled, rstd = kept
    d_branch = (0.5 * grad).astype(jnp.bfloat16)
    d_hidden = (back_prop(d_branch, weight_out) * slope.astype(jnp.float32)).astype(jnp.bfloat16)
    d_values, grad_gain = norm_backward(back_prop(d_hidden, weight_in), scaled, rstd, gain)
    return (grad + d_values, grad_gain, d_branch)


def ffn_again(act_all, part_in):
    hidden = matmul(act_all, part_in)
    return (jax.nn.silu(hidden).astype(jnp.bfloat16), silu_slope(hidden).astype(jnp.bfloat16))


def ffn_weight_grads(act_all, again, branch_all, part_out):
    act_mid, slope = again
    grad_out = reduce_rows(weight_grad(act_mid, branch_all))
    d_hidden = (back_prop(branch_all, part_out) * slope.astype(jnp.float32)).astype(jnp.bfloat16)
    grad_in = reduce_rows(weight_grad(act_all, d_hidden))
    return (spread_tm(grad_in), spread_tm(grad_out))


def shards(
    features,
    lengths,
    buckets,
    gain_first,
    first_in,
    first_out,
    gain_attend,
    query_weight,
    key_weight,
    value_weight,
    output_weight,
    bias_table,
    gain_conv,
    point_in,
    depth_weight,
    batch_scale,
    batch_shift,
    point_out,
    gain_second,
    second_in,
    second_out,
    gain_final,
    cotangent,
):
    row_count, width, model = features.shape
    tokens = row_count * width
    heads, bucket_count = bias_table.shape
    head_dim = model // heads
    parts = lax.axis_size("tm")
    groups = lax.axis_size("rows")
    frames = width * parts
    half = depth_weight.shape[0] // 2
    taps = depth_weight.shape[0]
    place = lax.axis_index("tm")
    row_place = lax.axis_index("rows")
    side = place % 2
    far = place // 2
    is_low = side == 0
    offset = place * width
    near_heads = heads // 2
    near_width = near_heads * head_dim
    pair = 2 * width
    valid_flat = ((offset + jnp.arange(width)) < lengths[0]).astype(jnp.float32).reshape(tokens, 1)

    def near_half(array, axis, index):
        size = array.shape[axis] // 2
        return lax.dynamic_slice_in_dim(array, index * size, size, axis)

    near_table = lax.dynamic_slice_in_dim(bias_table, side * near_heads, near_heads, 0)
    span = pair + frames
    turned = jnp.pad(buckets[::-1], (0, 1), constant_values=-1)
    window = lax.dynamic_slice_in_dim(turned, far * pair, span, 0)
    one_hot = (window[:, None] == jnp.arange(bucket_count)[None, :]).astype(jnp.float32)
    bias_lines = lax.dot_general(
        near_table, one_hot, (((1,), (1,)), ((), ())), precision=lax.Precision.HIGHEST
    )
    bias = skewed(bias_lines[:, None, :])
    key_blocks = frames // LANES
    block = jnp.arange(key_blocks)
    block = (block + far * (key_blocks // 2)) % key_blocks
    at = jnp.concatenate(
        [frames - LANES - LANES * block, LANES * block, lengths[:1]]
    ).astype(jnp.int32)

    state = features.astype(jnp.float32).reshape(tokens, model)
    state, kept_first = ffn_forward(state, gain_first, first_in, first_out)

    normed, scaled_attend, rstd_attend = norm_forward(state, gain_attend)
    act_attend = normed.astype(jnp.bfloat16)
    act_near, act_far = swap(act_attend, "tm", 1), swap(act_attend, "tm", 2)
    act_pair = ordered(is_low, act_attend, act_near)
    act_all = jnp.concatenate([act_pair, ordered(is_low, act_far, swap(act_far, "tm", 1))], axis=0)
    near_query = near_half(query_weight, 1, side)
    near_keyval = jnp.concatenate(
        [near_half(key_weight, 1, side), near_half(value_weight, 1, side)], axis=1
    )
    query = matmul(act_pair, near_query).astype(jnp.bfloat16)
    keyval = matmul(act_all, near_keyval).astype(jnp.bfloat16)
    mixed, lse = attend(at, query, keyval, bias, near_heads, head_dim)
    own_mixed = near_half(mixed, 0, side)
    other_mixed = swap(near_half(mixed, 0, 1 - side), "tm", 1)
    attended = jnp.concatenate(
        [jnp.where(is_low, own_mixed, other_mixed), jnp.where(is_low, other_mixed, own_mixed)], axis=1
    )
    state = state + matmul(attended, output_weight)

    normed, scaled_conv, rstd_conv = norm_forward(state, gain_conv)
    act_conv = normed.astype(jnp.bfloat16)
    joined = matmul(act_conv, point_in)
    joined_value = joined[:, :model]
    gate_sig = jax.nn.sigmoid(joined[:, model:])
    gated = joined_value * gate_sig * valid_flat
    up = [(i, i + 1) for i in range(parts - 1)]
    down = [(j, i) for i, j in up]

    def rimmed_of(value):
        low = value.astype(jnp.bfloat16)
        before = lax.ppermute(low[width - half :], "tm", up).astype(jnp.float32)
        after = lax.ppermute(low[:half], "tm", down).astype(jnp.float32)
        return jnp.concatenate([before, value, after], axis=0)

    rimmed = rimmed_of(gated)
    filtered = jnp.zeros_like(gated)
    for tap in range(taps):
        filtered = filtered + depth_weight[tap] * rimmed[tap : tap + width]
    local_count = jnp.sum(valid_flat)
    local_mean = jnp.sum(filtered * valid_flat, axis=0) / jnp.maximum(local_count, 1.0)
    local_gap = (filtered - local_mean) * valid_flat
    count, batch_mean, spread = mesh_moments(local_count, local_mean, jnp.sum(local_gap * local_gap, axis=0))
    count = count[0]
    rstd_batch = lax.rsqrt(spread / count + EPS)
    scaled_batch = (filtered - batch_mean) * rstd_batch
    normalized = scaled_batch * batch_scale + batch_shift
    act_batch = jax.nn.silu(normalized).astype(jnp.bfloat16)
    state = state + matmul(act_batch, point_out)
    state, kept_second = ffn_forward(state, gain_second, second_in, second_out)
    normed, scaled_final, rstd_final = norm_forward(state, gain_final)
    output = (normed * valid_flat).astype(jnp.bfloat16).reshape(row_count, width, model)

    act_first_all = jnp.concatenate(spread_tm(kept_first[0]), axis=0)
    act_second_all = jnp.concatenate(spread_tm(kept_second[0]), axis=0)
    part_first_in = take_columns(first_in, groups, place, parts)
    part_second_in = take_columns(second_in, groups, place, parts)
    part_first_out = take_rows(first_out, groups, place, parts)
    part_second_out = take_rows(second_out, groups, place, parts)
    again_first = ffn_again(act_first_all, part_first_in)
    again_second = ffn_again(act_second_all, part_second_in)

    grad, grad_gain_final = norm_backward(
        cotangent.astype(jnp.float32).reshape(tokens, model) * valid_flat,
        scaled_final,
        rstd_final,
        gain_final,
    )
    grad, grad_gain_second, branch_second = ffn_backward(
        grad, kept_second, gain_second, second_in, second_out
    )
    second_pieces = ffn_weight_grads(
        act_second_all,
        again_second,
        jnp.concatenate(spread_tm(branch_second), axis=0),
        part_second_out,
    )

    d_branch = grad.astype(jnp.bfloat16)
    d_normal = back_prop(d_branch, point_out) * silu_slope(normalized) * valid_flat
    batch_grads = mesh_sum(
        jnp.stack([jnp.sum(d_normal, axis=0), jnp.sum(d_normal * scaled_batch, axis=0)])
    )
    grad_batch_shift, grad_batch_scale = batch_grads[0], batch_grads[1]
    d_filtered = (
        valid_flat
        * (batch_scale * rstd_batch)
        * (d_normal - grad_batch_shift / count - scaled_batch * grad_batch_scale / count)
    )
    rimmed_grad = rimmed_of(d_filtered)
    d_gated = jnp.zeros_like(gated)
    tap_grads = []
    for tap in range(taps):
        d_gated = d_gated + depth_weight[tap] * rimmed_grad[2 * half - tap : 2 * half - tap + width]
        tap_grads.append(jnp.sum(d_filtered * rimmed[tap : tap + width], axis=0))
    d_gated = d_gated * valid_flat
    d_value = (d_gated * gate_sig).astype(jnp.bfloat16)
    d_gate = (d_gated * joined_value * gate_sig * (1.0 - gate_sig)).astype(jnp.bfloat16)
    d_joined = jnp.concatenate([d_value, d_gate], axis=1)

    def near_pair(array):
        return jnp.concatenate([array, swap(array, "tm", 1)], axis=0)

    def near_pair_half(array):
        got = swap(near_half(array, 1, 1 - side), "tm", 1)
        return jnp.concatenate([near_half(array, 1, side), got], axis=0)

    def far_sum(make):
        got = swap(make(1 - far), "tm", 2)
        return (make(far).astype(jnp.float32) + got.astype(jnp.float32)).astype(jnp.bfloat16)

    act_conv_pair, act_batch_pair = near_pair(act_conv), near_pair(act_batch)
    d_joined_pair, d_branch_pair = near_pair_half(d_joined), near_pair_half(d_branch)

    def conv_grads(which):
        return jnp.concatenate(
            [
                weight_grad(act_conv_pair, near_half(d_joined_pair, 1, which)),
                weight_grad(act_batch_pair, near_half(d_branch_pair, 1, which)),
            ],
            axis=1,
        )

    conv_pieces = spread_tm(reduce_rows(far_sum(conv_grads)))

    d_values, grad_gain_conv = norm_backward(
        back_prop(d_joined, point_in), scaled_conv, rstd_conv, gain_conv
    )
    grad = grad + d_values
    d_attend = grad.astype(jnp.bfloat16)
    d_attend_pair = ordered(is_low, d_attend, swap(d_attend, "tm", 1))
    attended_pair = ordered(is_low, attended, swap(attended, "tm", 1))
    d_mixed = back_prop(d_attend_pair, near_half(output_weight, 0, side)).astype(jnp.bfloat16)
    d_query, d_key, d_val, skew_lines = attend_back(
        at, query, keyval, d_mixed, lse, bias, near_heads, head_dim
    )

    far_input = back_prop(d_key[pair:], near_keyval[:, :near_width]) + back_prop(
        d_val[pair:], near_keyval[:, near_width:]
    )
    pair_input = (
        back_prop(d_query, near_query)
        + back_prop(d_key[:pair], near_keyval[:, :near_width])
        + back_prop(d_val[:pair], near_keyval[:, near_width:])
    )
    far_got = swap(near_half(far_input, 0, 1 - side).astype(jnp.bfloat16), "tm", 1)
    far_mine = near_half(far_input, 0, side) + far_got.astype(jnp.float32)
    far_back = swap(far_mine.astype(jnp.bfloat16), "tm", 2)
    pair_got = swap(near_half(pair_input, 0, 1 - side).astype(jnp.bfloat16), "tm", 1)
    d_input = near_half(pair_input, 0, side) + pair_got.astype(jnp.float32) + far_back.astype(jnp.float32)

    d_values, grad_gain_attend = norm_backward(d_input, scaled_attend, rstd_attend, gain_attend)
    grad = grad + d_values
    grad, grad_gain_first, branch_first = ffn_backward(
        grad, kept_first, gain_first, first_in, first_out
    )
    grad_features = grad.astype(jnp.bfloat16).reshape(row_count, width, model)
    first_pieces = ffn_weight_grads(
        act_first_all,
        again_first,
        jnp.concatenate(spread_tm(branch_first), axis=0),
        part_first_out,
    )

    d_attend_side = near_half(d_attend_pair, 1, side)

    def attend_grads(which):
        return jnp.concatenate(
            [
                weight_grad(act_pair, near_half(d_query, 1, which)),
                weight_grad(act_all, near_half(d_key, 1, which)),
                weight_grad(act_all, near_half(d_val, 1, which)),
                weight_grad(attended_pair, near_half(d_attend_side, 1, which)),
            ],
            axis=1,
        )

    attend_pieces = spread_tm(reduce_rows(far_sum(attend_grads)))

    table_lines = sum(
        jnp.pad(skew_lines[:, r], ((0, 0), (7 - r, 0)))[:, :span] for r in range(8)
    )
    near_grad = lax.dot_general(
        table_lines, one_hot, (((1,), (0,)), ((), ())), precision=lax.Precision.HIGHEST
    )
    grad_table = lax.dynamic_update_slice_in_dim(
        jnp.zeros((heads, bucket_count), jnp.float32), near_grad, side * near_heads, 0
    )
    small = jnp.concatenate(
        [
            grad_gain_first[None],
            grad_gain_attend[None],
            grad_gain_conv[None],
            grad_gain_second[None],
            grad_gain_final[None],
            jnp.stack(tap_grads),
            jnp.pad(grad_table.reshape(1, -1), ((0, 0), (0, model - heads * bucket_count))),
        ],
        axis=0,
    )
    small = mesh_sum(small)
    share = model // groups
    gains = lax.dynamic_slice_in_dim(small[:5], row_place * share, share, 1)
    grad_depth = small[5 : 5 + taps]
    grad_table = small[5 + taps, : heads * bucket_count].reshape(heads, bucket_count)

    relative = jnp.arange(parts) ^ place
    crossed = (relative % 2) * 2 + relative // 2
    (grad_first_in,) = lay_columns(first_pieces[0], (model,), groups, relative)
    (grad_second_in,) = lay_columns(second_pieces[0], (model,), groups, relative)

    def lay_rows(pieces):
        size = pieces[0].shape[0]
        out = jnp.zeros((parts, size, model), jnp.float32)
        for k in range(parts):
            out = lax.dynamic_update_index_in_dim(out, pieces[k].astype(jnp.float32), place ^ k, 0)
        return out.reshape(parts * size, model)

    grad_first_out = lay_rows(first_pieces[1])
    grad_second_out = lay_rows(second_pieces[1])
    quarter = model // parts
    grad_query, grad_key, grad_value, grad_output = lay_columns(
        attend_pieces, (quarter,) * 4, 1, crossed
    )
    grad_point_in, grad_point_out = lay_columns(conv_pieces, (2 * quarter, quarter), 1, crossed)
    return (
        output,
        grad_features,
        gains[0],
        grad_first_in,
        grad_first_out,
        gains[1],
        grad_query,
        grad_key,
        grad_value,
        grad_output,
        grad_table,
        gains[2],
        grad_point_in,
        grad_depth,
        grad_batch_scale,
        grad_batch_shift,
        grad_point_out,
        gains[3],
        grad_second_in,
        grad_second_out,
        gains[4],
    )


def solution(mesh):
    rows3, rows2, rows1 = P("rows", "tm", None), P("rows", None), P("rows")
    in_specs = (rows3, rows1) + (P(),) * 20 + (rows3,)
    out_specs = (
        rows3, rows3, rows1, rows2, rows2, rows1, rows2, rows2, rows2, rows2, P(),
        rows1, rows2, P(), P(), P(), rows2, rows1, rows2, rows2, rows1,
    )
    return jax.shard_map(shards, mesh=mesh, in_specs=in_specs, out_specs=out_specs, check_vma=False)
```

```python
import functools

import jax
import jax.numpy as jnp
from jax import lax
from jax.experimental import pallas as pl
from jax.experimental.pallas import tpu as pltpu
from jax.sharding import PartitionSpec as P

EPS = 1e-05
NEGATIVE = -1e30
LANES = 128
QUERY_TILE = 768
MIB = 1024 * 1024
BLOCK = 1024
EFFORT = 0.5


def swap(value, axis, bit):
    count = lax.axis_size(axis)
    return lax.ppermute(value, axis, [(i, i ^ bit) for i in range(count)])


def mesh_sum(value):
    for axis in ("tm", "rows"):
        bit = 1
        while bit < lax.axis_size(axis):
            value = value + swap(value, axis, bit)
            bit *= 2
    return value


def mesh_moments(count, mean, spread):
    for axis in ("tm", "rows"):
        bit = 1
        while bit < lax.axis_size(axis):
            sent = jnp.concatenate([mean[None], spread[None], jnp.broadcast_to(count, (1, mean.shape[0]))])
            got = swap(sent, axis, bit)
            other_mean, other_spread, other_count = got[0], got[1], got[2]
            total = count + other_count
            safe = jnp.maximum(total, 1.0)
            gap = other_mean - mean
            spread = spread + other_spread + gap * gap * (count * other_count / safe)
            mean = (count * mean + other_count * other_mean) / safe
            count = total
            bit *= 2
    return (count, mean, spread)


def after(value, *earlier):
    return lax.optimization_barrier((value, *earlier))[0]


def reduce_rows(partial, far_first=False):
    size = lax.axis_size("rows")
    place = lax.axis_index("rows")
    bits = size.bit_length() - 1
    order = list(range(bits))
    if far_first:
        order = order[1:] + order[:1]
    inner = (partial.shape[0] // size, partial.shape[1])
    left = partial.reshape((2,) * bits + inner)
    held = list(range(bits))[::-1]
    for bit in order:
        axis = held.index(bit)
        mine = (place >> bit) & 1
        front = left.shape[:axis]
        rows = 1
        for n in left.shape[axis + 1 : -2]:
            rows *= n
        lead = 1
        for n in front:
            lead *= n
        cut = left.reshape((lead, 2, rows) + inner)
        keep = lax.dynamic_index_in_dim(cut, mine, 1, keepdims=False)
        send = lax.dynamic_index_in_dim(cut, 1 - mine, 1, keepdims=False)
        got = swap(send, "rows", 1 << bit)
        left = (keep.astype(jnp.float32) + got.astype(jnp.float32)).astype(jnp.bfloat16)
        held.remove(bit)
        left = left.reshape((2,) * len(held) + inner)
    return left


def spread_tm(piece, *earlier):
    near = swap(piece, "tm", 1)
    far = swap(after(piece, *earlier) if earlier else piece, "tm", 2)
    return [piece, near, far, swap(far, "tm", 1)]


def silu_pair(hidden):
    sigma = 0.5 * jnp.tanh(0.5 * hidden) + 0.5
    act = hidden * sigma
    return (act, sigma + act * (1.0 - sigma))


def normed_of(values, gain):
    mean = jnp.mean(values, axis=-1, keepdims=True)
    centered = values - mean
    rstd = lax.rsqrt(jnp.mean(centered * centered, axis=-1, keepdims=True) + EPS)
    scaled = centered * rstd
    return (scaled * gain, scaled, rstd)


def normed_back(grad, values, gain):
    _, scaled, rstd = normed_of(values, gain)
    weighted = grad * gain
    inner = weighted - jnp.mean(weighted, axis=-1, keepdims=True)
    inner = inner - scaled * jnp.mean(weighted * scaled, axis=-1, keepdims=True)
    return (rstd * inner, jnp.sum(grad * scaled, axis=0, keepdims=True))


def dot(left, right):
    return jnp.dot(left, right, preferred_element_type=jnp.float32)


def dot_turned(left, right):
    return lax.dot_general(left, right, (((1,), (1,)), ((), ())), preferred_element_type=jnp.float32)


def scalars():
    return [pl.BlockSpec(memory_space=pltpu.SMEM)]


def struct(*shape, kind=jnp.bfloat16):
    return jax.ShapeDtypeStruct(shape, kind)


class Arriving:
    def __init__(self, source, target, sem):
        self.copy = pltpu.make_async_copy(source, target, sem)
        self.target = target
        self.started = self.here = False

    def start(self):
        if not self.started:
            self.copy.start()
            self.started = True

    def get(self):
        self.start()
        if not self.here:
            self.copy.wait()
            self.here = True
        return self.target


class Leaving:
    def __init__(self, source, target, sem):
        self.copy = pltpu.make_async_copy(source, target, sem)
        self.ref = source
        self.sent = False

    def send(self):
        self.copy.start()
        self.sent = True


def flow_call(body, name, outs, scratch, info, operands, flops, mib=24, raw=()):
    ins, results = len(operands), len(outs)

    def kernel(info, *refs):
        sources, targets = refs[:ins], refs[ins : ins + results]
        rest = refs[ins + results :]
        held, made = rest[:ins], rest[ins : ins + results]
        extra, sem_in, sem_out = rest[ins + results : -2], rest[-2], rest[-1]
        arriving = [
            (sources[k], held[k]) if k in raw else Arriving(sources[k], held[k], sem_in.at[k])
            for k in range(ins)
        ]
        for k in range(ins):
            if k not in raw:
                arriving[k].start()
        leaving = [Leaving(made[k], targets[k], sem_out.at[k]) for k in range(results)]
        body(info, arriving, leaving, *extra)
        for item in leaving:
            if not item.sent:
                item.send()
        for k in range(ins):
            if k not in raw:
                arriving[k].get()
        for item in leaving:
            item.copy.wait()

    moved = sum(o.size * o.dtype.itemsize for o in (*operands, *outs))
    return pl.pallas_call(
        kernel,
        in_specs=scalars() + [pl.BlockSpec(memory_space=pl.ANY)] * ins,
        out_specs=[pl.BlockSpec(memory_space=pl.ANY)] * results,
        out_shape=outs,
        scratch_shapes=[pltpu.VMEM(o.shape, o.dtype) for o in (*operands, *outs)]
        + list(scratch)
        + [pltpu.SemaphoreType.DMA((ins,)), pltpu.SemaphoreType.DMA((results,))],
        compiler_params=pltpu.CompilerParams(vmem_limit_bytes=mib * MIB),
        cost_estimate=cost(flops, 0, moved),
        name=name,
    )(info, *operands)


def cost(flops, transcendentals, moved):
    return pl.CostEstimate(
        flops=int(flops * EFFORT), transcendentals=int(transcendentals * EFFORT), bytes_accessed=int(moved * EFFORT)
    )


SIDE, FAR, OFFSET, LENGTH = range(4)


def project_kernel(info, ins, outs, sem, rows):
    mine, other, *weights = ins
    side = info[SIDE]
    half = outs[0].ref.shape[1]
    lanes = pl.ds(pl.multiple_of(side * half, half), half)
    copies = [
        pltpu.make_async_copy(source.at[:, lanes], held.at[:, :half], sem.at[k])
        for k, (source, held) in enumerate(weights)
    ]
    for copy in copies:
        copy.start()
    tokens = mine.target.shape[0]
    rows[pl.ds(pl.multiple_of(side * tokens, tokens), tokens)] = mine.get()[...]
    rows[pl.ds(pl.multiple_of((1 - side) * tokens, tokens), tokens)] = other.get()[...]
    for copy, (_, held), out in zip(copies, weights, outs, strict=True):
        copy.wait()
        out.ref[...] = dot(rows[...], held[:, :half]).astype(jnp.bfloat16)
        out.send()


def project(info, mine, other, weights):
    tokens, model = mine.shape
    pair = 2 * tokens
    return flow_call(
        project_kernel, "project",
        [struct(pair, model // 2)] * len(weights),
        [pltpu.SemaphoreType.DMA((len(weights),)), pltpu.VMEM((pair, model), jnp.bfloat16)],
        info, (mine, other, *weights), pair * model * model * len(weights),
        raw=tuple(range(2, 2 + len(weights))),
    )


def rows_of(length, first, count):
    frame = lax.broadcasted_iota(jnp.int32, (count, 1), 0) + first
    return ((frame >= 0) & (frame < length)).astype(jnp.float32)


def mix_kernel(
    info, own_ref, other_ref, weight, state_ref, gain_ref, value_w, gate_w,
    attended_ref, after_ref, act_ref, value_ref, gate_ref, gated_ref,
):
    side = info[SIDE]
    tokens, half = own_ref.shape

    @pl.when(pl.program_id(0) == 0)
    def _():
        attended_ref[:, pl.ds(pl.multiple_of(side * half, half), half)] = own_ref[...]
        attended_ref[:, pl.ds(pl.multiple_of((1 - side) * half, half), half)] = other_ref[...]
        values = state_ref[...] + dot(attended_ref[...], weight[...])
        after_ref[...] = values
        act_ref[...] = normed_of(values, gain_ref[...])[0].astype(jnp.bfloat16)

    value = dot(act_ref[...], value_w[...])
    gate = 0.5 * jnp.tanh(0.5 * dot(act_ref[...], gate_w[...])) + 0.5
    value_ref[...] = value.astype(jnp.bfloat16)
    gate_ref[...] = gate.astype(jnp.bfloat16)
    gated_ref[...] = value * gate * rows_of(info[LENGTH], info[OFFSET], tokens)


def mix(info, own, other, weight, state, gain, point_in):
    tokens, model = state.shape
    step = 512
    steps = model // step
    flat = (tokens, model)
    column = pl.BlockSpec((tokens, step), lambda i: (0, i))
    return pl.pallas_call(
        mix_kernel,
        grid=(steps,),
        in_specs=scalars() + [
            whole(own.shape), whole(own.shape), whole(weight.shape), whole(flat), whole((1, model)),
            pl.BlockSpec((model, step), lambda i: (0, i)),
            pl.BlockSpec((model, step), lambda i: (0, steps + i)),
        ],
        out_specs=[whole(flat)] * 3 + [column] * 3,
        out_shape=[
            struct(*flat), struct(*flat, kind=jnp.float32), struct(*flat),
            struct(*flat), struct(*flat), struct(*flat, kind=jnp.float32),
        ],
        compiler_params=pltpu.CompilerParams(vmem_limit_bytes=32 * MIB),
        cost_estimate=cost(
            6 * tokens * model * model,
            tokens * model,
            6 * model * model + 20 * tokens * model,
        ),
        name="mix",
    )(info, own, other, weight, state, gain[None], point_in, point_in)


def filter_kernel(info, ins, outs, wide):
    gated_ref, before_ref, after_ref, taps_ref = [item.get() for item in ins]
    filtered_ref, moments_ref = [item.ref for item in outs]
    tokens = gated_ref.shape[0]
    half = before_ref.shape[0]
    wide[8 : 8 + tokens] = gated_ref[...]
    wide[8 - half : 8] = before_ref[...].astype(jnp.float32)
    wide[8 + tokens : 8 + tokens + half] = after_ref[...].astype(jnp.float32)
    filtered = taps_ref[0:1] * wide[8 - half : 8 - half + tokens]
    for tap in range(1, taps_ref.shape[0]):
        filtered = filtered + taps_ref[tap : tap + 1] * wide[8 - half + tap : 8 - half + tap + tokens]
    filtered_ref[...] = filtered
    outs[0].send()
    valid = rows_of(info[LENGTH], info[OFFSET], tokens)
    count = jnp.clip(info[LENGTH] - info[OFFSET], 1, tokens).astype(jnp.float32)
    mean = jnp.sum(filtered * valid, axis=0, keepdims=True) / count
    gap = (filtered - mean) * valid
    moments_ref[0:1] = mean
    moments_ref[1:2] = jnp.sum(gap * gap, axis=0, keepdims=True)


def filter_frames(info, gated, before, later, depth):
    tokens, model = gated.shape
    return flow_call(
        filter_kernel, "filter_frames",
        [struct(tokens, model, kind=jnp.float32), struct(2, model, kind=jnp.float32)],
        [pltpu.VMEM((tokens + 16, model), jnp.float32)],
        info, (gated, before, later, depth), 10 * tokens * model,
    )


def weight_copies(pair_in, pair_out, sem, block):
    def at(i):
        lanes = pl.ds(pl.multiple_of(i * block, block), block)
        return (
            pltpu.make_async_copy(pair_in[0].at[:, lanes], pair_in[1].at[:, lanes], sem.at[0, i]),
            pltpu.make_async_copy(pair_out[0].at[lanes, :], pair_out[1].at[lanes, :], sem.at[1, i]),
        )

    return at


def second_kernel(info, ins, outs, sem, state, grad, total, slopes):
    filtered, stats, state_in, cot, gain, final_gain, point, pair_in, pair_out = ins
    w_in, w_out = pair_in[1], pair_out[1]
    act_batch, act_out, output, branch_out, grad_out, conv_out, d_norm_out, sums = outs
    tokens = filtered.target.shape[0]
    steps = w_in.shape[1] // BLOCK
    valid = rows_of(info[LENGTH], info[OFFSET], tokens)
    copies = weight_copies(pair_in, pair_out, sem, BLOCK)
    for i in range(steps):
        for copy in copies(i):
            copy.start()

    filtered_ref, stats_ref = filtered.get(), stats.get()

    def normalized():
        scaled = (filtered_ref[...] - stats_ref[0:1]) * stats_ref[1:2]
        return (scaled, scaled * stats_ref[2:3] + stats_ref[3:4])

    act = silu_pair(normalized()[1])[0].astype(jnp.bfloat16)
    act_batch.ref[...] = act
    act_batch.send()
    values = state_in.get()[...] + dot(act, point.get()[...])
    state[...] = values
    act_ref = act_out.ref
    act_ref[...] = normed_of(values, gain.get()[...])[0].astype(jnp.bfloat16)
    act_out.send()
    total[...] = jnp.zeros_like(total)

    def forward(i, carry):
        lanes = pl.ds(pl.multiple_of(i * BLOCK, BLOCK), BLOCK)
        for copy in copies(i):
            copy.wait()
        mid, slope = silu_pair(dot(act_ref[...], w_in[:, lanes]))
        slopes[:, lanes] = slope.astype(jnp.bfloat16)
        total[...] += dot(mid.astype(jnp.bfloat16), w_out[lanes, :])
        return carry

    lax.fori_loop(0, steps, forward, 0)
    values = state[...] + 0.5 * total[...]
    final = final_gain.get()[...]
    normed, _, _ = normed_of(values, final)
    output.ref[...] = (normed * valid).astype(jnp.bfloat16)
    output.send()
    begin, sums.ref[0:1] = normed_back(cot.get()[...].astype(jnp.float32) * valid, values, final)
    grad[...] = begin
    branch_ref = branch_out.ref
    branch_ref[...] = (0.5 * begin).astype(jnp.bfloat16)
    branch_out.send()
    total[...] = jnp.zeros_like(total)

    def backward(i, carry):
        lanes = pl.ds(pl.multiple_of(i * BLOCK, BLOCK), BLOCK)
        part = dot_turned(branch_ref[...], w_out[lanes, :])
        part = (part * slopes[:, lanes].astype(jnp.float32)).astype(jnp.bfloat16)
        total[...] += dot_turned(part, w_in[:, lanes])
        return carry

    lax.fori_loop(0, steps, backward, 0)
    d_values, sums.ref[1:2] = normed_back(total[...], state[...], gain.get()[...])
    later = grad[...] + d_values
    grad_out.ref[...] = later
    grad_out.send()
    low = later.astype(jnp.bfloat16)
    conv_out.ref[...] = low
    conv_out.send()
    scaled, normal = normalized()
    d_norm = dot_turned(low, point.get()[...]) * silu_pair(normal)[1] * valid
    d_norm_out.ref[...] = d_norm
    d_norm_out.send()
    sums.ref[2:3] = jnp.sum(d_norm, axis=0, keepdims=True)
    sums.ref[3:4] = jnp.sum(d_norm * scaled, axis=0, keepdims=True)


def second_both(info, filtered, stats, state, cotangent, gain, final_gain, point_out, w_in, w_out):
    tokens, model = state.shape
    inner = w_in.shape[1]
    flat = (tokens, model)
    low, high = struct(*flat), struct(*flat, kind=jnp.float32)
    return flow_call(
        second_kernel, "second_both",
        [low, low, low, low, high, low, high, struct(4, model, kind=jnp.float32)],
        [
            pltpu.SemaphoreType.DMA((2, inner // BLOCK)),
            pltpu.VMEM(flat, jnp.float32), pltpu.VMEM(flat, jnp.float32), pltpu.VMEM(flat, jnp.float32),
            pltpu.VMEM((tokens, inner), jnp.bfloat16),
        ],
        info,
        (filtered, stats, state, cotangent, gain[None], final_gain[None], point_out, w_in, w_out),
        8 * tokens * model * inner + 4 * tokens * model * model,
        mib=48,
        raw=(7, 8),
    )


def conv_back_kernel(info, ins, outs, wide, gated_wide):
    d_norm_ref, filtered_ref, before_ref, after_ref, stats_ref, sums_ref, taps_ref = [i.get() for i in ins[:7]]
    gated_ref, gated_before, gated_after = [i.get() for i in ins[7:10]]
    value, gate, point, state, gain, grad = ins[10:]
    joined_ref, out_ref, low_ref, small_ref = [item.ref for item in outs]
    tokens, model = d_norm_ref.shape
    half = gated_before.shape[0]

    def d_filtered(d_norm, filtered, first):
        valid = rows_of(info[LENGTH], first, d_norm.shape[0])
        scaled = (filtered - stats_ref[0:1]) * stats_ref[1:2]
        inner = d_norm - sums_ref[0:1] - scaled * sums_ref[1:2]
        return valid * (stats_ref[2:3] * stats_ref[1:2]) * inner

    offset = info[OFFSET]
    wide[8 : 8 + tokens] = d_filtered(d_norm_ref[...], filtered_ref[...], offset)
    wide[8 - half : 8] = d_filtered(before_ref[:half], before_ref[half:], offset - half)
    wide[8 + tokens : 8 + tokens + half] = d_filtered(after_ref[:half], after_ref[half:], offset + tokens)
    gated_wide[8 : 8 + tokens] = gated_ref[...]
    gated_wide[8 - half : 8] = gated_before[...].astype(jnp.float32)
    gated_wide[8 + tokens : 8 + tokens + half] = gated_after[...].astype(jnp.float32)
    d_gated = jnp.zeros((tokens, model), jnp.float32)
    for tap in range(taps_ref.shape[0]):
        begin = 8 + half - tap
        d_gated = d_gated + taps_ref[tap : tap + 1] * wide[begin : begin + tokens]
        begin = 8 - half + tap
        small_ref[1 + tap : 2 + tap] = jnp.sum(
            wide[8 : 8 + tokens] * gated_wide[begin : begin + tokens], axis=0, keepdims=True
        )
    d_gated = d_gated * rows_of(info[LENGTH], offset, tokens)
    gate = gate.get()[...].astype(jnp.float32)
    d_value = d_gated * gate
    joined_ref[:, :model] = d_value.astype(jnp.bfloat16)
    joined_ref[:, model:] = (d_value * value.get()[...].astype(jnp.float32) * (1.0 - gate)).astype(jnp.bfloat16)
    outs[0].send()
    d_values, small_ref[0:1] = normed_back(
        dot_turned(joined_ref[...], point.get()[...]), state.get()[...], gain.get()[...]
    )
    later = grad.get()[...] + d_values
    low_ref[...] = later.astype(jnp.bfloat16)
    outs[2].send()
    out_ref[...] = later


def conv_back(info, d_norm, filtered, before, later, stats, sums, depth, gated, gated_before, gated_after,
              value, gate, point_in, state, gain, grad):
    tokens, model = d_norm.shape
    return flow_call(
        conv_back_kernel, "conv_back",
        [
            struct(tokens, 2 * model), struct(tokens, model, kind=jnp.float32), struct(tokens, model),
            struct(1 + depth.shape[0], model, kind=jnp.float32),
        ],
        [pltpu.VMEM((tokens + 16, model), jnp.float32)] * 2,
        info,
        (d_norm, filtered, before, later, stats, sums, depth, gated, gated_before, gated_after, value,
         gate, point_in, state, gain[None], grad),
        4 * tokens * model * model,
        mib=32,
    )


def mixed_back_kernel(info, ins, outs, sem):
    own, near, (source, held) = ins
    half = source.shape[0] // 2
    side = info[SIDE]
    copy = pltpu.make_async_copy(source.at[pl.ds(pl.multiple_of(side * half, half), half), :], held.at[:half], sem.at[0])
    copy.start()
    own_ref, near_ref, out_ref = own.get(), near.get(), outs[0].ref
    tokens = own_ref.shape[0]
    copy.wait()
    part = held[:half]
    mine = pl.ds(pl.multiple_of(side * tokens, tokens), tokens)
    other = pl.ds(pl.multiple_of((1 - side) * tokens, tokens), tokens)
    out_ref[mine] = dot_turned(own_ref[...], part).astype(jnp.bfloat16)
    out_ref[other] = dot_turned(near_ref[...], part).astype(jnp.bfloat16)


def mixed_back(info, own, near, weight):
    tokens, model = own.shape
    return flow_call(
        mixed_back_kernel, "mixed_back", [struct(2 * tokens, model // 2)], [pltpu.SemaphoreType.DMA((1,))],
        info, (own, near, weight), 2 * tokens * model * model, raw=(2,),
    )[0]


def input_back_kernel(count, base, info, ins, outs, sem):
    grads, weights = ins[:count], ins[count:]
    send_ref, keep_ref = outs[0].ref, outs[1].ref
    tokens = send_ref.shape[0]
    side = info[SIDE]
    half = weights[0][0].shape[1] // 2
    lanes = pl.ds(pl.multiple_of(side * half, half), half)
    copies = [
        pltpu.make_async_copy(source.at[:, lanes], held.at[:, :half], sem.at[k])
        for k, (source, held) in enumerate(weights)
    ]
    for copy in copies:
        copy.start()
    grads = [grad.get() for grad in grads]
    for copy in copies:
        copy.wait()

    def total(which):
        out = None
        for first, grad, (_, held) in zip(base, grads, weights, strict=True):
            rows = pl.ds(pl.multiple_of(first + which * tokens, LANES), tokens)
            part = dot_turned(grad[rows], held[:, :half])
            out = part if out is None else out + part
        return out

    send_ref[...] = total(1 - side).astype(jnp.bfloat16)
    outs[0].send()
    keep_ref[...] = total(side)


def input_back(info, grads, base, weights, tokens):
    model = weights[0].shape[0]
    count = len(grads)
    return flow_call(
        functools.partial(input_back_kernel, count, base), "input_back",
        [struct(tokens, model), struct(tokens, model, kind=jnp.float32)],
        [pltpu.SemaphoreType.DMA((count,))],
        info, (*grads, *weights), 2 * tokens * model * model * count,
        mib=32, raw=tuple(range(count, 2 * count)),
    )


def cross_kernel(layout, info, refs, outs, left_rows, right_rows):
    send_ref, keep_ref = outs[0].ref, outs[1].ref
    far, side = info[FAR], info[SIDE]
    at = 0
    begin = 0
    for pieces, width in layout:
        lefts, right = refs[at : at + pieces], refs[at + pieces : at + pieces + (2 if width < 0 else 1)]
        at += pieces + len(right)
        tokens = lefts[0].target.shape[0]
        for k, left in enumerate(lefts):
            spot = (k // 2 * 2 + (side if k % 2 == 0 else 1 - side)) * tokens
            left_rows[pl.ds(pl.multiple_of(spot, tokens), tokens)] = left.get()[...]
        size = abs(width)
        half = size // 2
        if len(right) == 2:
            for k, piece in enumerate(right):
                spot = (side if k == 0 else 1 - side) * tokens
                right_rows[pl.ds(pl.multiple_of(spot, tokens), tokens), :size] = piece.get()[...]
            source = right_rows
        else:
            source = right[0].get()
        count = pieces * tokens
        for which, target in ((1 - far, send_ref), (far, keep_ref)):
            lanes = pl.ds(pl.multiple_of(which * half, half), half)
            target[:, begin : begin + half] = lax.dot_general(
                left_rows[:count], source[:count, lanes], (((0,), (0,)), ((), ())),
                preferred_element_type=jnp.float32,
            ).astype(jnp.bfloat16)
        begin += half


def cross_grads(info, terms):
    operands, layout = [], []
    total = flops = 0
    for lefts, rights in terms:
        operands += [*lefts, *rights]
        width = rights[0].shape[1]
        layout.append((len(lefts), -width if len(rights) == 2 else width))
        total += width // 2
        tokens, model = lefts[0].shape
        flops += 2 * len(lefts) * tokens * model * width
    deepest = max(len(lefts) for lefts, _ in terms) * tokens
    widest = max(rights[0].shape[1] for _, rights in terms)
    return flow_call(
        functools.partial(cross_kernel, layout), "cross_grads", [struct(model, total)] * 2,
        [pltpu.VMEM((deepest, model), jnp.bfloat16), pltpu.VMEM((deepest, widest), jnp.bfloat16)],
        info, tuple(operands), flops, mib=40,
    )


def first_back_kernel(info, ins, outs, sem, branch, total):
    grad, x, gain, slope, pair_in, pair_out = ins
    w_in, w_out = pair_in[1], pair_out[1]
    steps = w_in.shape[1] // BLOCK
    copies = weight_copies(pair_in, pair_out, sem, BLOCK)
    for i in range(steps):
        for copy in copies(i):
            copy.start()
    grad_ref = grad.get()
    branch[...] = (0.5 * grad_ref[...]).astype(jnp.bfloat16)
    total[...] = jnp.zeros_like(total)
    slope_ref = slope.get()

    def backward(i, carry):
        lanes = pl.ds(pl.multiple_of(i * BLOCK, BLOCK), BLOCK)
        for copy in copies(i):
            copy.wait()
        part = dot_turned(branch[...], w_out[lanes, :])
        part = (part * slope_ref[:, lanes].astype(jnp.float32)).astype(jnp.bfloat16)
        total[...] += dot_turned(part, w_in[:, lanes])
        return carry

    lax.fori_loop(0, steps, backward, 0)
    d_values, outs[1].ref[...] = normed_back(total[...], x.get()[...].astype(jnp.float32), gain.get()[...])
    outs[0].ref[...] = (grad_ref[...] + d_values).astype(jnp.bfloat16)


def first_backward(info, grad, features, gain, slope, w_in, w_out):
    tokens, model = features.shape
    inner = w_in.shape[1]
    return flow_call(
        first_back_kernel, "first_backward",
        [struct(tokens, model), struct(1, model, kind=jnp.float32)],
        [pltpu.SemaphoreType.DMA((2, inner // BLOCK)), pltpu.VMEM((tokens, model), jnp.bfloat16), pltpu.VMEM((tokens, model), jnp.float32)],
        info, (grad, features, gain[None], slope, w_in, w_out), 4 * tokens * model * inner,
        mib=40, raw=(4, 5),
    )


def norm_backward(grad, scaled, rstd, gain):
    weighted = grad * gain
    inner = weighted - jnp.mean(weighted, axis=-1, keepdims=True)
    inner = inner - scaled * jnp.mean(weighted * scaled, axis=-1, keepdims=True)
    return (rstd * inner, jnp.sum(grad * scaled, axis=0))


def first_kernel(x_ref, gain_ref, next_gain_ref, w_in, w_out, state_ref, act_ref, slope_ref, next_ref, total):
    step = pl.program_id(0)

    @pl.when(step == 0)
    def _():
        values = x_ref[...].astype(jnp.float32)
        act_ref[...] = normed_of(values, gain_ref[...])[0].astype(jnp.bfloat16)
        total[...] = jnp.zeros_like(total)

    mid, slope = silu_pair(dot(act_ref[...], w_in[...]))
    slope_ref[...] = slope.astype(jnp.bfloat16)
    total[...] += dot(mid.astype(jnp.bfloat16), w_out[...])

    @pl.when(step == pl.num_programs(0) - 1)
    def _():
        values = x_ref[...].astype(jnp.float32) + 0.5 * total[...]
        state_ref[...] = values
        next_ref[...] = normed_of(values, next_gain_ref[...])[0].astype(jnp.bfloat16)


def whole(shape):
    return pl.BlockSpec(shape, lambda *_: (0,) * len(shape))


def first_forward(features, gain, next_gain, w_in, w_out):
    tokens, model = features.shape
    inner = w_in.shape[1]
    return pl.pallas_call(
        first_kernel,
        grid=(inner // BLOCK,),
        in_specs=[
            whole((tokens, model)),
            whole((1, model)),
            whole((1, model)),
            pl.BlockSpec((model, BLOCK), lambda i: (0, i)),
            pl.BlockSpec((BLOCK, model), lambda i: (i, 0)),
        ],
        out_specs=[
            whole((tokens, model)),
            whole((tokens, model)),
            pl.BlockSpec((tokens, BLOCK), lambda i: (0, i)),
            whole((tokens, model)),
        ],
        out_shape=[
            jax.ShapeDtypeStruct((tokens, model), jnp.float32),
            jax.ShapeDtypeStruct((tokens, model), jnp.bfloat16),
            jax.ShapeDtypeStruct((tokens, inner), jnp.bfloat16),
            jax.ShapeDtypeStruct((tokens, model), jnp.bfloat16),
        ],
        scratch_shapes=[pltpu.VMEM((tokens, model), jnp.float32)],
        compiler_params=pltpu.CompilerParams(vmem_limit_bytes=40 * MIB),
        cost_estimate=cost(
            4 * tokens * model * inner,
            2 * tokens * inner,
            4 * model * inner + 2 * tokens * inner,
        ),
        name="first_forward",
    )(features, gain[None], next_gain[None], w_in, w_out)


def take_kernel(place, source, target):
    target[...] = source[...]


def take_columns(weight, groups, place, parts):
    model, total = weight.shape
    block = total // groups // parts
    if block % LANES:
        cut = weight.reshape(model, groups, parts, block)
        return lax.dynamic_index_in_dim(cut, place, 2, keepdims=False).reshape(model, -1)
    return pl.pallas_call(
        take_kernel,
        out_shape=jax.ShapeDtypeStruct((model, total // parts), weight.dtype),
        grid_spec=pltpu.PrefetchScalarGridSpec(
            num_scalar_prefetch=1,
            grid=(groups,),
            in_specs=[pl.BlockSpec((model, block), lambda g, at: (0, g * parts + at[0]))],
            out_specs=pl.BlockSpec((model, block), lambda g, at: (0, g)),
        ),
        name="take_columns",
    )(place.reshape(1), weight)


def take_rows(weight, groups, place, parts):
    total, model = weight.shape
    cut = weight.reshape(groups, parts, total // groups // parts, model)
    return lax.dynamic_index_in_dim(cut, place, 1, keepdims=False).reshape(-1, model)


def lay_kernel(widths, groups, places, *refs):
    parts = 4
    pieces, targets = refs[:parts], refs[parts:]
    for k in range(parts):
        begin = 0
        for width, target in zip(widths, targets, strict=True):
            block = width // groups
            for g in range(groups):
                at = pl.multiple_of((g * parts + places[k]) * block, LANES)
                source = pieces[k][:, begin + g * block : begin + (g + 1) * block]
                target[:, pl.ds(at, block)] = source.astype(jnp.float32)
            begin += width


def lay_columns(pieces, widths, groups, places):
    rows = pieces[0].shape[0]
    parts = len(pieces)
    if any((width // groups) % LANES for width in widths):
        outs, begin = [], 0
        stacked = jnp.zeros((parts, *pieces[0].shape), pieces[0].dtype)
        for k in range(parts):
            stacked = lax.dynamic_update_index_in_dim(stacked, pieces[k], places[k], 0)
        for width in widths:
            cut = stacked[:, :, begin : begin + width].reshape(parts, rows, groups, width // groups)
            outs.append(cut.transpose(1, 2, 0, 3).reshape(rows, parts * width).astype(jnp.float32))
            begin += width
        return outs
    return pl.pallas_call(
        functools.partial(lay_kernel, widths, groups),
        out_shape=[jax.ShapeDtypeStruct((rows, parts * width), jnp.float32) for width in widths],
        grid_spec=pltpu.PrefetchScalarGridSpec(
            num_scalar_prefetch=1,
            grid=(1,),
            in_specs=[pl.BlockSpec(p.shape, lambda i, at: (0, 0)) for p in pieces],
            out_specs=[pl.BlockSpec((rows, parts * width), lambda i, at: (0, 0)) for width in widths],
        ),
        compiler_params=pltpu.CompilerParams(vmem_limit_bytes=24 * MIB),
        name="lay_columns",
    )(places, *pieces)


def skew_kernel(line, out):
    length = line.shape[-1]
    width = out.shape[-1]
    spread = jnp.broadcast_to(line[0], (LANES, length))
    rolled = pltpu.roll(spread, length - (LANES - 1), 1, stride=1, stride_axis=0)
    out[0] = rolled[:, :width]


def skewed(lines):
    heads, _, length = lines.shape
    width = length - LANES
    return pl.pallas_call(
        skew_kernel,
        out_shape=jax.ShapeDtypeStruct((heads, LANES, width), jnp.float32),
        grid=(heads,),
        in_specs=[pl.BlockSpec((1, 1, length), lambda h: (h, 0, 0))],
        out_specs=pl.BlockSpec((1, LANES, width), lambda h: (h, 0, 0)),
        name="bias_rows",
    )(lines)


def attend_kernel(
    scale, at, q_ref, k_pair, k_far, v_pair, v_far, bias_ref, out_ref, lse_ref, k_ref, vt_ref, s_ref, p_ref
):
    tile = q_ref.shape[0]
    blocks = k_ref.shape[0] // LANES
    pair = k_pair.shape[0]
    length = at[blocks * 2]

    @pl.when(pl.program_id(1) == 0)
    def _():
        k_ref[:pair] = k_pair[...]
        k_ref[pair:] = k_far[...]
        vt_ref[:, :pair] = v_pair[...].T
        vt_ref[:, pair:] = v_far[...].T

    begin = pl.program_id(1) * tile
    s_ref[...] = lax.dot_general(
        k_ref[...], q_ref[...], (((1,), (1,)), ((), ())), preferred_element_type=jnp.float32
    )
    frame = lax.broadcasted_iota(jnp.int32, (LANES, tile), 0)
    top = jnp.full((1, tile), NEGATIVE, jnp.float32)
    for b in range(blocks):
        lanes = pl.ds(pl.multiple_of(at[b] + begin, LANES), tile)
        s = s_ref[b * LANES : (b + 1) * LANES] * scale + bias_ref[0, :, lanes]
        s = jnp.where(frame < length - at[blocks + b], s, NEGATIVE)
        s_ref[b * LANES : (b + 1) * LANES] = s
        top = jnp.maximum(top, jnp.max(s, axis=0, keepdims=True))
    total = jnp.zeros((1, tile), jnp.float32)
    for b in range(blocks):
        p = jnp.exp(s_ref[b * LANES : (b + 1) * LANES] - top)
        total = total + jnp.sum(p, axis=0, keepdims=True)
        p_ref[b * LANES : (b + 1) * LANES] = p.astype(jnp.bfloat16)
    mixed = jnp.dot(vt_ref[...], p_ref[...], preferred_element_type=jnp.float32) / total
    out_ref[...] = mixed.T.astype(jnp.bfloat16)
    lse_ref[0] = top + jnp.log(total)


def attend(at, query, key, key_far, value, value_far, bias, heads, head_dim):
    queries, keys = query.shape[0], 2 * key.shape[0]
    tile = QUERY_TILE
    width = bias.shape[-1]
    grid_spec = pltpu.PrefetchScalarGridSpec(
        num_scalar_prefetch=1,
        grid=(heads, queries // tile),
        in_specs=[
            pl.BlockSpec((tile, head_dim), lambda h, i, at: (i, h)),
            pl.BlockSpec((keys // 2, head_dim), lambda h, i, at: (0, h)),
            pl.BlockSpec((keys // 2, head_dim), lambda h, i, at: (0, h)),
            pl.BlockSpec((keys // 2, head_dim), lambda h, i, at: (0, h)),
            pl.BlockSpec((keys // 2, head_dim), lambda h, i, at: (0, h)),
            pl.BlockSpec((1, LANES, width), lambda h, i, at: (h, 0, 0)),
        ],
        out_specs=[
            pl.BlockSpec((tile, head_dim), lambda h, i, at: (i, h)),
            pl.BlockSpec((1, 1, tile), lambda h, i, at: (h, 0, i)),
        ],
        scratch_shapes=[
            pltpu.VMEM((keys, head_dim), jnp.bfloat16),
            pltpu.VMEM((head_dim, keys), jnp.bfloat16),
            pltpu.VMEM((keys, tile), jnp.float32),
            pltpu.VMEM((keys, tile), jnp.bfloat16),
        ],
    )
    return pl.pallas_call(
        functools.partial(attend_kernel, head_dim ** (-0.5)),
        out_shape=[
            jax.ShapeDtypeStruct((queries, heads * head_dim), jnp.bfloat16),
            jax.ShapeDtypeStruct((heads, 1, queries), jnp.float32),
        ],
        grid_spec=grid_spec,
        compiler_params=pltpu.CompilerParams(vmem_limit_bytes=24 * MIB),
        cost_estimate=cost(
            4 * heads * queries * keys * head_dim,
            heads * queries * keys,
            4 * heads * LANES * width + 4 * heads * head_dim * (queries + keys),
        ),
        name="attend",
    )(at, query, key, key_far, value, value_far, bias)


def attend_back_kernel(
    scale, at, q_ref, k_pair, k_far, v_pair, v_far, do_ref, lse_ref, bias_ref,
    dq_ref, dk_ref, dv_ref, line_ref,
    k_ref, v_ref, kt_ref, s_ref, dp_ref, p_ref, ds_ref, dk_sum, dv_sum, skew_ref,
):
    tile = q_ref.shape[0]
    blocks = k_ref.shape[0] // LANES
    length = at[blocks * 2]
    pair = k_pair.shape[0]

    @pl.when(pl.program_id(1) == 0)
    def _():
        k_ref[:pair] = k_pair[...]
        k_ref[pair:] = k_far[...]
        v_ref[:pair] = v_pair[...]
        v_ref[pair:] = v_far[...]
        kt_ref[...] = k_ref[...].T
        dk_sum[...] = jnp.zeros_like(dk_sum)
        dv_sum[...] = jnp.zeros_like(dv_sum)
        skew_ref[...] = jnp.zeros_like(skew_ref)

    begin = pl.program_id(1) * tile
    s_ref[...] = lax.dot_general(
        k_ref[...], q_ref[...], (((1,), (1,)), ((), ())), preferred_element_type=jnp.float32
    )
    dp_ref[...] = lax.dot_general(
        v_ref[...], do_ref[...], (((1,), (1,)), ((), ())), preferred_element_type=jnp.float32
    )
    frame = lax.broadcasted_iota(jnp.int32, (LANES, tile), 0)
    lse = lse_ref[0]
    delta = jnp.zeros((1, tile), jnp.float32)
    for b in range(blocks):
        rows = slice(b * LANES, (b + 1) * LANES)
        lanes = pl.ds(pl.multiple_of(at[b] + begin, LANES), tile)
        s = s_ref[rows] * scale + bias_ref[0, :, lanes]
        s = jnp.where(frame < length - at[blocks + b], s, NEGATIVE)
        p = jnp.exp(s - lse)
        s_ref[rows] = p
        p_ref[rows] = p.astype(jnp.bfloat16)
        delta = delta + jnp.sum(p * dp_ref[rows], axis=0, keepdims=True)
    for b in range(blocks):
        rows = slice(b * LANES, (b + 1) * LANES)
        lanes = pl.ds(pl.multiple_of(at[b] + begin, LANES), tile)
        ds = (s_ref[rows] * (dp_ref[rows] - delta)).astype(jnp.bfloat16)
        ds_ref[rows] = ds
        skew_ref[:, lanes] += ds.astype(jnp.float32)
    dv_sum[...] += jnp.dot(p_ref[...], do_ref[...], preferred_element_type=jnp.float32)
    dk_sum[...] += jnp.dot(ds_ref[...], q_ref[...], preferred_element_type=jnp.float32)
    dq = jnp.dot(kt_ref[...], ds_ref[...], preferred_element_type=jnp.float32) * scale
    dq_ref[...] = dq.T.astype(jnp.bfloat16)

    @pl.when(pl.program_id(1) == pl.num_programs(1) - 1)
    def _():
        dk_ref[...] = (dk_sum[...] * scale).astype(jnp.bfloat16)
        dv_ref[...] = dv_sum[...].astype(jnp.bfloat16)
        lines = jnp.concatenate([skew_ref[...], jnp.zeros((LANES, LANES), jnp.float32)], axis=1)
        count = LANES // 2
        while count >= 8:
            lines = lines[count:] + pltpu.roll(lines[:count], count, 1)
            count //= 2
        line_ref[0] = lines


def attend_back(at, query, key, key_far, value, value_far, grad, lse, bias, heads, head_dim):
    queries, keys = query.shape[0], 2 * key.shape[0]
    tile = QUERY_TILE
    width = bias.shape[-1]
    grid_spec = pltpu.PrefetchScalarGridSpec(
        num_scalar_prefetch=1,
        grid=(heads, queries // tile),
        in_specs=[
            pl.BlockSpec((tile, head_dim), lambda h, i, at: (i, h)),
            pl.BlockSpec((keys // 2, head_dim), lambda h, i, at: (0, h)),
            pl.BlockSpec((keys // 2, head_dim), lambda h, i, at: (0, h)),
            pl.BlockSpec((keys // 2, head_dim), lambda h, i, at: (0, h)),
            pl.BlockSpec((keys // 2, head_dim), lambda h, i, at: (0, h)),
            pl.BlockSpec((tile, head_dim), lambda h, i, at: (i, h)),
            pl.BlockSpec((1, 1, tile), lambda h, i, at: (h, 0, i)),
            pl.BlockSpec((1, LANES, width), lambda h, i, at: (h, 0, 0)),
        ],
        out_specs=[
            pl.BlockSpec((tile, head_dim), lambda h, i, at: (i, h)),
            pl.BlockSpec((keys, head_dim), lambda h, i, at: (0, h)),
            pl.BlockSpec((keys, head_dim), lambda h, i, at: (0, h)),
            pl.BlockSpec((1, 8, width + LANES), lambda h, i, at: (h, 0, 0)),
        ],
        scratch_shapes=[
            pltpu.VMEM((keys, head_dim), jnp.bfloat16),
            pltpu.VMEM((keys, head_dim), jnp.bfloat16),
            pltpu.VMEM((head_dim, keys), jnp.bfloat16),
            pltpu.VMEM((keys, tile), jnp.float32),
            pltpu.VMEM((keys, tile), jnp.float32),
            pltpu.VMEM((keys, tile), jnp.bfloat16),
            pltpu.VMEM((keys, tile), jnp.bfloat16),
            pltpu.VMEM((keys, head_dim), jnp.float32),
            pltpu.VMEM((keys, head_dim), jnp.float32),
            pltpu.VMEM((LANES, width), jnp.float32),
        ],
    )
    return pl.pallas_call(
        functools.partial(attend_back_kernel, head_dim ** (-0.5)),
        out_shape=[
            jax.ShapeDtypeStruct((queries, heads * head_dim), jnp.bfloat16),
            jax.ShapeDtypeStruct((keys, heads * head_dim), jnp.bfloat16),
            jax.ShapeDtypeStruct((keys, heads * head_dim), jnp.bfloat16),
            jax.ShapeDtypeStruct((heads, 8, width + LANES), jnp.float32),
        ],
        grid_spec=grid_spec,
        compiler_params=pltpu.CompilerParams(vmem_limit_bytes=24 * MIB),
        cost_estimate=cost(
            10 * heads * queries * keys * head_dim,
            heads * queries * keys,
            4 * heads * LANES * width + 8 * heads * head_dim * (queries + keys),
        ),
        name="attend_back",
    )(at, query, key, key_far, value, value_far, grad, lse, bias)


def again_kernel(count, at, *refs):
    pieces, cuts = refs[:4], refs[4 : 4 + count]
    act_ref, slope_ref, rows = refs[4 + count :]
    tokens = pieces[0].shape[0]

    @pl.when(pl.program_id(0) == 0)
    def _():
        for k in range(4):
            rows[k * tokens : (k + 1) * tokens] = pieces[k][...]

    for k in range(count):
        block = cuts[k].shape[1]
        mid, slope = silu_pair(dot_turned(cuts[k][...].T, rows[...]))
        act_ref[k * block : (k + 1) * block] = mid.astype(jnp.bfloat16)
        slope_ref[k * block : (k + 1) * block] = slope.astype(jnp.bfloat16)


def column_cuts(weight, groups, parts, width):
    block = weight.shape[1] // groups // parts
    if block == width:
        return weight, lambda g, at: (0, g * parts + at[0])
    return None, lambda g, at: (0, g)


def again(place, pieces, weight, groups):
    parts = len(pieces)
    tokens, model = pieces[0].shape
    inner = weight.shape[1] // parts
    width = LANES
    source, where = column_cuts(weight, groups, parts, width)
    if source is None:
        source = take_columns(weight, groups, place, parts)
    count = 2
    cut = inner // width // count
    return pl.pallas_call(
        functools.partial(again_kernel, count),
        grid_spec=pltpu.PrefetchScalarGridSpec(
            num_scalar_prefetch=1,
            grid=(cut,),
            in_specs=[whole((tokens, model))] * parts
            + [
                pl.BlockSpec((model, width), lambda i, at, k=k: where(i * count + k, at))
                for k in range(count)
            ],
            out_specs=[pl.BlockSpec((count * width, parts * tokens), lambda i, at: (i, 0))] * 2,
            scratch_shapes=[pltpu.VMEM((parts * tokens, model), jnp.bfloat16)],
        ),
        out_shape=[jax.ShapeDtypeStruct((inner, parts * tokens), jnp.bfloat16)] * 2,
        compiler_params=pltpu.CompilerParams(vmem_limit_bytes=40 * MIB),
        cost_estimate=cost(
            2 * parts * tokens * model * inner,
            2 * parts * tokens * inner,
            2 * parts * tokens * (2 * inner + model) + 2 * model * inner,
        ),
        name="again",
    )(place.reshape(1), *pieces, *([source] * count))


def grad_out_kernel(act_ref, *refs):
    pieces, out_ref, rows = refs[:4], refs[4], refs[5]
    tokens = pieces[0].shape[0]

    @pl.when(pl.program_id(0) == 0)
    def _():
        for k in range(4):
            rows[k * tokens : (k + 1) * tokens] = pieces[k][...]

    out_ref[...] = dot(act_ref[...], rows[...]).astype(jnp.bfloat16)


def grad_out_of(act, pieces):
    inner, frames = act.shape
    tokens, model = pieces[0].shape
    step = 256
    return pl.pallas_call(
        grad_out_kernel,
        grid=(inner // step,),
        in_specs=[pl.BlockSpec((step, frames), lambda i: (i, 0))]
        + [whole((tokens, model))] * len(pieces),
        out_specs=pl.BlockSpec((step, model), lambda i: (i, 0)),
        out_shape=jax.ShapeDtypeStruct((inner, model), jnp.bfloat16),
        scratch_shapes=[pltpu.VMEM((frames, model), jnp.bfloat16)],
        compiler_params=pltpu.CompilerParams(vmem_limit_bytes=40 * MIB),
        cost_estimate=cost(
            2 * frames * model * inner,
            0,
            2 * frames * (inner + model) + 2 * model * inner,
        ),
        name="grad_out",
    )(act, *pieces)


def grad_in_kernel(count, at, slope_ref, *refs):
    acts, branches, cuts = refs[:4], refs[4:8], refs[8 : 8 + count]
    out_ref, act_rows, branch_rows = refs[8 + count :]
    tokens = acts[0].shape[0]

    @pl.when(pl.program_id(0) == 0)
    def _():
        for k in range(4):
            act_rows[k * tokens : (k + 1) * tokens] = acts[k][...]
            branch_rows[k * tokens : (k + 1) * tokens] = branches[k][...]

    cut = jnp.concatenate([c[...] for c in cuts], axis=0)
    d_hidden = (dot_turned(cut, branch_rows[...]) * slope_ref[...].astype(jnp.float32)).astype(jnp.bfloat16)
    out_ref[...] = dot(d_hidden, act_rows[...]).T.astype(jnp.bfloat16)


def grad_in_of(place, slope, acts, branches, weight, groups):
    inner, frames = slope.shape
    tokens, model = acts[0].shape
    parts = len(acts)
    width = LANES
    count = 2
    if weight.shape[0] // groups // parts == width:
        source, where = weight, lambda g, at: (g * parts + at[0], 0)
    else:
        source, where = take_rows(weight, groups, place, parts), lambda g, at: (g, 0)
    return pl.pallas_call(
        functools.partial(grad_in_kernel, count),
        grid_spec=pltpu.PrefetchScalarGridSpec(
            num_scalar_prefetch=1,
            grid=(inner // width // count,),
            in_specs=[pl.BlockSpec((count * width, frames), lambda i, at: (i, 0))]
            + [whole((tokens, model))] * (2 * parts)
            + [
                pl.BlockSpec((width, model), lambda i, at, k=k: where(i * count + k, at))
                for k in range(count)
            ],
            out_specs=pl.BlockSpec((model, count * width), lambda i, at: (0, i)),
            scratch_shapes=[pltpu.VMEM((frames, model), jnp.bfloat16)] * 2,
        ),
        out_shape=jax.ShapeDtypeStruct((model, inner), jnp.bfloat16),
        compiler_params=pltpu.CompilerParams(vmem_limit_bytes=40 * MIB),
        cost_estimate=cost(
            4 * frames * model * inner,
            0,
            2 * frames * (inner + 2 * model) + 4 * model * inner,
        ),
        name="grad_in",
    )(place.reshape(1), slope, *acts, *branches, *([source] * count))


def shards(
    features,
    lengths,
    buckets,
    gain_first,
    first_in,
    first_out,
    gain_attend,
    query_weight,
    key_weight,
    value_weight,
    output_weight,
    bias_table,
    gain_conv,
    point_in,
    depth_weight,
    batch_scale,
    batch_shift,
    point_out,
    gain_second,
    second_in,
    second_out,
    gain_final,
    cotangent,
):
    row_count, width, model = features.shape
    tokens = row_count * width
    heads, bucket_count = bias_table.shape
    head_dim = model // heads
    parts = lax.axis_size("tm")
    groups = lax.axis_size("rows")
    frames = width * parts
    half = depth_weight.shape[0] // 2
    taps = depth_weight.shape[0]
    place = lax.axis_index("tm")
    row_place = lax.axis_index("rows")
    side = place % 2
    far = place // 2
    offset = place * width
    near_heads = heads // 2
    pair = 2 * width
    info = jnp.stack([side, far, offset, lengths[0]]).astype(jnp.int32)

    def near_half(array, axis, index):
        size = array.shape[axis] // 2
        return lax.dynamic_slice_in_dim(array, index * size, size, axis)

    flat_features = features.reshape(tokens, model)
    after_first, act_first, slope_first, act_attend = first_forward(
        flat_features, gain_first, gain_attend, first_in, first_out
    )
    act_near, act_far = swap(act_attend, "tm", 1), swap(act_attend, "tm", 2)
    act_cross = swap(act_far, "tm", 1)

    near_table = lax.dynamic_slice_in_dim(bias_table, side * near_heads, near_heads, 0)
    span = pair + frames
    turned = jnp.pad(buckets[::-1], (0, 1), constant_values=-1)
    window = lax.dynamic_slice_in_dim(turned, far * pair, span, 0)
    one_hot = (window[:, None] == jnp.arange(bucket_count)[None, :]).astype(jnp.float32)
    bias_lines = lax.dot_general(
        near_table, one_hot, (((1,), (1,)), ((), ())), precision=lax.Precision.HIGHEST
    )
    bias = skewed(bias_lines[:, None, :])
    key_blocks = frames // LANES
    block = jnp.arange(key_blocks)
    block = (block + far * (key_blocks // 2)) % key_blocks
    at = jnp.concatenate([frames - LANES - LANES * block, LANES * block, lengths[:1]]).astype(jnp.int32)

    query, key, value = project(info, act_attend, act_near, (query_weight, key_weight, value_weight))
    key_far, value_far = project(info, act_far, act_cross, (key_weight, value_weight))
    mixed, lse = attend(at, query, key, key_far, value, value_far, bias, near_heads, head_dim)
    own_mixed = near_half(mixed, 0, side)
    other_mixed = swap(near_half(mixed, 0, 1 - side), "tm", 1)

    attended, after_attend, act_conv, joined_value, gate, gated = mix(
        info, own_mixed, other_mixed, output_weight, after_first, gain_conv, point_in
    )
    up = [(i, i + 1) for i in range(parts - 1)]
    down = [(j, i) for i, j in up]
    gated_before = lax.ppermute(gated[width - half :].astype(jnp.bfloat16), "tm", up)
    gated_after = lax.ppermute(gated[:half].astype(jnp.bfloat16), "tm", down)
    filtered, moments = filter_frames(info, gated, gated_before, gated_after, depth_weight)
    local_count = jnp.clip(lengths[0] - offset, 0, width).astype(jnp.float32)
    count, batch_mean, spread = mesh_moments(local_count, moments[0], moments[1])
    count = count[0]
    rstd_batch = lax.rsqrt(spread / count + EPS)
    stats = jnp.stack([batch_mean, rstd_batch, batch_scale, batch_shift])
    act_batch, act_second, output, branch_second, grad, d_branch, d_normal, second_sums = second_both(
        info, filtered, stats, after_attend, cotangent.reshape(tokens, model), gain_second, gain_final,
        point_out, second_in, second_out,
    )
    output = output.reshape(row_count, width, model)

    edge_before = lax.ppermute(
        jnp.concatenate([d_normal[width - half :], filtered[width - half :]], axis=0), "tm", up
    )
    edge_after = lax.ppermute(jnp.concatenate([d_normal[:half], filtered[:half]], axis=0), "tm", down)
    batch_grads = mesh_sum(second_sums[2:])
    branch_second = after(branch_second, batch_grads)
    d_joined, grad, d_attend, conv_small = conv_back(
        info, d_normal, filtered, edge_before, edge_after, stats, batch_grads / count, depth_weight,
        gated, gated_before, gated_after, joined_value, gate, point_in, after_attend, gain_conv, grad,
    )
    d_attend_near = swap(d_attend, "tm", 1)
    d_mixed = mixed_back(info, d_attend, d_attend_near, output_weight)
    d_query, d_key, d_value, skew_lines = attend_back(
        at, query, key, key_far, value, value_far, d_mixed, lse, bias, near_heads, head_dim
    )
    far_send, far_keep = input_back(info, (d_key, d_value), (pair, pair), (key_weight, value_weight), width)
    far_mine = far_keep + swap(far_send, "tm", 1).astype(jnp.float32)
    far_back = swap(far_mine.astype(jnp.bfloat16), "tm", 2)
    pair_send, pair_keep = input_back(
        info, (d_query, d_key, d_value), (0, 0, 0), (query_weight, key_weight, value_weight), width
    )
    d_input = pair_keep + swap(pair_send, "tm", 1).astype(jnp.float32) + far_back.astype(jnp.float32)
    _, scaled_attend, rstd_attend = normed_of(after_first, gain_attend)
    d_values, grad_gain_attend = norm_backward(d_input, scaled_attend, rstd_attend, gain_attend)
    grad = grad + d_values
    branch_first = (0.5 * grad).astype(jnp.bfloat16)
    branch_first_all = spread_tm(branch_first)
    grad_features, grad_gain_first = first_backward(
        info, grad, flat_features, gain_first, slope_first, first_in, first_out
    )
    grad_features = grad_features.reshape(row_count, width, model)

    act_first_all = spread_tm(act_first, act_far)
    mid_first, slope_first_part = again(place, act_first_all, first_in, groups)
    branch_second_all = spread_tm(branch_second)
    act_second_all = spread_tm(act_second, branch_second_all[2])
    mid_second, slope_second_part = again(place, act_second_all, second_in, groups)
    second_out_piece = reduce_rows(grad_out_of(mid_second, branch_second_all))
    second_in_piece = reduce_rows(
        grad_in_of(place, slope_second_part, act_second_all, branch_second_all, second_out, groups), True
    )
    first_out_piece = reduce_rows(grad_out_of(mid_first, branch_first_all))
    first_in_piece = reduce_rows(
        grad_in_of(place, slope_first_part, act_first_all, branch_first_all, first_out, groups), True
    )

    def near_exchange(array):
        return (near_half(array, 1, side), swap(near_half(array, 1, 1 - side), "tm", 1))

    conv_send, conv_keep = cross_grads(
        info,
        [
            ((act_conv, swap(act_conv, "tm", 1)), near_exchange(d_joined)),
            ((act_batch, swap(act_batch, "tm", 1)), near_exchange(d_branch)),
        ],
    )
    attend_send, attend_keep = cross_grads(
        info,
        [
            ((act_attend, act_near), (d_query,)),
            ((act_attend, act_near, act_far, act_cross), (d_key,)),
            ((act_attend, act_near, act_far, act_cross), (d_value,)),
            (
                (attended, swap(attended, "tm", 1)),
                (near_half(d_attend, 1, side), near_half(d_attend_near, 1, side)),
            ),
        ],
    )

    def far_sum(send, keep, *earlier):
        got = swap(after(send, *earlier), "tm", 2)
        return (keep.astype(jnp.float32) + got.astype(jnp.float32)).astype(jnp.bfloat16)

    conv_piece = reduce_rows(far_sum(conv_send, conv_keep, far_back))
    attend_piece = reduce_rows(far_sum(attend_send, attend_keep, branch_first_all[2]))
    second_in_pieces = spread_tm(second_in_piece, branch_first_all[2])
    second_out_pieces = spread_tm(second_out_piece, branch_first_all[2])
    conv_pieces = spread_tm(conv_piece, branch_first_all[2])
    attend_pieces = spread_tm(attend_piece)
    first_out_pieces = spread_tm(first_out_piece)
    first_in_pieces = spread_tm(first_in_piece)

    table_lines = sum(jnp.pad(skew_lines[:, r], ((0, 0), (7 - r, 0)))[:, :span] for r in range(8))
    near_grad = lax.dot_general(
        table_lines, one_hot, (((1,), (0,)), ((), ())), precision=lax.Precision.HIGHEST
    )
    grad_table = lax.dynamic_update_slice_in_dim(
        jnp.zeros((heads, bucket_count), jnp.float32), near_grad, side * near_heads, 0
    )
    small = jnp.concatenate(
        [
            grad_gain_first,
            grad_gain_attend[None],
            second_sums[:2],
            conv_small,
            jnp.pad(grad_table.reshape(1, -1), ((0, 0), (0, model - heads * bucket_count))),
        ],
        axis=0,
    )
    small = mesh_sum(small)
    share = model // groups
    gains = lax.dynamic_slice_in_dim(small[:5], row_place * share, share, 1)
    grad_depth = small[5 : 5 + taps]
    grad_table = small[5 + taps, : heads * bucket_count].reshape(heads, bucket_count)

    relative = jnp.arange(parts) ^ place
    crossed = (relative % 2) * 2 + relative // 2
    (grad_first_in,) = lay_columns(first_in_pieces, (model,), groups, relative)
    (grad_second_in,) = lay_columns(second_in_pieces, (model,), groups, relative)

    def lay_rows(pieces):
        size = pieces[0].shape[0]
        out = jnp.zeros((parts, size, model), jnp.float32)
        for k in range(parts):
            out = lax.dynamic_update_index_in_dim(out, pieces[k].astype(jnp.float32), place ^ k, 0)
        return out.reshape(parts * size, model)

    grad_first_out = lay_rows(first_out_pieces)
    grad_second_out = lay_rows(second_out_pieces)
    quarter = model // parts
    grad_query, grad_key, grad_value, grad_output = lay_columns(attend_pieces, (quarter,) * 4, 1, crossed)
    grad_point_in, grad_point_out = lay_columns(conv_pieces, (2 * quarter, quarter), 1, crossed)
    return (
        output,
        grad_features,
        gains[0],
        grad_first_in,
        grad_first_out,
        gains[1],
        grad_query,
        grad_key,
        grad_value,
        grad_output,
        grad_table,
        gains[4],
        grad_point_in,
        grad_depth,
        batch_grads[1],
        batch_grads[0],
        grad_point_out,
        gains[3],
        grad_second_in,
        grad_second_out,
        gains[2],
    )


def solution(mesh):
    rows3, rows2, rows1 = P("rows", "tm", None), P("rows", None), P("rows")
    in_specs = (rows3, rows1) + (P(),) * 20 + (rows3,)
    out_specs = (
        rows3, rows3, rows1, rows2, rows2, rows1, rows2, rows2, rows2, rows2, P(),
        rows1, rows2, P(), P(), P(), rows2, rows1, rows2, rows2, rows1,
    )
    return jax.shard_map(shards, mesh=mesh, in_specs=in_specs, out_specs=out_specs, check_vma=False)
```

```python
import functools

import jax
import jax.numpy as jnp
from jax import lax
from jax.experimental import pallas as pl
from jax.experimental.pallas import tpu as pltpu
from jax.sharding import PartitionSpec as P

EPS = 1e-05
NEGATIVE = -1e30
LANES = 128
MIB = 1024 * 1024
BLOCK = 1024
EFFORT = 0.0005


def swap(value, axis, bit):
    count = lax.axis_size(axis)
    return lax.ppermute(value, axis, [(i, i ^ bit) for i in range(count)])


def hops():
    wide, deep = lax.axis_size("tm"), lax.axis_size("rows")
    found = [("tm", 1 << b) for b in range(wide.bit_length() - 1)][::-1]
    return found + [("rows", 1 << b) for b in range(deep.bit_length() - 1)]


def mesh_sum(value, steps):
    for axis, bit in steps:
        value = value + swap(value, axis, bit)
    return value


def mesh_moments(count, mean, spread):
    for axis, bit in hops():
        sent = jnp.concatenate([mean[None], spread[None], jnp.broadcast_to(count, (1, mean.shape[0]))])
        got = swap(sent, axis, bit)
        other_mean, other_spread, other_count = got[0], got[1], got[2]
        total = count + other_count
        safe = jnp.maximum(total, 1.0)
        gap = other_mean - mean
        spread = spread + other_spread + gap * gap * (count * other_count / safe)
        mean = (count * mean + other_count * other_mean) / safe
        count = total
    return (count, mean, spread)


def tie(*values):
    return lax.optimization_barrier(values)


def spread_tm(piece):
    far = swap(piece, "tm", 2)
    return [piece, swap(piece, "tm", 1), far, swap(far, "tm", 1)]


def silu_pair(hidden):
    sigma = 0.5 * jnp.tanh(0.5 * hidden) + 0.5
    act = hidden * sigma
    return (act, sigma + act * (1.0 - sigma))


def normed_of(values, gain):
    mean = jnp.mean(values, axis=-1, keepdims=True)
    centered = values - mean
    rstd = lax.rsqrt(jnp.mean(centered * centered, axis=-1, keepdims=True) + EPS)
    scaled = centered * rstd
    return (scaled * gain, scaled, rstd)


def normed_back(grad, values, gain):
    _, scaled, rstd = normed_of(values, gain)
    weighted = grad * gain
    inner = weighted - jnp.mean(weighted, axis=-1, keepdims=True)
    inner = inner - scaled * jnp.mean(weighted * scaled, axis=-1, keepdims=True)
    return (rstd * inner, jnp.sum(grad * scaled, axis=0, keepdims=True))


def dot(left, right):
    return jnp.dot(left, right, preferred_element_type=jnp.float32)


def dot_turned(left, right):
    return lax.dot_general(left, right, (((1,), (1,)), ((), ())), preferred_element_type=jnp.float32)


def scalars():
    return [pl.BlockSpec(memory_space=pltpu.SMEM)]


def in_hbm(value):
    return pltpu.with_memory_space_constraint(value, pltpu.HBM)


def struct(*shape, kind=jnp.bfloat16):
    return jax.ShapeDtypeStruct(shape, kind)


class Arriving:
    def __init__(self, source, target, sem):
        self.copy = pltpu.make_async_copy(source, target, sem)
        self.target = target
        self.started = self.here = False

    def start(self):
        if not self.started:
            self.copy.start()
            self.started = True

    def get(self):
        self.start()
        if not self.here:
            self.copy.wait()
            self.here = True
        return self.target


class Leaving:
    def __init__(self, source, target, sem):
        self.ref = source
        self.target, self.sem = target, sem
        self.copy = None

    def send(self, source=None):
        self.copy = pltpu.make_async_copy(self.ref if source is None else source, self.target, self.sem)
        self.copy.start()


def flow_call(body, name, outs, scratch, info, operands, flops, mib=24, raw=(), late=(), deps=()):
    ins, results = len(operands), len(outs)

    def kernel(info, *refs):
        sources, targets = refs[:ins], refs[ins + len(deps) : ins + len(deps) + results]
        rest = refs[ins + len(deps) + results :]
        held, made = rest[:ins], rest[ins : ins + results]
        extra, sem_in, sem_out = rest[ins + results : -2], rest[-2], rest[-1]
        arriving = [
            (sources[k], held[k]) if k in raw else Arriving(sources[k], held[k], sem_in.at[k])
            for k in range(ins)
        ]
        for k in range(ins):
            if k not in raw and k not in late:
                arriving[k].start()
        leaving = [Leaving(made[k], targets[k], sem_out.at[k]) for k in range(results)]
        body(info, arriving, leaving, *extra)
        for item in leaving:
            if item.copy is None:
                item.send()
        for k in range(ins):
            if k not in raw:
                arriving[k].get()
        for item in leaving:
            item.copy.wait()

    moved = sum(o.size * o.dtype.itemsize for o in (*operands, *outs))
    return pl.pallas_call(
        kernel,
        in_specs=scalars() + [pl.BlockSpec(memory_space=pltpu.HBM)] * (ins + len(deps)),
        out_specs=[pl.BlockSpec(memory_space=pltpu.HBM)] * results,
        out_shape=[pltpu.HBM(o.shape, o.dtype) for o in outs],
        scratch_shapes=[pltpu.VMEM(o.shape, o.dtype) for o in (*operands, *outs)]
        + list(scratch)
        + [pltpu.SemaphoreType.DMA((ins,)), pltpu.SemaphoreType.DMA((results,))],
        compiler_params=pltpu.CompilerParams(vmem_limit_bytes=mib * MIB),
        cost_estimate=cost(flops, 0, moved),
        name=name,
    )(info, *[in_hbm(o) for o in (*operands, *deps)])


def cost(flops, transcendentals, moved):
    return pl.CostEstimate(
        flops=int(flops * EFFORT), transcendentals=int(transcendentals * EFFORT), bytes_accessed=int(moved * EFFORT)
    )


SIDE, FAR, OFFSET, LENGTH, ROW = range(5)


def row_bits():
    return lax.axis_size("rows").bit_length() - 1


def take_half(source, index, lead, size, ways=2):
    return [
        source[pl.ds(pl.multiple_of((k * ways + index) * size, size), size)] for k in range(lead)
    ]


def phases():
    return [(bit, 1) for bit in range(row_bits())]


def total_of(parts):
    total = parts[0].astype(jnp.float32)
    for part in parts[1:]:
        total = total + part.astype(jnp.float32)
    return total.astype(jnp.bfloat16)


def merge_kernel(counts, low, wide, share, info, ins, outs):
    ways = 1 << wide
    mine = (info[ROW] >> low) & (ways - 1)
    at = 0
    groups = []
    for count in counts:
        groups.append([item.get for item in ins[at : at + count]])
        at += count
    for g, gets in enumerate(groups):
        held = [get() for get in gets]
        lead = held[0].shape[0] // share // ways
        for offset in list(range(1, ways)) + [0]:
            out = outs[g * ways + (offset - 1) % ways]
            parts = [take_half(h, mine ^ offset, lead, share, ways) for h in held]
            for k in range(lead):
                out.ref[k * share : (k + 1) * share] = total_of([p[k] for p in parts])
            out.send()


def join_kernel(counts, info, ins, outs):
    begin = at = 0
    for count in counts:
        held = [item.get()[...] for item in ins[at : at + count]]
        at += count
        width = held[0].shape[1]
        outs[0].ref[:, begin : begin + width] = total_of(held)
        begin += width


class RowSum:
    def __init__(self, send, keep, share):
        self.share = share
        self.left = phases()
        self.exchange([send], keep)

    def exchange(self, sends, keep):
        low, _ = self.left.pop(0)
        self.terms = [keep] + [swap(x, "rows", (k + 1) << low) for k, x in enumerate(sends)]


def merge(info, sums, *deps):
    low, wide = sums[0].left[0]
    ways = 1 << wide
    outs = []
    for total in sums:
        rows, columns = total.terms[0].shape
        outs += [struct(rows // ways, columns)] * ways
    made = flow_call(
        functools.partial(merge_kernel, [len(t.terms) for t in sums], low, wide, sums[0].share), "merge",
        outs, [], info, tuple(x for t in sums for x in t.terms), 0, deps=deps,
    )
    for k, total in enumerate(sums):
        part = made[k * ways : (k + 1) * ways]
        total.exchange(part[:-1], part[-1])
    return sums[-1].terms[0]


def joined(info, sums, *deps):
    while sums[0].left:
        merge(info, sums)
    return join(info, [t.terms for t in sums], *deps)


def join(info, groups, *deps):
    columns = sum(g[0].shape[1] for g in groups)
    return flow_call(
        functools.partial(join_kernel, [len(g) for g in groups]), "join",
        [struct(groups[0][0].shape[0], columns)], [], info, tuple(x for g in groups for x in g), 0, deps=deps,
    )[0]


def opened(info, keep, got, share, *deps):
    rows, columns = keep.shape
    return RowSum(
        *flow_call(
            functools.partial(merge_kernel, [2], 0, 1, share), "merge",
            [struct(rows // 2, columns)] * 2, [], info, (keep, got), 0, deps=deps,
        ),
        share,
    )


def project_kernel(info, ins, outs, sem, rows):
    mine, other, *weights = ins
    side = info[SIDE]
    half = outs[0].ref.shape[1]
    lanes = pl.ds(pl.multiple_of(side * half, half), half)
    copies = [
        pltpu.make_async_copy(source.at[:, lanes], held.at[:, :half], sem.at[k])
        for k, (source, held) in enumerate(weights)
    ]
    for copy in copies:
        copy.start()
    tokens = mine.target.shape[0]
    rows[pl.ds(pl.multiple_of(side * tokens, tokens), tokens)] = mine.get()[...]
    rows[pl.ds(pl.multiple_of((1 - side) * tokens, tokens), tokens)] = other.get()[...]
    for copy, (_, held), out in zip(copies, weights, outs, strict=True):
        copy.wait()
        out.ref[...] = dot(rows[...], held[:, :half]).astype(jnp.bfloat16)
        out.send()


def project(info, mine, other, weights, deps=()):
    tokens, model = mine.shape
    pair = 2 * tokens
    return flow_call(
        project_kernel, "project",
        [struct(pair, model // 2)] * len(weights),
        [pltpu.SemaphoreType.DMA((len(weights),)), pltpu.VMEM((pair, model), jnp.bfloat16)],
        info, (mine, other, *weights), pair * model * model * len(weights),
        raw=tuple(range(2, 2 + len(weights))),
        deps=deps,
    )


def rows_of(length, first, count):
    frame = lax.broadcasted_iota(jnp.int32, (count, 1), 0) + first
    return ((frame >= 0) & (frame < length)).astype(jnp.float32)


def mix_kernel(
    info, own_ref, other_ref, weight, state_ref, gain_ref, value_w, gate_w, dep,
    attended_ref, after_ref, act_ref, value_ref, gate_ref, gated_ref,
):
    side = info[SIDE]
    tokens, half = own_ref.shape

    @pl.when(pl.program_id(0) == 0)
    def _():
        attended_ref[:, pl.ds(pl.multiple_of(side * half, half), half)] = own_ref[...]
        attended_ref[:, pl.ds(pl.multiple_of((1 - side) * half, half), half)] = other_ref[...]
        values = state_ref[...] + dot(attended_ref[...], weight[...])
        after_ref[...] = values
        act_ref[...] = normed_of(values, gain_ref[...])[0].astype(jnp.bfloat16)

    value = dot(act_ref[...], value_w[...])
    gate = 0.5 * jnp.tanh(0.5 * dot(act_ref[...], gate_w[...])) + 0.5
    value_ref[...] = value.astype(jnp.bfloat16)
    gate_ref[...] = gate.astype(jnp.bfloat16)
    gated_ref[...] = value * gate * rows_of(info[LENGTH], info[OFFSET], tokens)


def mix(info, own, other, weight, state, gain, point_in, dep):
    tokens, model = state.shape
    step = 512
    steps = model // step
    flat = (tokens, model)
    column = pl.BlockSpec((tokens, step), lambda i: (0, i))
    return pl.pallas_call(
        mix_kernel,
        grid=(steps,),
        in_specs=scalars() + [
            whole(own.shape), whole(own.shape), whole(weight.shape), whole(flat), whole((1, model)),
            pl.BlockSpec((model, step), lambda i: (0, i)),
            pl.BlockSpec((model, step), lambda i: (0, steps + i)),
            pl.BlockSpec(memory_space=pl.ANY),
        ],
        out_specs=[whole(flat)] * 3 + [column] * 3,
        out_shape=[
            pltpu.HBM(flat, jnp.bfloat16), pltpu.HBM(flat, jnp.float32), pltpu.HBM(flat, jnp.bfloat16),
            pltpu.HBM(flat, jnp.bfloat16), pltpu.HBM(flat, jnp.bfloat16), pltpu.HBM(flat, jnp.float32),
        ],
        compiler_params=pltpu.CompilerParams(vmem_limit_bytes=32 * MIB),
        cost_estimate=cost(
            6 * tokens * model * model,
            tokens * model,
            6 * model * model + 20 * tokens * model,
        ),
        name="mix",
    )(info, own, other, weight, state, gain[None], point_in, point_in, in_hbm(dep))


def filter_kernel(info, ins, outs, wide):
    gated_ref, before_ref, after_ref, taps_ref = [item.get() for item in ins]
    filtered_ref, moments_ref = [item.ref for item in outs]
    tokens = gated_ref.shape[0]
    half = before_ref.shape[0]
    wide[8 : 8 + tokens] = gated_ref[...]
    wide[8 - half : 8] = before_ref[...].astype(jnp.float32)
    wide[8 + tokens : 8 + tokens + half] = after_ref[...].astype(jnp.float32)
    filtered = taps_ref[0:1] * wide[8 - half : 8 - half + tokens]
    for tap in range(1, taps_ref.shape[0]):
        filtered = filtered + taps_ref[tap : tap + 1] * wide[8 - half + tap : 8 - half + tap + tokens]
    filtered_ref[...] = filtered
    outs[0].send()
    valid = rows_of(info[LENGTH], info[OFFSET], tokens)
    count = jnp.clip(info[LENGTH] - info[OFFSET], 1, tokens).astype(jnp.float32)
    mean = jnp.sum(filtered * valid, axis=0, keepdims=True) / count
    gap = (filtered - mean) * valid
    moments_ref[0:1] = mean
    moments_ref[1:2] = jnp.sum(gap * gap, axis=0, keepdims=True)


def filter_frames(info, gated, before, later, depth):
    tokens, model = gated.shape
    return flow_call(
        filter_kernel, "filter_frames",
        [struct(tokens, model, kind=jnp.float32), struct(2, model, kind=jnp.float32)],
        [pltpu.VMEM((tokens + 16, model), jnp.float32)],
        info, (gated, before, later, depth), 10 * tokens * model,
    )


def weight_copies(pair_in, pair_out, sem, block):
    def at(i):
        lanes = pl.ds(pl.multiple_of(i * block, block), block)
        return (
            pltpu.make_async_copy(pair_in[0].at[:, lanes], pair_in[1].at[:, lanes], sem.at[0, i]),
            pltpu.make_async_copy(pair_out[0].at[lanes, :], pair_out[1].at[lanes, :], sem.at[1, i]),
        )

    return at


def second_kernel(info, ins, outs, sem, state, grad, total, slopes, low_ref):
    filtered, stats, state_in, cot, gain, final_gain, point, pair_in, pair_out = ins
    w_in, w_out = pair_in[1], pair_out[1]
    act_batch, act_out, output, branch_out, grad_out, conv_send, conv_keep, d_norm_out, sums = outs
    tokens = filtered.target.shape[0]
    steps = w_in.shape[1] // BLOCK
    valid = rows_of(info[LENGTH], info[OFFSET], tokens)
    copies = weight_copies(pair_in, pair_out, sem, BLOCK)
    filtered_ref, stats_ref = filtered.get(), stats.get()

    def normalized():
        scaled = (filtered_ref[...] - stats_ref[0:1]) * stats_ref[1:2]
        return (scaled, scaled * stats_ref[2:3] + stats_ref[3:4])

    act = silu_pair(normalized()[1])[0].astype(jnp.bfloat16)
    act_batch.ref[...] = act
    point_ref = point.get()
    for i in range(2):
        for copy in copies(i):
            copy.start()
    act_batch.send()
    values = state_in.get()[...] + dot(act, point_ref[...])
    state[...] = values
    act_ref = act_out.ref
    act_ref[...] = normed_of(values, gain.get()[...])[0].astype(jnp.bfloat16)
    act_out.send()
    cot.start()
    total[...] = jnp.zeros_like(total)

    def forward(i, carry):
        lanes = pl.ds(pl.multiple_of(i * BLOCK, BLOCK), BLOCK)
        for copy in copies(i):
            copy.wait()

        @pl.when(i + 2 < steps)
        def _():
            for copy in copies(i + 2):
                copy.start()

        mid, slope = silu_pair(dot(act_ref[...], w_in[:, lanes]))
        slopes[:, lanes] = slope.astype(jnp.bfloat16)
        total[...] += dot(mid.astype(jnp.bfloat16), w_out[lanes, :])
        return carry

    lax.fori_loop(0, steps, forward, 0)
    values = state[...] + 0.5 * total[...]
    final = final_gain.get()[...]
    normed, _, _ = normed_of(values, final)
    output.ref[...] = (normed * valid).astype(jnp.bfloat16)
    output.send()
    begin, sums.ref[0:1] = normed_back(cot.get()[...].astype(jnp.float32) * valid, values, final)
    grad[...] = begin
    branch_ref = branch_out.ref
    branch_ref[...] = (0.5 * begin).astype(jnp.bfloat16)
    branch_out.send()
    total[...] = jnp.zeros_like(total)

    def backward(i, carry):
        lanes = pl.ds(pl.multiple_of(i * BLOCK, BLOCK), BLOCK)
        part = dot_turned(branch_ref[...], w_out[lanes, :])
        part = (part * slopes[:, lanes].astype(jnp.float32)).astype(jnp.bfloat16)
        total[...] += dot_turned(part, w_in[:, lanes])
        return carry

    lax.fori_loop(0, steps, backward, 0)
    d_values, sums.ref[1:2] = normed_back(total[...], state[...], gain.get()[...])
    later = grad[...] + d_values
    grad_out.ref[...] = later
    grad_out.send()
    low = later.astype(jnp.bfloat16)
    low_ref[...] = low
    side = info[SIDE]
    half = low.shape[1] // 2
    conv_send.send(low_ref.at[:, pl.ds(pl.multiple_of((1 - side) * half, half), half)])
    conv_keep.send(low_ref.at[:, pl.ds(pl.multiple_of(side * half, half), half)])
    scaled, normal = normalized()
    d_norm = dot_turned(low, point.get()[...]) * silu_pair(normal)[1] * valid
    d_norm_out.ref[...] = d_norm
    d_norm_out.send()
    sums.ref[2:3] = jnp.sum(d_norm, axis=0, keepdims=True)
    sums.ref[3:4] = jnp.sum(d_norm * scaled, axis=0, keepdims=True)


def second_both(info, filtered, stats, state, cotangent, gain, final_gain, point_out, w_in, w_out, deps):
    tokens, model = state.shape
    inner = w_in.shape[1]
    flat = (tokens, model)
    low, high = struct(*flat), struct(*flat, kind=jnp.float32)
    return flow_call(
        second_kernel, "second_both",
        [low, low, low, low, high, struct(tokens, model // 2), struct(tokens, model // 2), high,
         struct(4, model, kind=jnp.float32)],
        [
            pltpu.SemaphoreType.DMA((2, inner // BLOCK)),
            pltpu.VMEM(flat, jnp.float32), pltpu.VMEM(flat, jnp.float32), pltpu.VMEM(flat, jnp.float32),
            pltpu.VMEM((tokens, inner), jnp.bfloat16), pltpu.VMEM(flat, jnp.bfloat16),
        ],
        info,
        (filtered, stats, state, cotangent, gain[None], final_gain[None], point_out, w_in, w_out),
        8 * tokens * model * inner + 4 * tokens * model * model,
        mib=48,
        raw=(7, 8),
        late=(3,),
        deps=deps,
    )


def conv_back_kernel(info, ins, outs, wide, gated_wide, joined_ref):
    d_norm_ref, filtered_ref, before_ref, after_ref, stats_ref, sums_ref, taps_ref = [i.get() for i in ins[:7]]
    for item in ins[10:13]:
        item.start()
    gated_ref, gated_before, gated_after = [i.get() for i in ins[7:10]]
    value, gate, point, state, gain, grad = ins[10:]
    out_ref, low_ref, small_ref = [item.ref for item in outs[2:]]
    tokens, model = d_norm_ref.shape
    half = gated_before.shape[0]

    def d_filtered(d_norm, filtered, first):
        valid = rows_of(info[LENGTH], first, d_norm.shape[0])
        scaled = (filtered - stats_ref[0:1]) * stats_ref[1:2]
        inner = d_norm - sums_ref[0:1] - scaled * sums_ref[1:2]
        return valid * (stats_ref[2:3] * stats_ref[1:2]) * inner

    offset = info[OFFSET]
    wide[8 : 8 + tokens] = d_filtered(d_norm_ref[...], filtered_ref[...], offset)
    wide[8 - half : 8] = d_filtered(before_ref[:half], before_ref[half:], offset - half)
    wide[8 + tokens : 8 + tokens + half] = d_filtered(after_ref[:half], after_ref[half:], offset + tokens)
    gated_wide[8 : 8 + tokens] = gated_ref[...]
    gated_wide[8 - half : 8] = gated_before[...].astype(jnp.float32)
    gated_wide[8 + tokens : 8 + tokens + half] = gated_after[...].astype(jnp.float32)
    d_gated = jnp.zeros((tokens, model), jnp.float32)
    for tap in range(taps_ref.shape[0]):
        begin = 8 + half - tap
        d_gated = d_gated + taps_ref[tap : tap + 1] * wide[begin : begin + tokens]
        begin = 8 - half + tap
        small_ref[1 + tap : 2 + tap] = jnp.sum(
            wide[8 : 8 + tokens] * gated_wide[begin : begin + tokens], axis=0, keepdims=True
        )
    for item in ins[13:]:
        item.start()
    d_gated = d_gated * rows_of(info[LENGTH], offset, tokens)
    gate = gate.get()[...].astype(jnp.float32)
    d_value = d_gated * gate
    joined_ref[:, :model] = d_value.astype(jnp.bfloat16)
    joined_ref[:, model:] = (d_value * value.get()[...].astype(jnp.float32) * (1.0 - gate)).astype(jnp.bfloat16)
    side = info[SIDE]
    outs[0].send(joined_ref.at[:, pl.ds(pl.multiple_of((1 - side) * model, model), model)])
    outs[1].send(joined_ref.at[:, pl.ds(pl.multiple_of(side * model, model), model)])
    d_values, small_ref[0:1] = normed_back(
        dot_turned(joined_ref[...], point.get()[...]), state.get()[...], gain.get()[...]
    )
    later = grad.get()[...] + d_values
    low_ref[...] = later.astype(jnp.bfloat16)
    outs[3].send()
    out_ref[...] = later


def conv_back(info, d_norm, filtered, before, later, stats, sums, depth, gated, gated_before, gated_after,
              value, gate, point_in, state, gain, grad):
    tokens, model = d_norm.shape
    return flow_call(
        conv_back_kernel, "conv_back",
        [
            struct(tokens, model), struct(tokens, model),
            struct(tokens, model, kind=jnp.float32), struct(tokens, model),
            struct(1 + depth.shape[0], model, kind=jnp.float32),
        ],
        [pltpu.VMEM((tokens + 16, model), jnp.float32)] * 2 + [pltpu.VMEM((tokens, 2 * model), jnp.bfloat16)],
        info,
        (d_norm, filtered, before, later, stats, sums, depth, gated, gated_before, gated_after, value,
         gate, point_in, state, gain[None], grad),
        4 * tokens * model * model,
        mib=32,
        late=tuple(range(10, 16)),
    )


def add_kernel(info, ins, outs):
    total = ins[0].get()[...].astype(jnp.float32)
    for item in ins[1:]:
        total = total + item.get()[...].astype(jnp.float32)
    outs[0].ref[...] = total.astype(outs[0].ref.dtype)


def add(info, terms, kind, *deps):
    return flow_call(
        add_kernel, "add", [struct(*terms[0].shape, kind=kind)], [], info, tuple(terms), 0, deps=deps
    )[0]


def branch_kernel(info, ins, outs):
    keep, got, far, state, gain, grad = ins
    d_input = keep.get()[...] + got.get()[...].astype(jnp.float32) + far.get()[...].astype(jnp.float32)
    d_values, outs[2].ref[...] = normed_back(d_input, state.get()[...], gain.get()[...])
    later = grad.get()[...] + d_values
    outs[1].ref[...] = (0.5 * later).astype(jnp.bfloat16)
    outs[1].send()
    outs[0].ref[...] = later


def branch_of(info, keep, got, far, state, gain, grad, deps):
    tokens, model = keep.shape
    return flow_call(
        branch_kernel, "branch",
        [struct(tokens, model, kind=jnp.float32), struct(tokens, model), struct(1, model, kind=jnp.float32)],
        [], info, (keep, got, far, state, gain[None], grad), 0, deps=deps,
    )


def input_back_kernel(count, base, info, ins, outs, sem):
    grads, weights = ins[:count], ins[count:]
    send_ref, keep_ref = outs[0].ref, outs[1].ref
    tokens = send_ref.shape[0]
    side = info[SIDE]
    half = weights[0][0].shape[1] // 2
    lanes = pl.ds(pl.multiple_of(side * half, half), half)
    copies = [
        pltpu.make_async_copy(source.at[:, lanes], held.at[:, :half], sem.at[k])
        for k, (source, held) in enumerate(weights)
    ]
    for copy in copies:
        copy.start()
    grads = [grad.get() for grad in grads]
    for copy in copies:
        copy.wait()

    def total(which):
        out = None
        for first, grad, (_, held) in zip(base, grads, weights, strict=True):
            rows = pl.ds(pl.multiple_of(first + which * tokens, LANES), tokens)
            part = dot_turned(grad[rows], held[:, :half])
            out = part if out is None else out + part
        return out

    send_ref[...] = total(1 - side).astype(jnp.bfloat16)
    outs[0].send()
    keep_ref[...] = total(side)


def input_back(info, grads, base, weights, tokens, deps=()):
    model = weights[0].shape[0]
    count = len(grads)
    return flow_call(
        functools.partial(input_back_kernel, count, base), "input_back",
        [struct(tokens, model), struct(tokens, model, kind=jnp.float32)],
        [pltpu.SemaphoreType.DMA((count,))],
        info, (*grads, *weights), 2 * tokens * model * model * count,
        mib=32, raw=tuple(range(count, 2 * count)), deps=deps,
    )


def cross_kernel(layout, split, lead, chunk, info, refs, outs, left_rows, right_rows, *held):
    far, side = info[FAR], info[SIDE]
    at = 0
    begin = 0
    for pieces, width in layout:
        lefts, right = refs[at : at + pieces], refs[at + pieces : at + pieces + (2 if width < 0 else 1)]
        at += pieces + len(right)
        tokens = lefts[0].target.shape[0]
        for k, left in enumerate(lefts):
            spot = (k // 2 * 2 + (side if k % 2 == 0 else 1 - side)) * tokens
            left_rows[pl.ds(pl.multiple_of(spot, tokens), tokens)] = left.get()[...]
        size = abs(width)
        half = size // 2 if split else size
        if len(right) == 2:
            for k, piece in enumerate(right):
                spot = (side if k == 0 else 1 - side) * tokens
                held = piece.get()
                lanes = pl.ds(0, size)
                if held.shape[1] != size:
                    lanes = pl.ds(pl.multiple_of(side * size, size), size)
                right_rows[pl.ds(pl.multiple_of(spot, tokens), tokens), :size] = held[:, lanes]
            source = right_rows
        else:
            source = right[0].get()
        count = pieces * tokens
        targets = ((1 - far, outs[0].ref), (far, outs[1].ref)) if split else ((0, held[0]),)
        for which, target in targets:
            lanes = pl.ds(pl.multiple_of(which * half, half), half)
            target[:, begin : begin + half] = lax.dot_general(
                left_rows[:count], source[:count, lanes], (((0,), (0,)), ((), ())),
                preferred_element_type=jnp.float32,
            ).astype(jnp.bfloat16)
        begin += half
    if not split:
        store_halves(held[0], info[ROW] & 1, lead, chunk, outs[0].ref, outs[1].ref)


def cross_grads(info, terms, split=True, deps=()):
    operands, layout = [], []
    total = flops = 0
    for lefts, rights, width in terms:
        operands += [*lefts, *rights]
        layout.append((len(lefts), -width if len(rights) == 2 else width))
        total += width // 2 if split else width
        tokens, model = lefts[0].shape
        flops += 2 * len(lefts) * tokens * model * width
    deepest = max(len(lefts) for lefts, *_ in terms) * tokens
    widest = max(width for *_, width in terms)
    size = model >> row_bits()
    rows = model if split else model // 2
    scratch = [pltpu.VMEM((deepest, model), jnp.bfloat16), pltpu.VMEM((deepest, widest), jnp.bfloat16)]
    if not split:
        scratch.append(pltpu.VMEM((model, total), jnp.bfloat16))
    return flow_call(
        functools.partial(cross_kernel, layout, split, model // size // 2, size), "cross_grads",
        [struct(rows, total)] * 2, scratch, info, tuple(operands), flops, mib=40, deps=deps,
    )


def first_back_kernel(info, ins, outs, sem, branch, total):
    grad, x, gain, slope, pair_in, pair_out = ins
    w_in, w_out = pair_in[1], pair_out[1]
    steps = w_in.shape[1] // BLOCK
    copies = weight_copies(pair_in, pair_out, sem, BLOCK)
    for i in range(2):
        for copy in copies(i):
            copy.start()
    grad_ref = grad.get()
    branch[...] = (0.5 * grad_ref[...]).astype(jnp.bfloat16)
    total[...] = jnp.zeros_like(total)
    slope_ref = slope.get()
    x.start()

    def backward(i, carry):
        lanes = pl.ds(pl.multiple_of(i * BLOCK, BLOCK), BLOCK)
        for copy in copies(i):
            copy.wait()

        @pl.when(i + 2 < steps)
        def _():
            for copy in copies(i + 2):
                copy.start()

        part = dot_turned(branch[...], w_out[lanes, :])
        part = (part * slope_ref[:, lanes].astype(jnp.float32)).astype(jnp.bfloat16)
        total[...] += dot_turned(part, w_in[:, lanes])
        return carry

    lax.fori_loop(0, steps, backward, 0)
    d_values, outs[1].ref[...] = normed_back(total[...], x.get()[...].astype(jnp.float32), gain.get()[...])
    outs[0].ref[...] = (grad_ref[...] + d_values).astype(jnp.bfloat16)


def first_backward(info, grad, features, gain, slope, w_in, w_out, deps):
    tokens, model = features.shape
    inner = w_in.shape[1]
    return flow_call(
        first_back_kernel, "first_backward",
        [struct(tokens, model), struct(1, model, kind=jnp.float32)],
        [pltpu.SemaphoreType.DMA((2, inner // BLOCK)), pltpu.VMEM((tokens, model), jnp.bfloat16), pltpu.VMEM((tokens, model), jnp.float32)],
        info, (grad, features, gain[None], slope, w_in, w_out), 4 * tokens * model * inner,
        mib=40, raw=(4, 5), late=(1,), deps=deps,
    )


def norm_backward(grad, scaled, rstd, gain):
    weighted = grad * gain
    inner = weighted - jnp.mean(weighted, axis=-1, keepdims=True)
    inner = inner - scaled * jnp.mean(weighted * scaled, axis=-1, keepdims=True)
    return (rstd * inner, jnp.sum(grad * scaled, axis=0))


def first_kernel(x_ref, gain_ref, next_gain_ref, w_in, w_out, state_ref, act_ref, slope_ref, next_ref, total):
    step = pl.program_id(0)

    @pl.when(step == 0)
    def _():
        values = x_ref[...].astype(jnp.float32)
        act_ref[...] = normed_of(values, gain_ref[...])[0].astype(jnp.bfloat16)
        total[...] = jnp.zeros_like(total)

    mid, slope = silu_pair(dot(act_ref[...], w_in[...]))
    slope_ref[...] = slope.astype(jnp.bfloat16)
    total[...] += dot(mid.astype(jnp.bfloat16), w_out[...])

    @pl.when(step == pl.num_programs(0) - 1)
    def _():
        values = x_ref[...].astype(jnp.float32) + 0.5 * total[...]
        state_ref[...] = values
        next_ref[...] = normed_of(values, next_gain_ref[...])[0].astype(jnp.bfloat16)


def whole(shape):
    return pl.BlockSpec(shape, lambda *_: (0,) * len(shape))


def first_forward(features, gain, next_gain, w_in, w_out):
    tokens, model = features.shape
    inner = w_in.shape[1]
    return pl.pallas_call(
        first_kernel,
        grid=(inner // BLOCK,),
        in_specs=[
            whole((tokens, model)),
            whole((1, model)),
            whole((1, model)),
            pl.BlockSpec((model, BLOCK), lambda i: (0, i)),
            pl.BlockSpec((BLOCK, model), lambda i: (i, 0)),
        ],
        out_specs=[
            whole((tokens, model)),
            whole((tokens, model)),
            pl.BlockSpec((tokens, BLOCK), lambda i: (0, i)),
            whole((tokens, model)),
        ],
        out_shape=[
            pltpu.HBM((tokens, model), jnp.float32),
            pltpu.HBM((tokens, model), jnp.bfloat16),
            pltpu.HBM((tokens, inner), jnp.bfloat16),
            pltpu.HBM((tokens, model), jnp.bfloat16),
        ],
        scratch_shapes=[pltpu.VMEM((tokens, model), jnp.float32)],
        compiler_params=pltpu.CompilerParams(vmem_limit_bytes=40 * MIB),
        cost_estimate=cost(
            4 * tokens * model * inner,
            2 * tokens * inner,
            4 * model * inner + 2 * tokens * inner,
        ),
        name="first_forward",
    )(in_hbm(features), gain[None], next_gain[None], in_hbm(w_in), in_hbm(w_out))


def take_kernel(place, source, target):
    target[...] = source[...]


def take_columns(weight, groups, place, parts):
    model, total = weight.shape
    block = total // groups // parts
    if block % LANES:
        cut = weight.reshape(model, groups, parts, block)
        return lax.dynamic_index_in_dim(cut, place, 2, keepdims=False).reshape(model, -1)
    return pl.pallas_call(
        take_kernel,
        out_shape=jax.ShapeDtypeStruct((model, total // parts), weight.dtype),
        grid_spec=pltpu.PrefetchScalarGridSpec(
            num_scalar_prefetch=1,
            grid=(groups,),
            in_specs=[pl.BlockSpec((model, block), lambda g, at: (0, g * parts + at[0]))],
            out_specs=pl.BlockSpec((model, block), lambda g, at: (0, g)),
        ),
        name="take_columns",
    )(place.reshape(1), weight)


def take_rows(weight, groups, place, parts):
    total, model = weight.shape
    cut = weight.reshape(groups, parts, total // groups // parts, model)
    return lax.dynamic_index_in_dim(cut, place, 1, keepdims=False).reshape(-1, model)


def lay_kernel(parts, widths, groups, places, *refs):
    pieces, targets = refs[:parts], refs[parts:]
    for k in range(parts):
        begin = 0
        for width, target in zip(widths, targets, strict=True):
            block = width // groups
            for g in range(groups):
                at = pl.multiple_of((g * parts + places[k]) * block, LANES)
                source = pieces[k][:, begin + g * block : begin + (g + 1) * block]
                target[:, pl.ds(at, block)] = source.astype(jnp.float32)
            begin += width


def lay_columns(pieces, widths, groups, places):
    rows = pieces[0].shape[0]
    parts = len(pieces)
    if any((width // groups) % LANES for width in widths):
        outs, begin = [], 0
        stacked = jnp.zeros((parts, *pieces[0].shape), pieces[0].dtype)
        for k in range(parts):
            stacked = lax.dynamic_update_index_in_dim(stacked, pieces[k], places[k], 0)
        for width in widths:
            cut = stacked[:, :, begin : begin + width].reshape(parts, rows, groups, width // groups)
            outs.append(cut.transpose(1, 2, 0, 3).reshape(rows, parts * width).astype(jnp.float32))
            begin += width
        return outs
    return pl.pallas_call(
        functools.partial(lay_kernel, parts, widths, groups),
        out_shape=[jax.ShapeDtypeStruct((rows, parts * width), jnp.float32) for width in widths],
        grid_spec=pltpu.PrefetchScalarGridSpec(
            num_scalar_prefetch=1,
            grid=(1,),
            in_specs=[pl.BlockSpec(p.shape, lambda i, at: (0, 0)) for p in pieces],
            out_specs=[pl.BlockSpec((rows, parts * width), lambda i, at: (0, 0)) for width in widths],
        ),
        compiler_params=pltpu.CompilerParams(vmem_limit_bytes=24 * MIB),
        name="lay_columns",
    )(places, *pieces)


def skew_kernel(line, out):
    length = line.shape[-1]
    width = out.shape[-1]
    spread = jnp.broadcast_to(line[0], (LANES, length))
    rolled = pltpu.roll(spread, length - (LANES - 1), 1, stride=1, stride_axis=0)
    out[0] = rolled[:, :width]


def skewed(lines):
    heads, _, length = lines.shape
    width = length - LANES
    return pl.pallas_call(
        skew_kernel,
        out_shape=pltpu.HBM((heads, LANES, width), jnp.float32),
        grid=(heads,),
        in_specs=[pl.BlockSpec((1, 1, length), lambda h: (h, 0, 0))],
        out_specs=pl.BlockSpec((1, LANES, width), lambda h: (h, 0, 0)),
        name="bias_rows",
    )(lines)


def attend_kernel(
    scale, at, q_ref, k_pair, k_far, v_pair, v_far, bias_ref, own_ref, other_ref, lse_ref,
    k_ref, vt_ref, s_ref, p_ref, out_ref,
):
    tile = q_ref.shape[0]
    blocks = k_ref.shape[0] // LANES
    pair = k_pair.shape[0]
    length = at[blocks * 2]

    @pl.when(pl.program_id(1) == 0)
    def _():
        k_ref[:pair] = k_pair[...]
        k_ref[pair:] = k_far[...]
        vt_ref[:, :pair] = v_pair[...].T
        vt_ref[:, pair:] = v_far[...].T

    begin = pl.program_id(1) * tile
    s_ref[...] = lax.dot_general(
        k_ref[...], q_ref[...], (((1,), (1,)), ((), ())), preferred_element_type=jnp.float32
    )
    frame = lax.broadcasted_iota(jnp.int32, (LANES, tile), 0)
    top = jnp.full((1, tile), NEGATIVE, jnp.float32)
    for b in range(blocks):
        lanes = pl.ds(pl.multiple_of(at[b] + begin, LANES), tile)
        s = s_ref[b * LANES : (b + 1) * LANES] * scale + bias_ref[0, :, lanes]
        s = jnp.where(frame < length - at[blocks + b], s, NEGATIVE)
        s_ref[b * LANES : (b + 1) * LANES] = s
        top = jnp.maximum(top, jnp.max(s, axis=0, keepdims=True))
    total = jnp.zeros((1, tile), jnp.float32)
    for b in range(blocks):
        p = jnp.exp(s_ref[b * LANES : (b + 1) * LANES] - top)
        total = total + jnp.sum(p, axis=0, keepdims=True)
        p_ref[b * LANES : (b + 1) * LANES] = p.astype(jnp.bfloat16)
    mixed = jnp.dot(vt_ref[...], p_ref[...], preferred_element_type=jnp.float32) / total
    out_ref[...] = mixed.T.astype(jnp.bfloat16)
    half = tile // 2
    side = at[blocks * 2 + 1]
    own_ref[...] = out_ref[pl.ds(pl.multiple_of(side * half, half), half)]
    other_ref[...] = out_ref[pl.ds(pl.multiple_of((1 - side) * half, half), half)]
    lse_ref[0] = top + jnp.log(total)


def attend(at, query, key, key_far, value, value_far, bias, heads, head_dim):
    queries, keys = query.shape[0], 2 * key.shape[0]
    tile = queries
    width = bias.shape[-1]
    grid_spec = pltpu.PrefetchScalarGridSpec(
        num_scalar_prefetch=1,
        grid=(heads, queries // tile),
        in_specs=[
            pl.BlockSpec((tile, head_dim), lambda h, i, at: (i, h)),
            pl.BlockSpec((keys // 2, head_dim), lambda h, i, at: (0, h)),
            pl.BlockSpec((keys // 2, head_dim), lambda h, i, at: (0, h)),
            pl.BlockSpec((keys // 2, head_dim), lambda h, i, at: (0, h)),
            pl.BlockSpec((keys // 2, head_dim), lambda h, i, at: (0, h)),
            pl.BlockSpec((1, LANES, width), lambda h, i, at: (h, 0, 0)),
        ],
        out_specs=[
            pl.BlockSpec((tile // 2, head_dim), lambda h, i, at: (0, h)),
            pl.BlockSpec((tile // 2, head_dim), lambda h, i, at: (0, h)),
            pl.BlockSpec((1, 1, tile), lambda h, i, at: (h, 0, i)),
        ],
        scratch_shapes=[
            pltpu.VMEM((keys, head_dim), jnp.bfloat16),
            pltpu.VMEM((head_dim, keys), jnp.bfloat16),
            pltpu.VMEM((keys, tile), jnp.float32),
            pltpu.VMEM((keys, tile), jnp.bfloat16),
            pltpu.VMEM((tile, head_dim), jnp.bfloat16),
        ],
    )
    return pl.pallas_call(
        functools.partial(attend_kernel, head_dim ** (-0.5)),
        out_shape=[
            pltpu.HBM((queries // 2, heads * head_dim), jnp.bfloat16),
            pltpu.HBM((queries // 2, heads * head_dim), jnp.bfloat16),
            pltpu.HBM((heads, 1, queries), jnp.float32),
        ],
        grid_spec=grid_spec,
        compiler_params=pltpu.CompilerParams(vmem_limit_bytes=24 * MIB),
        cost_estimate=cost(
            4 * heads * queries * keys * head_dim,
            heads * queries * keys,
            4 * heads * LANES * width + 4 * heads * head_dim * (queries + keys),
        ),
        name="attend",
    )(at, query, key, key_far, value, value_far, in_hbm(bias))


def attend_back_kernel(
    scale, at, q_ref, k_pair, k_far, v_pair, v_far, da_own, da_near, wo_ref, wk_ref, wv_ref, lse_ref, bias_ref,
    dq_ref, dk_ref, dv_ref, line_ref, send_ref, far_ref,
    do_ref, all_dk, all_dv, k_ref, v_ref, kt_ref, s_ref, dp_ref, p_ref, ds_ref, skew_ref,
):
    tile = q_ref.shape[0]
    blocks = k_ref.shape[0] // LANES
    length = at[blocks * 2]
    pair = k_pair.shape[0]

    side = at[blocks * 2 + 1]
    own = da_own.shape[0]
    mine = pl.ds(pl.multiple_of(side * own, own), own)
    other = pl.ds(pl.multiple_of((1 - side) * own, own), own)
    do_ref[mine] = dot_turned(da_own[...], wo_ref[...]).astype(jnp.bfloat16)
    do_ref[other] = dot_turned(da_near[...], wo_ref[...]).astype(jnp.bfloat16)
    k_ref[:pair] = k_pair[...]
    k_ref[pair:] = k_far[...]
    v_ref[:pair] = v_pair[...]
    v_ref[pair:] = v_far[...]
    kt_ref[...] = k_ref[...].T
    skew_ref[...] = jnp.zeros_like(skew_ref)
    s_ref[...] = lax.dot_general(
        k_ref[...], q_ref[...], (((1,), (1,)), ((), ())), preferred_element_type=jnp.float32
    )
    dp_ref[...] = lax.dot_general(
        v_ref[...], do_ref[...], (((1,), (1,)), ((), ())), preferred_element_type=jnp.float32
    )
    frame = lax.broadcasted_iota(jnp.int32, (LANES, tile), 0)
    lse = lse_ref[0]
    delta = jnp.zeros((1, tile), jnp.float32)
    for b in range(blocks):
        rows = slice(b * LANES, (b + 1) * LANES)
        lanes = pl.ds(pl.multiple_of(at[b], LANES), tile)
        s = s_ref[rows] * scale + bias_ref[0, :, lanes]
        s = jnp.where(frame < length - at[blocks + b], s, NEGATIVE)
        p = jnp.exp(s - lse)
        s_ref[rows] = p
        p_ref[rows] = p.astype(jnp.bfloat16)
        delta = delta + jnp.sum(p * dp_ref[rows], axis=0, keepdims=True)
    for b in range(blocks):
        rows = slice(b * LANES, (b + 1) * LANES)
        lanes = pl.ds(pl.multiple_of(at[b], LANES), tile)
        ds = (s_ref[rows] * (dp_ref[rows] - delta)).astype(jnp.bfloat16)
        ds_ref[rows] = ds
        skew_ref[:, lanes] += ds.astype(jnp.float32)
    dv = jnp.dot(p_ref[...], do_ref[...], preferred_element_type=jnp.float32).astype(jnp.bfloat16)
    dk = jnp.dot(ds_ref[...], q_ref[...], preferred_element_type=jnp.float32) * scale
    dk = dk.astype(jnp.bfloat16)
    dq = jnp.dot(kt_ref[...], ds_ref[...], preferred_element_type=jnp.float32) * scale
    dq_ref[...] = dq.T.astype(jnp.bfloat16)
    dk_ref[...] = dk
    dv_ref[...] = dv
    head = pl.program_id(0)
    all_dk[head] = dk[pair:]
    all_dv[head] = dv[pair:]
    lines = jnp.concatenate([skew_ref[...], jnp.zeros((LANES, LANES), jnp.float32)], axis=1)
    count = LANES // 2
    while count >= 8:
        lines = lines[count:] + pltpu.roll(lines[:count], count, 1)
        count //= 2
    line_ref[0] = lines

    @pl.when(head == pl.num_programs(0) - 1)
    def _():
        def total(rows):
            heads = all_dk.shape[0]
            d_key = jnp.concatenate([all_dk[h, rows] for h in range(heads)], axis=1)
            d_value = jnp.concatenate([all_dv[h, rows] for h in range(heads)], axis=1)
            return dot_turned(d_key, wk_ref[...]) + dot_turned(d_value, wv_ref[...])

        send_ref[...] = total(other).astype(jnp.bfloat16)
        far_ref[...] = total(mine)


def attend_back(at, query, key, key_far, value, value_far, own, near, weights, lse, bias, heads, head_dim):
    queries, keys = query.shape[0], 2 * key.shape[0]
    tokens, model = own.shape
    width = bias.shape[-1]
    blocks = keys // LANES
    column = lambda h, at: (0, h)
    half = pl.BlockSpec((keys // 2, head_dim), column)
    low = jnp.bfloat16
    wo, wk, wv = weights
    grid_spec = pltpu.PrefetchScalarGridSpec(
        num_scalar_prefetch=1,
        grid=(heads,),
        in_specs=[
            pl.BlockSpec((queries, head_dim), column), half, half, half, half,
            whole((tokens, model)), whole((tokens, model)),
            pl.BlockSpec((head_dim, model), lambda h, at: (at[2 * blocks + 1] * heads + h, 0)),
            pl.BlockSpec((model, model // 2), lambda h, at: (0, at[2 * blocks + 1])),
            pl.BlockSpec((model, model // 2), lambda h, at: (0, at[2 * blocks + 1])),
            pl.BlockSpec((1, 1, queries), lambda h, at: (h, 0, 0)),
            pl.BlockSpec((1, LANES, width), lambda h, at: (h, 0, 0)),
        ],
        out_specs=[
            pl.BlockSpec((queries, head_dim), column),
            pl.BlockSpec((keys, head_dim), column),
            pl.BlockSpec((keys, head_dim), column),
            pl.BlockSpec((1, 8, width + LANES), lambda h, at: (h, 0, 0)),
            whole((tokens, model)),
            whole((tokens, model)),
        ],
        scratch_shapes=[
            pltpu.VMEM((queries, head_dim), low),
            pltpu.VMEM((heads, keys // 2, head_dim), low),
            pltpu.VMEM((heads, keys // 2, head_dim), low),
            pltpu.VMEM((keys, head_dim), low),
            pltpu.VMEM((keys, head_dim), low),
            pltpu.VMEM((head_dim, keys), low),
            pltpu.VMEM((keys, queries), jnp.float32),
            pltpu.VMEM((keys, queries), jnp.float32),
            pltpu.VMEM((keys, queries), low),
            pltpu.VMEM((keys, queries), low),
            pltpu.VMEM((LANES, width), jnp.float32),
        ],
    )
    return pl.pallas_call(
        functools.partial(attend_back_kernel, head_dim ** (-0.5)),
        out_shape=[
            pltpu.HBM((queries, heads * head_dim), low),
            pltpu.HBM((keys, heads * head_dim), low),
            pltpu.HBM((keys, heads * head_dim), low),
            pltpu.HBM((heads, 8, width + LANES), jnp.float32),
            pltpu.HBM((tokens, model), low),
            pltpu.HBM((tokens, model), jnp.float32),
        ],
        grid_spec=grid_spec,
        compiler_params=pltpu.CompilerParams(vmem_limit_bytes=48 * MIB),
        cost_estimate=cost(
            10 * heads * queries * keys * head_dim,
            heads * queries * keys,
            4 * heads * LANES * width + 8 * heads * head_dim * (queries + keys),
        ),
        name="attend_back",
    )(
        at, *[in_hbm(x) for x in (query, key, key_far, value, value_far, own, near, wo, wk, wv, lse, bias)]
    )


def again_kernel(count, at, *refs):
    pieces, cuts = refs[:4], refs[4 : 4 + count]
    act_ref, slope_ref, rows = refs[5 + count :]
    tokens = pieces[0].shape[0]

    @pl.when(pl.program_id(0) == 0)
    def _():
        for k in range(4):
            rows[k * tokens : (k + 1) * tokens] = pieces[k][...]

    for k in range(count):
        block = cuts[k].shape[1]
        mid, slope = silu_pair(dot_turned(cuts[k][...].T, rows[...]))
        act_ref[k * block : (k + 1) * block] = mid.astype(jnp.bfloat16)
        slope_ref[k * block : (k + 1) * block] = slope.astype(jnp.bfloat16)


def column_cuts(weight, groups, parts, width):
    block = weight.shape[1] // groups // parts
    if block == width:
        return weight, lambda g, at: (0, g * parts + at[0])
    return None, lambda g, at: (0, g)


def again(place, pieces, weight, groups, dep):
    parts = len(pieces)
    tokens, model = pieces[0].shape
    inner = weight.shape[1] // parts
    width = LANES
    source, where = column_cuts(weight, groups, parts, width)
    if source is None:
        source = take_columns(weight, groups, place[0], parts)
    count = 2
    cut = inner // width // count
    return pl.pallas_call(
        functools.partial(again_kernel, count),
        grid_spec=pltpu.PrefetchScalarGridSpec(
            num_scalar_prefetch=1,
            grid=(cut,),
            in_specs=[whole((tokens, model))] * parts
            + [
                pl.BlockSpec((model, width), lambda i, at, k=k: where(i * count + k, at))
                for k in range(count)
            ]
            + [pl.BlockSpec(memory_space=pl.ANY)],
            out_specs=[pl.BlockSpec((count * width, parts * tokens), lambda i, at: (i, 0))] * 2,
            scratch_shapes=[pltpu.VMEM((parts * tokens, model), jnp.bfloat16)],
        ),
        out_shape=[pltpu.HBM((inner, parts * tokens), jnp.bfloat16)] * 2,
        compiler_params=pltpu.CompilerParams(vmem_limit_bytes=40 * MIB),
        cost_estimate=cost(
            2 * parts * tokens * model * inner,
            2 * parts * tokens * inner,
            2 * parts * tokens * (2 * inner + model) + 2 * model * inner,
        ),
        name="again",
    )(place[:1], *[in_hbm(p) for p in pieces], *([in_hbm(source)] * count), in_hbm(dep))


def store_halves(held, mine, lead, size, send_ref, keep_ref):
    for index, target in ((1 - mine, send_ref), (mine, keep_ref)):
        for k, part in enumerate(take_half(held, index, lead, size)):
            target[k * size : (k + 1) * size] = part


def grad_out_kernel(share, at, act_ref, *refs):
    pieces, dep, send_ref, keep_ref, rows, held = refs[:4], *refs[4:]
    tokens = pieces[0].shape[0]

    @pl.when(pl.program_id(0) == 0)
    def _():
        for k in range(4):
            rows[k * tokens : (k + 1) * tokens] = pieces[k][...]

    held[...] = dot(act_ref[...], rows[...]).astype(jnp.bfloat16)
    store_halves(held, at[1] & 1, held.shape[0] // share // 2, share, send_ref, keep_ref)


def grad_out_of(place, act, pieces, share, dep):
    inner, frames = act.shape
    tokens, model = pieces[0].shape
    step = 512
    return pl.pallas_call(
        functools.partial(grad_out_kernel, share),
        grid_spec=pltpu.PrefetchScalarGridSpec(
            num_scalar_prefetch=1,
            grid=(inner // step,),
            in_specs=[pl.BlockSpec((step, frames), lambda i, at: (i, 0))]
            + [whole((tokens, model))] * len(pieces)
            + [pl.BlockSpec(memory_space=pl.ANY)],
            out_specs=[pl.BlockSpec((step // 2, model), lambda i, at: (i, 0))] * 2,
            scratch_shapes=[
                pltpu.VMEM((frames, model), jnp.bfloat16), pltpu.VMEM((step, model), jnp.bfloat16)
            ],
        ),
        out_shape=[pltpu.HBM((inner // 2, model), jnp.bfloat16)] * 2,
        compiler_params=pltpu.CompilerParams(vmem_limit_bytes=40 * MIB),
        cost_estimate=cost(
            2 * frames * model * inner, 0, 2 * frames * (inner + model) + 2 * model * inner
        ),
        name="grad_out",
    )(place, in_hbm(act), *[in_hbm(p) for p in pieces], in_hbm(dep))


def grad_in_kernel(count, share, at, slope_ref, *refs):
    acts, branches, cuts = refs[:4], refs[4:8], refs[8 : 8 + count]
    dep, send_ref, keep_ref, act_rows, branch_rows, held = refs[8 + count :]
    tokens = acts[0].shape[0]

    @pl.when(pl.program_id(0) == 0)
    def _():
        for k in range(4):
            act_rows[k * tokens : (k + 1) * tokens] = acts[k][...]
            branch_rows[k * tokens : (k + 1) * tokens] = branches[k][...]

    cut = jnp.concatenate([c[...] for c in cuts], axis=0)
    d_hidden = (dot_turned(cut, branch_rows[...]) * slope_ref[...].astype(jnp.float32)).astype(jnp.bfloat16)
    held[...] = dot(d_hidden, act_rows[...]).astype(jnp.bfloat16).T
    store_halves(held, at[1] & 1, held.shape[0] // share // 2, share, send_ref, keep_ref)


def grad_in_of(place, slope, acts, branches, weight, groups, share, dep):
    inner, frames = slope.shape
    tokens, model = acts[0].shape
    parts = len(acts)
    width = LANES
    count = 4
    if weight.shape[0] // groups // parts == width:
        source, where = weight, lambda g, at: (g * parts + at[0], 0)
    else:
        source, where = take_rows(weight, groups, place[0], parts), lambda g, at: (g, 0)
    return pl.pallas_call(
        functools.partial(grad_in_kernel, count, share),
        grid_spec=pltpu.PrefetchScalarGridSpec(
            num_scalar_prefetch=1,
            grid=(inner // width // count,),
            in_specs=[pl.BlockSpec((count * width, frames), lambda i, at: (i, 0))]
            + [whole((tokens, model))] * (2 * parts)
            + [
                pl.BlockSpec((width, model), lambda i, at, k=k: where(i * count + k, at))
                for k in range(count)
            ]
            + [pl.BlockSpec(memory_space=pl.ANY)],
            out_specs=[pl.BlockSpec((model // 2, count * width), lambda i, at: (0, i))] * 2,
            scratch_shapes=[pltpu.VMEM((frames, model), jnp.bfloat16)] * 2
            + [pltpu.VMEM((model, count * width), jnp.bfloat16)],
        ),
        out_shape=[pltpu.HBM((model // 2, inner), jnp.bfloat16)] * 2,
        compiler_params=pltpu.CompilerParams(vmem_limit_bytes=48 * MIB),
        cost_estimate=cost(
            4 * frames * model * inner, 0, 2 * frames * (inner + 2 * model) + 4 * model * inner
        ),
        name="grad_in",
    )(place, in_hbm(slope), *[in_hbm(p) for p in (*acts, *branches)], *([in_hbm(source)] * count), in_hbm(dep))


def both_kernel(count, share, in_share, at, *refs):
    acts, branches = refs[:4], refs[4:8]
    ins, outs = refs[8 : 8 + count], refs[8 + count : 8 + 2 * count]
    dep, out_send, out_keep, in_send, in_keep, act_rows, branch_rows, out_held, in_held = refs[8 + 2 * count :]
    tokens = acts[0].shape[0]

    @pl.when(pl.program_id(0) == 0)
    def _():
        for k in range(4):
            act_rows[k * tokens : (k + 1) * tokens] = acts[k][...]
            branch_rows[k * tokens : (k + 1) * tokens] = branches[k][...]

    w_in = jnp.concatenate([c[...] for c in ins], axis=1).T
    w_out = jnp.concatenate([c[...] for c in outs], axis=0)
    mid, slope = silu_pair(dot_turned(w_in, act_rows[...]))
    d_hidden = (dot_turned(w_out, branch_rows[...]) * slope).astype(jnp.bfloat16)
    out_held[...] = dot(mid.astype(jnp.bfloat16), branch_rows[...]).astype(jnp.bfloat16)
    in_held[...] = dot(d_hidden, act_rows[...]).astype(jnp.bfloat16).T
    store_halves(out_held, at[1] & 1, out_held.shape[0] // share // 2, share, out_send, out_keep)
    store_halves(in_held, at[1] & 1, in_held.shape[0] // in_share // 2, in_share, in_send, in_keep)


def grads_of_both(place, acts, branches, w_in, w_out, groups, dep):
    tokens, model = acts[0].shape
    parts = len(acts)
    frames = parts * tokens
    inner = w_in.shape[1] // parts
    width, count = LANES, 4
    if w_in.shape[1] // groups // parts == width:
        source_in, at_in = w_in, lambda g, at: (0, g * parts + at[0])
        source_out, at_out = w_out, lambda g, at: (g * parts + at[0], 0)
    else:
        source_in, at_in = take_columns(w_in, groups, place[0], parts), lambda g, at: (0, g)
        source_out, at_out = take_rows(w_out, groups, place[0], parts), lambda g, at: (g, 0)
    step = count * width
    return pl.pallas_call(
        functools.partial(both_kernel, count, inner // groups, model // groups),
        grid_spec=pltpu.PrefetchScalarGridSpec(
            num_scalar_prefetch=1,
            grid=(inner // step,),
            in_specs=[whole((tokens, model))] * (2 * parts)
            + [pl.BlockSpec((model, width), lambda i, at, k=k: at_in(i * count + k, at)) for k in range(count)]
            + [pl.BlockSpec((width, model), lambda i, at, k=k: at_out(i * count + k, at)) for k in range(count)]
            + [pl.BlockSpec(memory_space=pl.ANY)],
            out_specs=[pl.BlockSpec((step // 2, model), lambda i, at: (i, 0))] * 2
            + [pl.BlockSpec((model // 2, step), lambda i, at: (0, i))] * 2,
            scratch_shapes=[pltpu.VMEM((frames, model), jnp.bfloat16)] * 2
            + [pltpu.VMEM((step, model), jnp.bfloat16), pltpu.VMEM((model, step), jnp.bfloat16)],
        ),
        out_shape=[pltpu.HBM((inner // 2, model), jnp.bfloat16)] * 2
        + [pltpu.HBM((model // 2, inner), jnp.bfloat16)] * 2,
        compiler_params=pltpu.CompilerParams(vmem_limit_bytes=56 * MIB),
        cost_estimate=cost(8 * frames * model * inner, 2 * frames * inner, 4 * frames * model + 8 * model * inner),
        name="grads_of_both",
    )(place, *[in_hbm(p) for p in (*acts, *branches)], *([in_hbm(source_in)] * count), *([in_hbm(source_out)] * count), in_hbm(dep))


def shards(
    features,
    lengths,
    buckets,
    gain_first,
    first_in,
    first_out,
    gain_attend,
    query_weight,
    key_weight,
    value_weight,
    output_weight,
    bias_table,
    gain_conv,
    point_in,
    depth_weight,
    batch_scale,
    batch_shift,
    point_out,
    gain_second,
    second_in,
    second_out,
    gain_final,
    cotangent,
):
    row_count, width, model = features.shape
    tokens = row_count * width
    heads, bucket_count = bias_table.shape
    head_dim = model // heads
    parts = lax.axis_size("tm")
    groups = lax.axis_size("rows")
    frames = width * parts
    half = depth_weight.shape[0] // 2
    taps = depth_weight.shape[0]
    place = lax.axis_index("tm")
    row_place = lax.axis_index("rows")
    side = place % 2
    far = place // 2
    offset = place * width
    near_heads = heads // 2
    pair = 2 * width
    places = jnp.stack([place, row_place]).astype(jnp.int32)
    info = jnp.stack([side, far, offset, lengths[0], row_place]).astype(jnp.int32)

    flat_features = features.reshape(tokens, model)
    after_first, act_first, slope_first, act_attend = first_forward(
        flat_features, gain_first, gain_attend, first_in, first_out
    )
    act_near, act_far = swap(act_attend, "tm", 1), swap(act_attend, "tm", 2)

    near_table = lax.dynamic_slice_in_dim(bias_table, side * near_heads, near_heads, 0)
    span = pair + frames
    turned = jnp.pad(buckets[::-1], (0, 1), constant_values=-1)
    window = lax.dynamic_slice_in_dim(turned, far * pair, span, 0)
    one_hot = (window[:, None] == jnp.arange(bucket_count)[None, :]).astype(jnp.float32)
    bias_lines = lax.dot_general(
        near_table, one_hot, (((1,), (1,)), ((), ())), precision=lax.Precision.HIGHEST
    )
    bias = skewed(bias_lines[:, None, :])
    key_blocks = frames // LANES
    block = jnp.arange(key_blocks)
    block = (block + far * (key_blocks // 2)) % key_blocks
    at = jnp.concatenate([frames - LANES - LANES * block, LANES * block, lengths[:1], side[None]]).astype(jnp.int32)

    query, key, value = project(info, act_attend, act_near, (query_weight, key_weight, value_weight))
    act_far, act_first, key, bias = tie(act_far, act_first, key, bias)
    act_cross = swap(act_far, "tm", 1)
    act_first_near, act_first_far = swap(act_first, "tm", 1), swap(act_first, "tm", 2)
    key_far, value_far = project(info, act_far, act_cross, (key_weight, value_weight))
    own_mixed, other_mixed, lse = attend(
        at, query, key, key_far, value, value_far, bias, near_heads, head_dim
    )
    other_mixed = swap(other_mixed, "tm", 1)

    attended, after_attend, act_conv, joined_value, gate, gated = mix(
        info, own_mixed, other_mixed, output_weight, after_first, gain_conv, point_in, act_first_far
    )
    act_first_all = [act_first, act_first_near, act_first_far, swap(act_first_far, "tm", 1)]
    up = [(i, i + 1) for i in range(parts - 1)]
    down = [(j, i) for i, j in up]
    gated_before = lax.ppermute(gated[width - half :].astype(jnp.bfloat16), "tm", up)
    gated_after = lax.ppermute(gated[:half].astype(jnp.bfloat16), "tm", down)
    filtered, moments = filter_frames(info, gated, gated_before, gated_after, depth_weight)
    local_count = jnp.clip(lengths[0] - offset, 0, width).astype(jnp.float32)
    count, batch_mean, spread = mesh_moments(local_count, moments[0], moments[1])
    count = count[0]
    rstd_batch = lax.rsqrt(spread / count + EPS)
    stats = jnp.stack([batch_mean, rstd_batch, batch_scale, batch_shift])
    (
        act_batch, act_second, output, branch_second, grad, d_branch_send, d_branch, d_normal, second_sums,
    ) = second_both(
        info, filtered, stats, after_attend, cotangent.reshape(tokens, model),
        gain_second, gain_final, point_out, second_in, second_out, (act_first_all[3],),
    )
    output = output.reshape(row_count, width, model)

    edge_before = lax.ppermute(
        jnp.concatenate([d_normal[width - half :], filtered[width - half :]], axis=0), "tm", up
    )
    edge_after = lax.ppermute(jnp.concatenate([d_normal[:half], filtered[:half]], axis=0), "tm", down)
    first_step = second_sums[2:] + swap(second_sums[2:], *hops()[0])
    first_step, act_second = tie(first_step, act_second)
    act_second_far = swap(act_second, "tm", 2)
    act_second_far, branch_second = tie(act_second_far, branch_second)
    branch_second_far = swap(branch_second, "tm", 2)
    batch_grads = mesh_sum(first_step, hops()[1:])
    joined_send, d_joined, grad, d_attend, conv_small = conv_back(
        info, d_normal, filtered, edge_before, edge_after, stats, batch_grads / count, depth_weight,
        gated, gated_before, gated_after, joined_value, gate, point_in, after_attend, gain_conv, grad,
    )
    d_attend_near = swap(d_attend, "tm", 1)

    held = near_heads * head_dim
    share = model // groups
    conv_send, conv_keep = cross_grads(
        info,
        [
            ((act_conv, swap(act_conv, "tm", 1)), (d_joined, swap(joined_send, "tm", 1)), model),
            ((act_batch, swap(act_batch, "tm", 1)), (d_branch, swap(d_branch_send, "tm", 1)), held),
            ((attended, swap(attended, "tm", 1)), (d_attend, d_attend_near), held),
        ],
    )

    act_second_all = [
        act_second, swap(act_second, "tm", 1), act_second_far, swap(act_second_far, "tm", 1)
    ]
    branch_second_far, conv_send = tie(branch_second_far, conv_send)
    conv_got = swap(conv_send, "tm", 2)
    branch_second_all = [
        branch_second, swap(branch_second, "tm", 1), branch_second_far, swap(branch_second_far, "tm", 1)
    ]
    out_send, out_keep, in_send, in_keep = grads_of_both(
        places, act_second_all, branch_second_all, second_in, second_out, groups, conv_keep
    )
    d_attend_near, in_keep = tie(d_attend_near, in_keep)
    second_sums_of = [RowSum(out_send, out_keep, share), RowSum(in_send, in_keep, share)]

    d_query, d_key, d_value, skew_lines, far_send, far_keep = attend_back(
        at, query, key, key_far, value, value_far, d_attend, d_attend_near,
        (output_weight, key_weight, value_weight), lse, bias, near_heads, head_dim,
    )
    far_mine = add(info, (far_keep, swap(far_send, "tm", 1)), jnp.bfloat16, second_sums_of[0].terms[1])
    far_back = swap(far_mine, "tm", 2)
    conv_sum = opened(info, conv_keep, conv_got, share, far_mine)
    kept = conv_sum.terms[0]
    pair_send, pair_keep = input_back(
        info, (d_query, d_key, d_value), (0, 0, 0), (query_weight, key_weight, value_weight), width, (kept,)
    )
    attend_sum = RowSum(*cross_grads(
        info,
        [
            ((act_attend, act_near), (d_query,), held),
            ((act_attend, act_near, act_far, act_cross), (d_key,), held),
            ((act_attend, act_near, act_far, act_cross), (d_value,), held),
        ],
        split=False,
        deps=(pair_keep, second_sums_of[1].terms[1]),
    ), share)
    mid_first, slope_first_part = again(places, act_first_all, first_in, groups, attend_sum.terms[0])
    grad, branch_first, grad_gain_attend = branch_of(
        info, pair_keep, swap(pair_send, "tm", 1), far_back, after_first, gain_attend, grad, (mid_first,)
    )
    branch_far = swap(branch_first, "tm", 2)
    grad_features, grad_gain_first = first_backward(
        info, grad, flat_features, gain_first, slope_first, first_in, first_out, ()
    )
    grad_features = grad_features.reshape(row_count, width, model)
    early_sums = [*second_sums_of, conv_sum]
    kept = merge(info, early_sums, grad_gain_first)
    branch_far, conv_sum.terms[0] = tie(branch_far, kept)
    branch_first_all = [branch_first, swap(branch_first, "tm", 1), branch_far, swap(branch_far, "tm", 1)]
    first_out_sum = RowSum(
        *grad_out_of(places, mid_first, branch_first_all, share, attend_sum.terms[1]), share
    )
    table_lines = sum(jnp.pad(skew_lines[:, r], ((0, 0), (7 - r, 0)))[:, :span] for r in range(8))
    near_grad = lax.dot_general(
        table_lines, one_hot, (((1,), (0,)), ((), ())), precision=lax.Precision.HIGHEST
    )
    grad_table = lax.dynamic_update_slice_in_dim(
        jnp.zeros((heads, bucket_count), jnp.float32), near_grad, side * near_heads, 0
    )
    small = jnp.concatenate(
        [
            grad_gain_first,
            grad_gain_attend,
            second_sums[:2],
            conv_small,
            jnp.pad(grad_table.reshape(1, -1), ((0, 0), (0, model - heads * bucket_count))),
        ],
        axis=0,
    )
    first_in_sum = RowSum(*grad_in_of(
        places, slope_first_part, act_first_all, branch_first_all, first_out, groups, share,
        first_out_sum.terms[0],
    ), share)
    steps = hops()
    kept = merge(info, early_sums, first_in_sum.terms[0])
    small = add(info, (small, swap(small, *steps[0])), jnp.float32, kept)
    late_sums = [attend_sum, first_out_sum]
    kept = merge(info, late_sums, small)
    small = add(info, (small, swap(small, *steps[1])), jnp.float32, kept)
    early = joined(info, early_sums, small)
    early_pieces = spread_tm(early)
    kept = merge(info, [first_in_sum], early)
    for step in steps[2:-2]:
        small = add(info, (small, swap(small, *step)), jnp.float32, kept)
    kept = merge(info, late_sums, small)
    small = add(info, (small, swap(small, *steps[-2])), jnp.float32, kept)
    kept = merge(info, [first_in_sum], small)
    attend_piece = joined(info, [attend_sum], kept)
    attend_got = swap(attend_piece, "tm", 2)
    first_out_piece = joined(info, [first_out_sum], attend_piece)
    first_out_pieces = spread_tm(first_out_piece)
    small = add(info, (small, swap(small, *steps[-1])), jnp.float32, first_out_piece)
    attend_piece = join(info, [[attend_piece, attend_got]], small)
    attend_pieces = [attend_piece, swap(attend_piece, "tm", 1)]
    gains = lax.dynamic_slice_in_dim(small[:5], row_place * share, share, 1)
    grad_depth = small[5 : 5 + taps]
    grad_table = small[5 + taps, : heads * bucket_count].reshape(heads, bucket_count)

    relative = jnp.arange(parts) ^ place
    crossed = (relative % 2) * 2 + relative // 2
    quarter = model // parts

    def lay_rows(pieces):
        size = pieces[0].shape[0]
        out = jnp.zeros((parts, size, model), jnp.float32)
        for k in range(parts):
            out = lax.dynamic_update_index_in_dim(out, pieces[k].astype(jnp.float32), place ^ k, 0)
        return out.reshape(parts * size, model)

    (grad_second_in,) = lay_columns([p[:, model : 2 * model] for p in early_pieces], (model,), groups, relative)
    grad_second_out = lay_rows([p[:, :model] for p in early_pieces])
    grad_point_in, grad_point_out, grad_output = lay_columns(
        [p[:, 2 * model :] for p in early_pieces], (2 * quarter, quarter, quarter), 1, crossed
    )
    grad_query, grad_key, grad_value = lay_columns(
        attend_pieces, (2 * quarter,) * 3, 1, jnp.stack([side, 1 - side])
    )
    first_in_pieces = spread_tm(
        joined(info, [first_in_sum], grad_second_in, grad_second_out, grad_point_out, grad_query)
    )
    grad_first_out = lay_rows(first_out_pieces)
    (grad_first_in,) = lay_columns(first_in_pieces, (model,), groups, relative)
    return (
        output,
        grad_features,
        gains[0],
        grad_first_in,
        grad_first_out,
        gains[1],
        grad_query,
        grad_key,
        grad_value,
        grad_output,
        grad_table,
        gains[4],
        grad_point_in,
        grad_depth,
        batch_grads[1],
        batch_grads[0],
        grad_point_out,
        gains[3],
        grad_second_in,
        grad_second_out,
        gains[2],
    )


def solution(mesh):
    rows3, rows2, rows1 = P("rows", "tm", None), P("rows", None), P("rows")
    in_specs = (rows3, rows1) + (P(),) * 20 + (rows3,)
    out_specs = (
        rows3, rows3, rows1, rows2, rows2, rows1, rows2, rows2, rows2, rows2, P(),
        rows1, rows2, P(), P(), P(), rows2, rows1, rows2, rows2, rows1,
    )
    return jax.shard_map(shards, mesh=mesh, in_specs=in_specs, out_specs=out_specs, check_vma=False)
```

```python
import functools

import jax
import jax.numpy as jnp
from jax import lax
from jax.experimental import pallas as pl
from jax.experimental.pallas import tpu as pltpu
from jax.sharding import PartitionSpec as P

EPS = 1e-05
NEGATIVE = -1e30
LANES = 128
MIB = 1024 * 1024
BLOCK = 1024
EFFORT = 0.0005


RECEIVED = []


def swap(value, axis, bit):
    count = lax.axis_size(axis)
    got = lax.ppermute(value, axis, [(i, i ^ bit) for i in range(count)])
    RECEIVED.append(got)
    return got


def is_received(value):
    return any(value is got for got in RECEIVED)


def hops():
    wide, deep = lax.axis_size("tm"), lax.axis_size("rows")
    found = [("tm", 1 << b) for b in range(wide.bit_length() - 1)][::-1]
    return found + [("rows", 1 << b) for b in range(deep.bit_length() - 1)]


def mesh_sum(value, steps):
    for axis, bit in steps:
        value = value + swap(value, axis, bit)
    return value


def mesh_moments(count, mean, spread):
    for axis, bit in hops():
        sent = jnp.concatenate([mean[None], spread[None], jnp.broadcast_to(count, (1, mean.shape[0]))])
        got = swap(sent, axis, bit)
        other_mean, other_spread, other_count = got[0], got[1], got[2]
        total = count + other_count
        safe = jnp.maximum(total, 1.0)
        gap = other_mean - mean
        spread = spread + other_spread + gap * gap * (count * other_count / safe)
        mean = (count * mean + other_count * other_mean) / safe
        count = total
    return (count, mean, spread)


def tie(*values):
    out = lax.optimization_barrier(values)
    RECEIVED.extend(b for a, b in zip(values, out, strict=True) if is_received(a))
    return out


def spread_tm(piece):
    far = swap(piece, "tm", 2)
    return [piece, swap(piece, "tm", 1), far, swap(far, "tm", 1)]


def silu_pair(hidden):
    sigma = 0.5 * jnp.tanh(0.5 * hidden) + 0.5
    act = hidden * sigma
    return (act, sigma + act * (1.0 - sigma))


def normed_of(values, gain):
    mean = jnp.mean(values, axis=-1, keepdims=True)
    centered = values - mean
    rstd = lax.rsqrt(jnp.mean(centered * centered, axis=-1, keepdims=True) + EPS)
    scaled = centered * rstd
    return (scaled * gain, scaled, rstd)


def normed_back(grad, values, gain):
    _, scaled, rstd = normed_of(values, gain)
    weighted = grad * gain
    inner = weighted - jnp.mean(weighted, axis=-1, keepdims=True)
    inner = inner - scaled * jnp.mean(weighted * scaled, axis=-1, keepdims=True)
    return (rstd * inner, jnp.sum(grad * scaled, axis=0, keepdims=True))


def dot(left, right):
    return jnp.dot(left, right, preferred_element_type=jnp.float32)


def dot_turned(left, right):
    return lax.dot_general(left, right, (((1,), (1,)), ((), ())), preferred_element_type=jnp.float32)


def scalars():
    return [pl.BlockSpec(memory_space=pltpu.SMEM)]


def in_hbm(value):
    if is_received(value):
        return value
    return pltpu.with_memory_space_constraint(value, pltpu.HBM)


def struct(*shape, kind=jnp.bfloat16):
    return jax.ShapeDtypeStruct(shape, kind)


class Arriving:
    def __init__(self, source, target, sem):
        self.copy = pltpu.make_async_copy(source, target, sem)
        self.target = target
        self.started = self.here = False

    def start(self):
        if not self.started:
            self.copy.start()
            self.started = True

    def get(self):
        self.start()
        if not self.here:
            self.copy.wait()
            self.here = True
        return self.target


class Leaving:
    def __init__(self, source, target, sem):
        self.ref = source
        self.target, self.sem = target, sem
        self.copy = None

    def send(self, source=None):
        self.copy = pltpu.make_async_copy(self.ref if source is None else source, self.target, self.sem)
        self.copy.start()


def flow_call(body, name, outs, scratch, info, operands, flops, mib=24, raw=(), late=(), deps=()):
    ins, results = len(operands), len(outs)

    def kernel(info, *refs):
        sources, targets = refs[:ins], refs[ins + len(deps) : ins + len(deps) + results]
        rest = refs[ins + len(deps) + results :]
        held, made = rest[:ins], rest[ins : ins + results]
        extra, sem_in, sem_out = rest[ins + results : -2], rest[-2], rest[-1]
        arriving = [
            (sources[k], held[k]) if k in raw else Arriving(sources[k], held[k], sem_in.at[k])
            for k in range(ins)
        ]
        for k in range(ins):
            if k not in raw and k not in late:
                arriving[k].start()
        leaving = [Leaving(made[k], targets[k], sem_out.at[k]) for k in range(results)]
        body(info, arriving, leaving, *extra)
        for item in leaving:
            if item.copy is None:
                item.send()
        for k in range(ins):
            if k not in raw:
                arriving[k].get()
        for item in leaving:
            item.copy.wait()

    moved = sum(o.size * o.dtype.itemsize for o in (*operands, *outs))
    return pl.pallas_call(
        kernel,
        in_specs=scalars() + [pl.BlockSpec(memory_space=pl.ANY)] * (ins + len(deps)),
        out_specs=[pl.BlockSpec(memory_space=pltpu.HBM)] * results,
        out_shape=[pltpu.HBM(o.shape, o.dtype) for o in outs],
        scratch_shapes=[pltpu.VMEM(o.shape, o.dtype) for o in (*operands, *outs)]
        + list(scratch)
        + [pltpu.SemaphoreType.DMA((ins,)), pltpu.SemaphoreType.DMA((results,))],
        compiler_params=pltpu.CompilerParams(vmem_limit_bytes=mib * MIB),
        cost_estimate=cost(flops, 0, moved),
        name=name,
    )(info, *[in_hbm(o) for o in (*operands, *deps)])


def cost(flops, transcendentals, moved):
    return pl.CostEstimate(
        flops=int(flops * EFFORT), transcendentals=int(transcendentals * EFFORT), bytes_accessed=int(moved * EFFORT)
    )


SIDE, FAR, OFFSET, LENGTH, ROW = range(5)


def row_bits():
    return lax.axis_size("rows").bit_length() - 1


def take_half(source, index, lead, size, ways=2):
    return [
        source[pl.ds(pl.multiple_of((k * ways + index) * size, size), size)] for k in range(lead)
    ]


def phases():
    return [(bit, 1) for bit in range(row_bits())]


def total_of(parts):
    total = parts[0].astype(jnp.float32)
    for part in parts[1:]:
        total = total + part.astype(jnp.float32)
    return total.astype(jnp.bfloat16)


def merge_kernel(counts, low, wide, share, info, ins, outs):
    ways = 1 << wide
    mine = (info[ROW] >> low) & (ways - 1)
    at = 0
    groups = []
    for count in counts:
        groups.append([item.get for item in ins[at : at + count]])
        at += count
    for g, gets in enumerate(groups):
        held = [get() for get in gets]
        lead = held[0].shape[0] // share // ways
        for offset in list(range(1, ways)) + [0]:
            out = outs[g * ways + (offset - 1) % ways]
            parts = [take_half(h, mine ^ offset, lead, share, ways) for h in held]
            for k in range(lead):
                out.ref[k * share : (k + 1) * share] = total_of([p[k] for p in parts])
            out.send()


def join_kernel(counts, info, ins, outs):
    begin = at = 0
    for count in counts:
        held = [item.get()[...] for item in ins[at : at + count]]
        at += count
        width = held[0].shape[1]
        outs[0].ref[:, begin : begin + width] = total_of(held)
        begin += width


class RowSum:
    def __init__(self, send, keep, share):
        self.share = share
        self.left = phases()
        self.exchange([send], keep)

    def exchange(self, sends, keep):
        low, _ = self.left.pop(0)
        self.terms = [keep] + [swap(x, "rows", (k + 1) << low) for k, x in enumerate(sends)]


def merge(info, sums, *deps):
    low, wide = sums[0].left[0]
    ways = 1 << wide
    outs = []
    for total in sums:
        rows, columns = total.terms[0].shape
        outs += [struct(rows // ways, columns)] * ways
    made = flow_call(
        functools.partial(merge_kernel, [len(t.terms) for t in sums], low, wide, sums[0].share), "merge",
        outs, [], info, tuple(x for t in sums for x in t.terms), 0, deps=deps,
    )
    for k, total in enumerate(sums):
        part = made[k * ways : (k + 1) * ways]
        total.exchange(part[:-1], part[-1])
    return sums[-1].terms[0]


def joined(info, sums, *deps):
    while sums[0].left:
        merge(info, sums)
    return join(info, [t.terms for t in sums], *deps)


def join(info, groups, *deps):
    columns = sum(g[0].shape[1] for g in groups)
    return flow_call(
        functools.partial(join_kernel, [len(g) for g in groups]), "join",
        [struct(groups[0][0].shape[0], columns)], [], info, tuple(x for g in groups for x in g), 0, deps=deps,
    )[0]


def opened(info, keep, got, share, *deps):
    rows, columns = keep.shape
    return RowSum(
        *flow_call(
            functools.partial(merge_kernel, [2], 0, 1, share), "merge",
            [struct(rows // 2, columns)] * 2, [], info, (keep, got), 0, deps=deps,
        ),
        share,
    )


def project_kernel(info, ins, outs, sem, rows):
    mine, other, *weights = ins
    side = info[SIDE]
    half = outs[0].ref.shape[1]
    lanes = pl.ds(pl.multiple_of(side * half, half), half)
    copies = [
        pltpu.make_async_copy(source.at[:, lanes], held.at[:, :half], sem.at[k])
        for k, (source, held) in enumerate(weights)
    ]
    for copy in copies:
        copy.start()
    tokens = mine.target.shape[0]
    rows[pl.ds(pl.multiple_of(side * tokens, tokens), tokens)] = mine.get()[...]
    rows[pl.ds(pl.multiple_of((1 - side) * tokens, tokens), tokens)] = other.get()[...]
    for copy, (_, held), out in zip(copies, weights, outs, strict=True):
        copy.wait()
        out.ref[...] = dot(rows[...], held[:, :half]).astype(jnp.bfloat16)
        out.send()


def project(info, mine, other, weights, deps=()):
    tokens, model = mine.shape
    pair = 2 * tokens
    return flow_call(
        project_kernel, "project",
        [struct(pair, model // 2)] * len(weights),
        [pltpu.SemaphoreType.DMA((len(weights),)), pltpu.VMEM((pair, model), jnp.bfloat16)],
        info, (mine, other, *weights), pair * model * model * len(weights),
        raw=tuple(range(2, 2 + len(weights))),
        deps=deps,
    )


def rows_of(length, first, count):
    frame = lax.broadcasted_iota(jnp.int32, (count, 1), 0) + first
    return ((frame >= 0) & (frame < length)).astype(jnp.float32)


def mix_kernel(
    info, own_ref, other_ref, weight, state_ref, gain_ref, value_w, gate_w, dep,
    attended_ref, after_ref, act_ref, value_ref, gate_ref, gated_ref, first_ref, last_ref,
):
    side = info[SIDE]
    tokens, half = own_ref.shape

    @pl.when(pl.program_id(0) == 0)
    def _():
        attended_ref[:, pl.ds(pl.multiple_of(side * half, half), half)] = own_ref[...]
        attended_ref[:, pl.ds(pl.multiple_of((1 - side) * half, half), half)] = other_ref[...]
        values = state_ref[...] + dot(attended_ref[...], weight[...])
        after_ref[...] = values
        act_ref[...] = normed_of(values, gain_ref[...])[0].astype(jnp.bfloat16)

    value = dot(act_ref[...], value_w[...])
    gate = 0.5 * jnp.tanh(0.5 * dot(act_ref[...], gate_w[...])) + 0.5
    value_ref[...] = value.astype(jnp.bfloat16)
    gate_ref[...] = gate.astype(jnp.bfloat16)
    gated_ref[...] = value * gate * rows_of(info[LENGTH], info[OFFSET], tokens)
    half = first_ref.shape[0]
    first_ref[...] = gated_ref[:half].astype(jnp.bfloat16)
    last_ref[...] = gated_ref[tokens - half :].astype(jnp.bfloat16)


def mix(info, own, other, weight, state, gain, point_in, half, dep):
    tokens, model = state.shape
    step = 512
    steps = model // step
    flat = (tokens, model)
    column = pl.BlockSpec((tokens, step), lambda i: (0, i))
    return pl.pallas_call(
        mix_kernel,
        grid=(steps,),
        in_specs=scalars() + [
            whole(own.shape), whole(own.shape), whole(weight.shape), whole(flat), whole((1, model)),
            pl.BlockSpec((model, step), lambda i: (0, i)),
            pl.BlockSpec((model, step), lambda i: (0, steps + i)),
            pl.BlockSpec(memory_space=pl.ANY),
        ],
        out_specs=[whole(flat)] * 3 + [column] * 3 + [pl.BlockSpec((half, step), lambda i: (0, i))] * 2,
        out_shape=[
            pltpu.HBM(flat, jnp.bfloat16), pltpu.HBM(flat, jnp.float32), pltpu.HBM(flat, jnp.bfloat16),
            pltpu.HBM(flat, jnp.bfloat16), pltpu.HBM(flat, jnp.bfloat16), pltpu.HBM(flat, jnp.float32),
            struct(half, model), struct(half, model),
        ],
        compiler_params=pltpu.CompilerParams(vmem_limit_bytes=32 * MIB),
        cost_estimate=cost(
            6 * tokens * model * model,
            tokens * model,
            6 * model * model + 20 * tokens * model,
        ),
        name="mix",
    )(info, in_hbm(own), other, weight, state, gain[None], point_in, point_in, in_hbm(dep))


def filter_kernel(info, ins, outs, wide):
    gated_ref, before_ref, after_ref, taps_ref = [item.get() for item in ins]
    filtered_ref, moments_ref = [item.ref for item in outs]
    tokens = gated_ref.shape[0]
    half = before_ref.shape[0]
    wide[8 : 8 + tokens] = gated_ref[...]
    wide[8 - half : 8] = before_ref[...].astype(jnp.float32)
    wide[8 + tokens : 8 + tokens + half] = after_ref[...].astype(jnp.float32)
    filtered = taps_ref[0:1] * wide[8 - half : 8 - half + tokens]
    for tap in range(1, taps_ref.shape[0]):
        filtered = filtered + taps_ref[tap : tap + 1] * wide[8 - half + tap : 8 - half + tap + tokens]
    filtered_ref[...] = filtered
    outs[0].send()
    valid = rows_of(info[LENGTH], info[OFFSET], tokens)
    count = jnp.clip(info[LENGTH] - info[OFFSET], 1, tokens).astype(jnp.float32)
    mean = jnp.sum(filtered * valid, axis=0, keepdims=True) / count
    gap = (filtered - mean) * valid
    moments_ref[0:1] = mean
    moments_ref[1:2] = jnp.sum(gap * gap, axis=0, keepdims=True)


def filter_frames(info, gated, before, later, depth):
    tokens, model = gated.shape
    return flow_call(
        filter_kernel, "filter_frames",
        [struct(tokens, model, kind=jnp.float32), struct(2, model, kind=jnp.float32)],
        [pltpu.VMEM((tokens + 16, model), jnp.float32)],
        info, (gated, before, later, depth), 10 * tokens * model,
    )


def weight_copies(pair_in, pair_out, sem, block):
    def at(i):
        lanes = pl.ds(pl.multiple_of(i * block, block), block)
        return (
            pltpu.make_async_copy(pair_in[0].at[:, lanes], pair_in[1].at[:, lanes], sem.at[0, i]),
            pltpu.make_async_copy(pair_out[0].at[lanes, :], pair_out[1].at[lanes, :], sem.at[1, i]),
        )

    return at


def second_kernel(info, ins, outs, sem, state, grad, total, slopes, low_ref):
    filtered, stats, state_in, cot, gain, final_gain, point, pair_in, pair_out = ins
    w_in, w_out = pair_in[1], pair_out[1]
    act_batch, act_out, output, branch_out, grad_out, conv_send, conv_keep, d_norm_out, sums, batch_sums, edge_first, edge_last = outs
    tokens = filtered.target.shape[0]
    steps = w_in.shape[1] // BLOCK
    valid = rows_of(info[LENGTH], info[OFFSET], tokens)
    copies = weight_copies(pair_in, pair_out, sem, BLOCK)
    filtered_ref, stats_ref = filtered.get(), stats.get()

    def normalized():
        scaled = (filtered_ref[...] - stats_ref[0:1]) * stats_ref[1:2]
        return (scaled, scaled * stats_ref[2:3] + stats_ref[3:4])

    act = silu_pair(normalized()[1])[0].astype(jnp.bfloat16)
    act_batch.ref[...] = act
    point_ref = point.get()
    for i in range(2):
        for copy in copies(i):
            copy.start()
    act_batch.send()
    values = state_in.get()[...] + dot(act, point_ref[...])
    state[...] = values
    act_ref = act_out.ref
    act_ref[...] = normed_of(values, gain.get()[...])[0].astype(jnp.bfloat16)
    act_out.send()
    cot.start()
    total[...] = jnp.zeros_like(total)

    def forward(i, carry):
        lanes = pl.ds(pl.multiple_of(i * BLOCK, BLOCK), BLOCK)
        for copy in copies(i):
            copy.wait()

        @pl.when(i + 2 < steps)
        def _():
            for copy in copies(i + 2):
                copy.start()

        mid, slope = silu_pair(dot(act_ref[...], w_in[:, lanes]))
        slopes[:, lanes] = slope.astype(jnp.bfloat16)
        total[...] += dot(mid.astype(jnp.bfloat16), w_out[lanes, :])
        return carry

    lax.fori_loop(0, steps, forward, 0)
    values = state[...] + 0.5 * total[...]
    final = final_gain.get()[...]
    normed, _, _ = normed_of(values, final)
    output.ref[...] = (normed * valid).astype(jnp.bfloat16)
    output.send()
    begin, sums.ref[0:1] = normed_back(cot.get()[...].astype(jnp.float32) * valid, values, final)
    grad[...] = begin
    branch_ref = branch_out.ref
    branch_ref[...] = (0.5 * begin).astype(jnp.bfloat16)
    branch_out.send()
    total[...] = jnp.zeros_like(total)

    def backward(i, carry):
        lanes = pl.ds(pl.multiple_of(i * BLOCK, BLOCK), BLOCK)
        part = dot_turned(branch_ref[...], w_out[lanes, :])
        part = (part * slopes[:, lanes].astype(jnp.float32)).astype(jnp.bfloat16)
        total[...] += dot_turned(part, w_in[:, lanes])
        return carry

    lax.fori_loop(0, steps, backward, 0)
    d_values, sums.ref[1:2] = normed_back(total[...], state[...], gain.get()[...])
    later = grad[...] + d_values
    grad_out.ref[...] = later
    grad_out.send()
    low = later.astype(jnp.bfloat16)
    low_ref[...] = low
    side = info[SIDE]
    half = low.shape[1] // 2
    conv_send.send(low_ref.at[:, pl.ds(pl.multiple_of((1 - side) * half, half), half)])
    conv_keep.send(low_ref.at[:, pl.ds(pl.multiple_of(side * half, half), half)])
    scaled, normal = normalized()
    d_norm = dot_turned(low, point.get()[...]) * silu_pair(normal)[1] * valid
    d_norm_out.ref[...] = d_norm
    d_norm_out.send()
    batch_sums.ref[0:1] = jnp.sum(d_norm, axis=0, keepdims=True)
    batch_sums.ref[1:2] = jnp.sum(d_norm * scaled, axis=0, keepdims=True)
    half = edge_first.ref.shape[0] // 2
    for edge, rows in ((edge_first, slice(0, half)), (edge_last, slice(tokens - half, tokens))):
        edge.ref[:half] = d_norm_out.ref[rows]
        edge.ref[half:] = filtered_ref[rows]


def second_both(info, filtered, stats, state, cotangent, gain, final_gain, point_out, w_in, w_out, half, deps):
    tokens, model = state.shape
    inner = w_in.shape[1]
    flat = (tokens, model)
    low, high = struct(*flat), struct(*flat, kind=jnp.float32)
    return flow_call(
        second_kernel, "second_both",
        [low, low, low, low, high, struct(tokens, model // 2), struct(tokens, model // 2), high,
         struct(2, model, kind=jnp.float32), struct(2, model, kind=jnp.float32),
         struct(2 * half, model, kind=jnp.float32), struct(2 * half, model, kind=jnp.float32)],
        [
            pltpu.SemaphoreType.DMA((2, inner // BLOCK)),
            pltpu.VMEM(flat, jnp.float32), pltpu.VMEM(flat, jnp.float32), pltpu.VMEM(flat, jnp.float32),
            pltpu.VMEM((tokens, inner), jnp.bfloat16), pltpu.VMEM(flat, jnp.bfloat16),
        ],
        info,
        (filtered, stats, state, cotangent, gain[None], final_gain[None], point_out, w_in, w_out),
        8 * tokens * model * inner + 4 * tokens * model * model,
        mib=48,
        raw=(7, 8),
        late=(3,),
        deps=deps,
    )


def conv_back_kernel(info, ins, outs, wide, gated_wide, joined_ref):
    d_norm_ref, filtered_ref, before_ref, after_ref, stats_ref, sums_ref, taps_ref = [i.get() for i in ins[:7]]
    for item in ins[10:13]:
        item.start()
    gated_ref, gated_before, gated_after = [i.get() for i in ins[7:10]]
    value, gate, point, state, gain, grad = ins[10:]
    out_ref, low_ref, small_ref = [item.ref for item in outs[2:]]
    tokens, model = d_norm_ref.shape
    half = gated_before.shape[0]

    def d_filtered(d_norm, filtered, first):
        valid = rows_of(info[LENGTH], first, d_norm.shape[0])
        scaled = (filtered - stats_ref[0:1]) * stats_ref[1:2]
        inner = d_norm - sums_ref[0:1] - scaled * sums_ref[1:2]
        return valid * (stats_ref[2:3] * stats_ref[1:2]) * inner

    offset = info[OFFSET]
    wide[8 : 8 + tokens] = d_filtered(d_norm_ref[...], filtered_ref[...], offset)
    wide[8 - half : 8] = d_filtered(before_ref[:half], before_ref[half:], offset - half)
    wide[8 + tokens : 8 + tokens + half] = d_filtered(after_ref[:half], after_ref[half:], offset + tokens)
    gated_wide[8 : 8 + tokens] = gated_ref[...]
    gated_wide[8 - half : 8] = gated_before[...].astype(jnp.float32)
    gated_wide[8 + tokens : 8 + tokens + half] = gated_after[...].astype(jnp.float32)
    d_gated = jnp.zeros((tokens, model), jnp.float32)
    for tap in range(taps_ref.shape[0]):
        begin = 8 + half - tap
        d_gated = d_gated + taps_ref[tap : tap + 1] * wide[begin : begin + tokens]
        begin = 8 - half + tap
        small_ref[1 + tap : 2 + tap] = jnp.sum(
            wide[8 : 8 + tokens] * gated_wide[begin : begin + tokens], axis=0, keepdims=True
        )
    for item in ins[13:]:
        item.start()
    d_gated = d_gated * rows_of(info[LENGTH], offset, tokens)
    gate = gate.get()[...].astype(jnp.float32)
    d_value = d_gated * gate
    joined_ref[:, :model] = d_value.astype(jnp.bfloat16)
    joined_ref[:, model:] = (d_value * value.get()[...].astype(jnp.float32) * (1.0 - gate)).astype(jnp.bfloat16)
    side = info[SIDE]
    outs[0].send(joined_ref.at[:, pl.ds(pl.multiple_of((1 - side) * model, model), model)])
    outs[1].send(joined_ref.at[:, pl.ds(pl.multiple_of(side * model, model), model)])
    d_values, small_ref[0:1] = normed_back(
        dot_turned(joined_ref[...], point.get()[...]), state.get()[...], gain.get()[...]
    )
    later = grad.get()[...] + d_values
    low_ref[...] = later.astype(jnp.bfloat16)
    outs[3].send()
    out_ref[...] = later


def conv_back(info, d_norm, filtered, before, later, stats, sums, depth, gated, gated_before, gated_after,
              value, gate, point_in, state, gain, grad, deps):
    tokens, model = d_norm.shape
    return flow_call(
        conv_back_kernel, "conv_back",
        [
            struct(tokens, model), struct(tokens, model),
            struct(tokens, model, kind=jnp.float32), struct(tokens, model),
            struct(1 + depth.shape[0], model, kind=jnp.float32),
        ],
        [pltpu.VMEM((tokens + 16, model), jnp.float32)] * 2 + [pltpu.VMEM((tokens, 2 * model), jnp.bfloat16)],
        info,
        (d_norm, filtered, before, later, stats, sums, depth, gated, gated_before, gated_after, value,
         gate, point_in, state, gain[None], grad),
        4 * tokens * model * model,
        mib=32,
        late=tuple(range(10, 16)),
        deps=deps,
    )


def add_kernel(info, ins, outs):
    total = ins[0].get()[...].astype(jnp.float32)
    for item in ins[1:]:
        total = total + item.get()[...].astype(jnp.float32)
    outs[0].ref[...] = total.astype(outs[0].ref.dtype)


def add(info, terms, kind, *deps):
    return flow_call(
        add_kernel, "add", [struct(*terms[0].shape, kind=kind)], [], info, tuple(terms), 0, deps=deps
    )[0]


def branch_kernel(info, ins, outs):
    keep, got, far, state, gain, grad = ins
    d_input = keep.get()[...] + got.get()[...].astype(jnp.float32) + far.get()[...].astype(jnp.float32)
    d_values, outs[2].ref[...] = normed_back(d_input, state.get()[...], gain.get()[...])
    later = grad.get()[...] + d_values
    outs[1].ref[...] = (0.5 * later).astype(jnp.bfloat16)
    outs[1].send()
    outs[0].ref[...] = later


def branch_of(info, keep, got, far, state, gain, grad, deps):
    tokens, model = keep.shape
    return flow_call(
        branch_kernel, "branch",
        [struct(tokens, model, kind=jnp.float32), struct(tokens, model), struct(1, model, kind=jnp.float32)],
        [], info, (keep, got, far, state, gain[None], grad), 0, deps=deps,
    )


def input_back_kernel(count, base, info, ins, outs, sem):
    grads, weights = ins[:count], ins[count:]
    send_ref, keep_ref = outs[0].ref, outs[1].ref
    tokens = send_ref.shape[0]
    side = info[SIDE]
    half = weights[0][0].shape[1] // 2
    lanes = pl.ds(pl.multiple_of(side * half, half), half)
    copies = [
        pltpu.make_async_copy(source.at[:, lanes], held.at[:, :half], sem.at[k])
        for k, (source, held) in enumerate(weights)
    ]
    for copy in copies:
        copy.start()
    grads = [grad.get() for grad in grads]
    for copy in copies:
        copy.wait()

    def total(which):
        out = None
        for first, grad, (_, held) in zip(base, grads, weights, strict=True):
            rows = pl.ds(pl.multiple_of(first + which * tokens, LANES), tokens)
            part = dot_turned(grad[rows], held[:, :half])
            out = part if out is None else out + part
        return out

    send_ref[...] = total(1 - side).astype(jnp.bfloat16)
    outs[0].send()
    keep_ref[...] = total(side)


def input_back(info, grads, base, weights, tokens, deps=()):
    model = weights[0].shape[0]
    count = len(grads)
    return flow_call(
        functools.partial(input_back_kernel, count, base), "input_back",
        [struct(tokens, model), struct(tokens, model, kind=jnp.float32)],
        [pltpu.SemaphoreType.DMA((count,))],
        info, (*grads, *weights), 2 * tokens * model * model * count,
        mib=32, raw=tuple(range(count, 2 * count)), deps=deps,
    )


def cross_kernel(layout, split, lead, chunk, info, refs, outs, left_rows, right_rows, *held):
    far, side = info[FAR], info[SIDE]
    at = 0
    begin = 0
    for pieces, width in layout:
        lefts, right = refs[at : at + pieces], refs[at + pieces : at + pieces + (2 if width < 0 else 1)]
        at += pieces + len(right)
        tokens = lefts[0].target.shape[0]
        for k, left in enumerate(lefts):
            spot = (k // 2 * 2 + (side if k % 2 == 0 else 1 - side)) * tokens
            left_rows[pl.ds(pl.multiple_of(spot, tokens), tokens)] = left.get()[...]
        size = abs(width)
        half = size // 2 if split else size
        if len(right) == 2:
            for k, piece in enumerate(right):
                spot = (side if k == 0 else 1 - side) * tokens
                held = piece.get()
                lanes = pl.ds(0, size)
                if held.shape[1] != size:
                    lanes = pl.ds(pl.multiple_of(side * size, size), size)
                right_rows[pl.ds(pl.multiple_of(spot, tokens), tokens), :size] = held[:, lanes]
            source = right_rows
        else:
            source = right[0].get()
        count = pieces * tokens
        targets = ((1 - far, outs[0].ref), (far, outs[1].ref)) if split else ((0, held[0]),)
        for which, target in targets:
            lanes = pl.ds(pl.multiple_of(which * half, half), half)
            target[:, begin : begin + half] = lax.dot_general(
                left_rows[:count], source[:count, lanes], (((0,), (0,)), ((), ())),
                preferred_element_type=jnp.float32,
            ).astype(jnp.bfloat16)
        begin += half
    if not split:
        store_halves(held[0], info[ROW] & 1, lead, chunk, outs[0].ref, outs[1].ref)


def cross_grads(info, terms, split=True, deps=()):
    operands, layout = [], []
    total = flops = 0
    for lefts, rights, width in terms:
        operands += [*lefts, *rights]
        layout.append((len(lefts), -width if len(rights) == 2 else width))
        total += width // 2 if split else width
        tokens, model = lefts[0].shape
        flops += 2 * len(lefts) * tokens * model * width
    deepest = max(len(lefts) for lefts, *_ in terms) * tokens
    widest = max(width for *_, width in terms)
    size = model >> row_bits()
    rows = model if split else model // 2
    scratch = [pltpu.VMEM((deepest, model), jnp.bfloat16), pltpu.VMEM((deepest, widest), jnp.bfloat16)]
    if not split:
        scratch.append(pltpu.VMEM((model, total), jnp.bfloat16))
    return flow_call(
        functools.partial(cross_kernel, layout, split, model // size // 2, size), "cross_grads",
        [struct(rows, total)] * 2, scratch, info, tuple(operands), flops, mib=40, deps=deps,
    )


def first_back_kernel(info, ins, outs, sem, branch, total):
    grad, x, gain, slope, pair_in, pair_out = ins
    w_in, w_out = pair_in[1], pair_out[1]
    steps = w_in.shape[1] // BLOCK
    copies = weight_copies(pair_in, pair_out, sem, BLOCK)
    for i in range(2):
        for copy in copies(i):
            copy.start()
    grad_ref = grad.get()
    branch[...] = (0.5 * grad_ref[...]).astype(jnp.bfloat16)
    total[...] = jnp.zeros_like(total)
    slope_ref = slope.get()
    x.start()

    def backward(i, carry):
        lanes = pl.ds(pl.multiple_of(i * BLOCK, BLOCK), BLOCK)
        for copy in copies(i):
            copy.wait()

        @pl.when(i + 2 < steps)
        def _():
            for copy in copies(i + 2):
                copy.start()

        part = dot_turned(branch[...], w_out[lanes, :])
        part = (part * slope_ref[:, lanes].astype(jnp.float32)).astype(jnp.bfloat16)
        total[...] += dot_turned(part, w_in[:, lanes])
        return carry

    lax.fori_loop(0, steps, backward, 0)
    d_values, outs[1].ref[...] = normed_back(total[...], x.get()[...].astype(jnp.float32), gain.get()[...])
    outs[0].ref[...] = (grad_ref[...] + d_values).astype(jnp.bfloat16)


def first_backward(info, grad, features, gain, slope, w_in, w_out, deps):
    tokens, model = features.shape
    inner = w_in.shape[1]
    return flow_call(
        first_back_kernel, "first_backward",
        [struct(tokens, model), struct(1, model, kind=jnp.float32)],
        [pltpu.SemaphoreType.DMA((2, inner // BLOCK)), pltpu.VMEM((tokens, model), jnp.bfloat16), pltpu.VMEM((tokens, model), jnp.float32)],
        info, (grad, features, gain[None], slope, w_in, w_out), 4 * tokens * model * inner,
        mib=40, raw=(4, 5), late=(1,), deps=deps,
    )


def norm_backward(grad, scaled, rstd, gain):
    weighted = grad * gain
    inner = weighted - jnp.mean(weighted, axis=-1, keepdims=True)
    inner = inner - scaled * jnp.mean(weighted * scaled, axis=-1, keepdims=True)
    return (rstd * inner, jnp.sum(grad * scaled, axis=0))


def first_kernel(x_ref, gain_ref, next_gain_ref, w_in, w_out, state_ref, act_ref, slope_ref, next_ref, total):
    step = pl.program_id(0)

    @pl.when(step == 0)
    def _():
        values = x_ref[...].astype(jnp.float32)
        act_ref[...] = normed_of(values, gain_ref[...])[0].astype(jnp.bfloat16)
        total[...] = jnp.zeros_like(total)

    mid, slope = silu_pair(dot(act_ref[...], w_in[...]))
    slope_ref[...] = slope.astype(jnp.bfloat16)
    total[...] += dot(mid.astype(jnp.bfloat16), w_out[...])

    @pl.when(step == pl.num_programs(0) - 1)
    def _():
        values = x_ref[...].astype(jnp.float32) + 0.5 * total[...]
        state_ref[...] = values
        next_ref[...] = normed_of(values, next_gain_ref[...])[0].astype(jnp.bfloat16)


def whole(shape):
    return pl.BlockSpec(shape, lambda *_: (0,) * len(shape))


def first_forward(features, gain, next_gain, w_in, w_out):
    tokens, model = features.shape
    inner = w_in.shape[1]
    return pl.pallas_call(
        first_kernel,
        grid=(inner // BLOCK,),
        in_specs=[
            whole((tokens, model)),
            whole((1, model)),
            whole((1, model)),
            pl.BlockSpec((model, BLOCK), lambda i: (0, i)),
            pl.BlockSpec((BLOCK, model), lambda i: (i, 0)),
        ],
        out_specs=[
            whole((tokens, model)),
            whole((tokens, model)),
            pl.BlockSpec((tokens, BLOCK), lambda i: (0, i)),
            whole((tokens, model)),
        ],
        out_shape=[
            pltpu.HBM((tokens, model), jnp.float32),
            pltpu.HBM((tokens, model), jnp.bfloat16),
            pltpu.HBM((tokens, inner), jnp.bfloat16),
            pltpu.HBM((tokens, model), jnp.bfloat16),
        ],
        scratch_shapes=[pltpu.VMEM((tokens, model), jnp.float32)],
        compiler_params=pltpu.CompilerParams(vmem_limit_bytes=40 * MIB),
        cost_estimate=cost(
            4 * tokens * model * inner,
            2 * tokens * inner,
            4 * model * inner + 2 * tokens * inner,
        ),
        name="first_forward",
    )(in_hbm(features), gain[None], next_gain[None], in_hbm(w_in), in_hbm(w_out))


def take_kernel(place, source, target):
    target[...] = source[...]


def take_columns(weight, groups, place, parts):
    model, total = weight.shape
    block = total // groups // parts
    if block % LANES:
        cut = weight.reshape(model, groups, parts, block)
        return lax.dynamic_index_in_dim(cut, place, 2, keepdims=False).reshape(model, -1)
    return pl.pallas_call(
        take_kernel,
        out_shape=jax.ShapeDtypeStruct((model, total // parts), weight.dtype),
        grid_spec=pltpu.PrefetchScalarGridSpec(
            num_scalar_prefetch=1,
            grid=(groups,),
            in_specs=[pl.BlockSpec((model, block), lambda g, at: (0, g * parts + at[0]))],
            out_specs=pl.BlockSpec((model, block), lambda g, at: (0, g)),
        ),
        name="take_columns",
    )(place.reshape(1), weight)


def take_rows(weight, groups, place, parts):
    total, model = weight.shape
    cut = weight.reshape(groups, parts, total // groups // parts, model)
    return lax.dynamic_index_in_dim(cut, place, 1, keepdims=False).reshape(-1, model)


def lay_kernel(parts, widths, groups, places, *refs):
    pieces, targets = refs[:parts], refs[parts:]
    for k in range(parts):
        begin = 0
        for width, target in zip(widths, targets, strict=True):
            block = width // groups
            for g in range(groups):
                at = pl.multiple_of((g * parts + places[k]) * block, LANES)
                source = pieces[k][:, begin + g * block : begin + (g + 1) * block]
                target[:, pl.ds(at, block)] = source.astype(jnp.float32)
            begin += width


def lay_columns(pieces, widths, groups, places):
    rows = pieces[0].shape[0]
    parts = len(pieces)
    if any((width // groups) % LANES for width in widths):
        outs, begin = [], 0
        stacked = jnp.zeros((parts, *pieces[0].shape), pieces[0].dtype)
        for k in range(parts):
            stacked = lax.dynamic_update_index_in_dim(stacked, pieces[k], places[k], 0)
        for width in widths:
            cut = stacked[:, :, begin : begin + width].reshape(parts, rows, groups, width // groups)
            outs.append(cut.transpose(1, 2, 0, 3).reshape(rows, parts * width).astype(jnp.float32))
            begin += width
        return outs
    return pl.pallas_call(
        functools.partial(lay_kernel, parts, widths, groups),
        out_shape=[jax.ShapeDtypeStruct((rows, parts * width), jnp.float32) for width in widths],
        grid_spec=pltpu.PrefetchScalarGridSpec(
            num_scalar_prefetch=1,
            grid=(1,),
            in_specs=[pl.BlockSpec(p.shape, lambda i, at: (0, 0)) for p in pieces],
            out_specs=[pl.BlockSpec((rows, parts * width), lambda i, at: (0, 0)) for width in widths],
        ),
        compiler_params=pltpu.CompilerParams(vmem_limit_bytes=24 * MIB),
        name="lay_columns",
    )(places, *pieces)


def skew_kernel(line, out):
    length = line.shape[-1]
    width = out.shape[-1]
    spread = jnp.broadcast_to(line[0], (LANES, length))
    rolled = pltpu.roll(spread, length - (LANES - 1), 1, stride=1, stride_axis=0)
    out[0] = rolled[:, :width]


def skewed(lines):
    heads, _, length = lines.shape
    width = length - LANES
    return pl.pallas_call(
        skew_kernel,
        out_shape=pltpu.HBM((heads, LANES, width), jnp.float32),
        grid=(heads,),
        in_specs=[pl.BlockSpec((1, 1, length), lambda h: (h, 0, 0))],
        out_specs=pl.BlockSpec((1, LANES, width), lambda h: (h, 0, 0)),
        name="bias_rows",
    )(lines)


def attend_kernel(
    scale, at, q_ref, k_pair, k_far, v_pair, v_far, bias_ref, own_ref, other_ref, lse_ref,
    k_ref, vt_ref, s_ref, p_ref, out_ref,
):
    tile = q_ref.shape[0]
    blocks = k_ref.shape[0] // LANES
    pair = k_pair.shape[0]
    length = at[blocks * 2]

    @pl.when(pl.program_id(1) == 0)
    def _():
        k_ref[:pair] = k_pair[...]
        k_ref[pair:] = k_far[...]
        vt_ref[:, :pair] = v_pair[...].T
        vt_ref[:, pair:] = v_far[...].T

    begin = pl.program_id(1) * tile
    s_ref[...] = lax.dot_general(
        k_ref[...], q_ref[...], (((1,), (1,)), ((), ())), preferred_element_type=jnp.float32
    )
    frame = lax.broadcasted_iota(jnp.int32, (LANES, tile), 0)
    top = jnp.full((1, tile), NEGATIVE, jnp.float32)
    for b in range(blocks):
        lanes = pl.ds(pl.multiple_of(at[b] + begin, LANES), tile)
        s = s_ref[b * LANES : (b + 1) * LANES] * scale + bias_ref[0, :, lanes]
        s = jnp.where(frame < length - at[blocks + b], s, NEGATIVE)
        s_ref[b * LANES : (b + 1) * LANES] = s
        top = jnp.maximum(top, jnp.max(s, axis=0, keepdims=True))
    total = jnp.zeros((1, tile), jnp.float32)
    for b in range(blocks):
        p = jnp.exp(s_ref[b * LANES : (b + 1) * LANES] - top)
        total = total + jnp.sum(p, axis=0, keepdims=True)
        p_ref[b * LANES : (b + 1) * LANES] = p.astype(jnp.bfloat16)
    mixed = jnp.dot(vt_ref[...], p_ref[...], preferred_element_type=jnp.float32) / total
    out_ref[...] = mixed.T.astype(jnp.bfloat16)
    half = tile // 2
    side = at[blocks * 2 + 1]
    own_ref[...] = out_ref[pl.ds(pl.multiple_of(side * half, half), half)]
    other_ref[...] = out_ref[pl.ds(pl.multiple_of((1 - side) * half, half), half)]
    lse_ref[0] = top + jnp.log(total)


def attend(at, query, key, key_far, value, value_far, bias, heads, head_dim):
    queries, keys = query.shape[0], 2 * key.shape[0]
    tile = queries
    width = bias.shape[-1]
    grid_spec = pltpu.PrefetchScalarGridSpec(
        num_scalar_prefetch=1,
        grid=(heads, queries // tile),
        in_specs=[
            pl.BlockSpec((tile, head_dim), lambda h, i, at: (i, h)),
            pl.BlockSpec((keys // 2, head_dim), lambda h, i, at: (0, h)),
            pl.BlockSpec((keys // 2, head_dim), lambda h, i, at: (0, h)),
            pl.BlockSpec((keys // 2, head_dim), lambda h, i, at: (0, h)),
            pl.BlockSpec((keys // 2, head_dim), lambda h, i, at: (0, h)),
            pl.BlockSpec((1, LANES, width), lambda h, i, at: (h, 0, 0)),
        ],
        out_specs=[
            pl.BlockSpec((tile // 2, head_dim), lambda h, i, at: (0, h)),
            pl.BlockSpec((tile // 2, head_dim), lambda h, i, at: (0, h)),
            pl.BlockSpec((1, 1, tile), lambda h, i, at: (h, 0, i)),
        ],
        scratch_shapes=[
            pltpu.VMEM((keys, head_dim), jnp.bfloat16),
            pltpu.VMEM((head_dim, keys), jnp.bfloat16),
            pltpu.VMEM((keys, tile), jnp.float32),
            pltpu.VMEM((keys, tile), jnp.bfloat16),
            pltpu.VMEM((tile, head_dim), jnp.bfloat16),
        ],
    )
    return pl.pallas_call(
        functools.partial(attend_kernel, head_dim ** (-0.5)),
        out_shape=[
            pltpu.HBM((queries // 2, heads * head_dim), jnp.bfloat16),
            pltpu.HBM((queries // 2, heads * head_dim), jnp.bfloat16),
            pltpu.HBM((heads, 1, queries), jnp.float32),
        ],
        grid_spec=grid_spec,
        compiler_params=pltpu.CompilerParams(vmem_limit_bytes=24 * MIB),
        cost_estimate=cost(
            4 * heads * queries * keys * head_dim,
            heads * queries * keys,
            4 * heads * LANES * width + 4 * heads * head_dim * (queries + keys),
        ),
        name="attend",
    )(at, *[in_hbm(x) for x in (query, key, key_far, value, value_far, bias)])


def attend_back_kernel(
    scale, at, q_ref, k_pair, k_far, v_pair, v_far, da_own, da_near, wo_ref, wk_ref, wv_ref, lse_ref, bias_ref,
    dq_ref, dk_ref, dv_ref, line_ref, send_ref, far_ref,
    do_ref, all_dk, all_dv, k_ref, v_ref, kt_ref, s_ref, dp_ref, p_ref, ds_ref, skew_ref,
):
    tile = q_ref.shape[0]
    blocks = k_ref.shape[0] // LANES
    length = at[blocks * 2]
    pair = k_pair.shape[0]

    side = at[blocks * 2 + 1]
    own = da_own.shape[0]
    mine = pl.ds(pl.multiple_of(side * own, own), own)
    other = pl.ds(pl.multiple_of((1 - side) * own, own), own)
    do_ref[mine] = dot_turned(da_own[...], wo_ref[...]).astype(jnp.bfloat16)
    do_ref[other] = dot_turned(da_near[...], wo_ref[...]).astype(jnp.bfloat16)
    k_ref[:pair] = k_pair[...]
    k_ref[pair:] = k_far[...]
    v_ref[:pair] = v_pair[...]
    v_ref[pair:] = v_far[...]
    kt_ref[...] = k_ref[...].T
    skew_ref[...] = jnp.zeros_like(skew_ref)
    s_ref[...] = lax.dot_general(
        k_ref[...], q_ref[...], (((1,), (1,)), ((), ())), preferred_element_type=jnp.float32
    )
    dp_ref[...] = lax.dot_general(
        v_ref[...], do_ref[...], (((1,), (1,)), ((), ())), preferred_element_type=jnp.float32
    )
    frame = lax.broadcasted_iota(jnp.int32, (LANES, tile), 0)
    lse = lse_ref[0]
    delta = jnp.zeros((1, tile), jnp.float32)
    for b in range(blocks):
        rows = slice(b * LANES, (b + 1) * LANES)
        lanes = pl.ds(pl.multiple_of(at[b], LANES), tile)
        s = s_ref[rows] * scale + bias_ref[0, :, lanes]
        s = jnp.where(frame < length - at[blocks + b], s, NEGATIVE)
        p = jnp.exp(s - lse)
        s_ref[rows] = p
        p_ref[rows] = p.astype(jnp.bfloat16)
        delta = delta + jnp.sum(p * dp_ref[rows], axis=0, keepdims=True)
    for b in range(blocks):
        rows = slice(b * LANES, (b + 1) * LANES)
        lanes = pl.ds(pl.multiple_of(at[b], LANES), tile)
        ds = (s_ref[rows] * (dp_ref[rows] - delta)).astype(jnp.bfloat16)
        ds_ref[rows] = ds
        skew_ref[:, lanes] += ds.astype(jnp.float32)
    dv = jnp.dot(p_ref[...], do_ref[...], preferred_element_type=jnp.float32).astype(jnp.bfloat16)
    dk = jnp.dot(ds_ref[...], q_ref[...], preferred_element_type=jnp.float32) * scale
    dk = dk.astype(jnp.bfloat16)
    dq = jnp.dot(kt_ref[...], ds_ref[...], preferred_element_type=jnp.float32) * scale
    dq_ref[...] = dq.T.astype(jnp.bfloat16)
    dk_ref[...] = dk
    dv_ref[...] = dv
    head = pl.program_id(0)
    all_dk[head] = dk[pair:]
    all_dv[head] = dv[pair:]
    lines = jnp.concatenate([skew_ref[...], jnp.zeros((LANES, LANES), jnp.float32)], axis=1)
    count = LANES // 2
    while count >= 8:
        lines = lines[count:] + pltpu.roll(lines[:count], count, 1)
        count //= 2
    line_ref[0] = lines

    @pl.when(head == pl.num_programs(0) - 1)
    def _():
        def total(rows):
            heads = all_dk.shape[0]
            d_key = jnp.concatenate([all_dk[h, rows] for h in range(heads)], axis=1)
            d_value = jnp.concatenate([all_dv[h, rows] for h in range(heads)], axis=1)
            return dot_turned(d_key, wk_ref[...]) + dot_turned(d_value, wv_ref[...])

        send_ref[...] = total(other).astype(jnp.bfloat16)
        far_ref[...] = total(mine)


def attend_back(at, query, key, key_far, value, value_far, own, near, weights, lse, bias, heads, head_dim):
    queries, keys = query.shape[0], 2 * key.shape[0]
    tokens, model = own.shape
    width = bias.shape[-1]
    blocks = keys // LANES
    column = lambda h, at: (0, h)
    half = pl.BlockSpec((keys // 2, head_dim), column)
    low = jnp.bfloat16
    wo, wk, wv = weights
    grid_spec = pltpu.PrefetchScalarGridSpec(
        num_scalar_prefetch=1,
        grid=(heads,),
        in_specs=[
            pl.BlockSpec((queries, head_dim), column), half, half, half, half,
            whole((tokens, model)), whole((tokens, model)),
            pl.BlockSpec((head_dim, model), lambda h, at: (at[2 * blocks + 1] * heads + h, 0)),
            pl.BlockSpec((model, model // 2), lambda h, at: (0, at[2 * blocks + 1])),
            pl.BlockSpec((model, model // 2), lambda h, at: (0, at[2 * blocks + 1])),
            pl.BlockSpec((1, 1, queries), lambda h, at: (h, 0, 0)),
            pl.BlockSpec((1, LANES, width), lambda h, at: (h, 0, 0)),
        ],
        out_specs=[
            pl.BlockSpec((queries, head_dim), column),
            pl.BlockSpec((keys, head_dim), column),
            pl.BlockSpec((keys, head_dim), column),
            pl.BlockSpec((1, 8, width + LANES), lambda h, at: (h, 0, 0)),
            whole((tokens, model)),
            whole((tokens, model)),
        ],
        scratch_shapes=[
            pltpu.VMEM((queries, head_dim), low),
            pltpu.VMEM((heads, keys // 2, head_dim), low),
            pltpu.VMEM((heads, keys // 2, head_dim), low),
            pltpu.VMEM((keys, head_dim), low),
            pltpu.VMEM((keys, head_dim), low),
            pltpu.VMEM((head_dim, keys), low),
            pltpu.VMEM((keys, queries), jnp.float32),
            pltpu.VMEM((keys, queries), jnp.float32),
            pltpu.VMEM((keys, queries), low),
            pltpu.VMEM((keys, queries), low),
            pltpu.VMEM((LANES, width), jnp.float32),
        ],
    )
    return pl.pallas_call(
        functools.partial(attend_back_kernel, head_dim ** (-0.5)),
        out_shape=[
            pltpu.HBM((queries, heads * head_dim), low),
            pltpu.HBM((keys, heads * head_dim), low),
            pltpu.HBM((keys, heads * head_dim), low),
            pltpu.HBM((heads, 8, width + LANES), jnp.float32),
            pltpu.HBM((tokens, model), low),
            pltpu.HBM((tokens, model), jnp.float32),
        ],
        grid_spec=grid_spec,
        compiler_params=pltpu.CompilerParams(vmem_limit_bytes=48 * MIB),
        cost_estimate=cost(
            10 * heads * queries * keys * head_dim,
            heads * queries * keys,
            4 * heads * LANES * width + 8 * heads * head_dim * (queries + keys),
        ),
        name="attend_back",
    )(
        at, *[in_hbm(x) for x in (query, key, key_far, value, value_far, own, near, wo, wk, wv, lse, bias)]
    )


def again_kernel(count, at, *refs):
    pieces, cuts = refs[:4], refs[4 : 4 + count]
    act_ref, slope_ref, rows = refs[5 + count :]
    tokens = pieces[0].shape[0]

    @pl.when(pl.program_id(0) == 0)
    def _():
        for k in range(4):
            rows[k * tokens : (k + 1) * tokens] = pieces[k][...]

    for k in range(count):
        block = cuts[k].shape[1]
        mid, slope = silu_pair(dot_turned(cuts[k][...].T, rows[...]))
        act_ref[k * block : (k + 1) * block] = mid.astype(jnp.bfloat16)
        slope_ref[k * block : (k + 1) * block] = slope.astype(jnp.bfloat16)


def column_cuts(weight, groups, parts, width):
    block = weight.shape[1] // groups // parts
    if block == width:
        return weight, lambda g, at: (0, g * parts + at[0])
    return None, lambda g, at: (0, g)


def again(place, pieces, weight, groups, dep):
    parts = len(pieces)
    tokens, model = pieces[0].shape
    inner = weight.shape[1] // parts
    width = LANES
    source, where = column_cuts(weight, groups, parts, width)
    if source is None:
        source = take_columns(weight, groups, place[0], parts)
    count = 2
    cut = inner // width // count
    return pl.pallas_call(
        functools.partial(again_kernel, count),
        grid_spec=pltpu.PrefetchScalarGridSpec(
            num_scalar_prefetch=1,
            grid=(cut,),
            in_specs=[whole((tokens, model))] * parts
            + [
                pl.BlockSpec((model, width), lambda i, at, k=k: where(i * count + k, at))
                for k in range(count)
            ]
            + [pl.BlockSpec(memory_space=pl.ANY)],
            out_specs=[pl.BlockSpec((count * width, parts * tokens), lambda i, at: (i, 0))] * 2,
            scratch_shapes=[pltpu.VMEM((parts * tokens, model), jnp.bfloat16)],
        ),
        out_shape=[pltpu.HBM((inner, parts * tokens), jnp.bfloat16)] * 2,
        compiler_params=pltpu.CompilerParams(vmem_limit_bytes=40 * MIB),
        cost_estimate=cost(
            2 * parts * tokens * model * inner,
            2 * parts * tokens * inner,
            2 * parts * tokens * (2 * inner + model) + 2 * model * inner,
        ),
        name="again",
    )(place[:1], *[in_hbm(p) for p in pieces], *([in_hbm(source)] * count), in_hbm(dep))


def store_halves(held, mine, lead, size, send_ref, keep_ref):
    for index, target in ((1 - mine, send_ref), (mine, keep_ref)):
        for k, part in enumerate(take_half(held, index, lead, size)):
            target[k * size : (k + 1) * size] = part


def grad_out_kernel(share, at, act_ref, *refs):
    pieces, dep, send_ref, keep_ref, rows, held = refs[:4], *refs[4:]
    tokens = pieces[0].shape[0]

    @pl.when(pl.program_id(0) == 0)
    def _():
        for k in range(4):
            rows[k * tokens : (k + 1) * tokens] = pieces[k][...]

    held[...] = dot(act_ref[...], rows[...]).astype(jnp.bfloat16)
    store_halves(held, at[1] & 1, held.shape[0] // share // 2, share, send_ref, keep_ref)


def grad_out_of(place, act, pieces, share, dep):
    inner, frames = act.shape
    tokens, model = pieces[0].shape
    step = 512
    return pl.pallas_call(
        functools.partial(grad_out_kernel, share),
        grid_spec=pltpu.PrefetchScalarGridSpec(
            num_scalar_prefetch=1,
            grid=(inner // step,),
            in_specs=[pl.BlockSpec((step, frames), lambda i, at: (i, 0))]
            + [whole((tokens, model))] * len(pieces)
            + [pl.BlockSpec(memory_space=pl.ANY)],
            out_specs=[pl.BlockSpec((step // 2, model), lambda i, at: (i, 0))] * 2,
            scratch_shapes=[
                pltpu.VMEM((frames, model), jnp.bfloat16), pltpu.VMEM((step, model), jnp.bfloat16)
            ],
        ),
        out_shape=[pltpu.HBM((inner // 2, model), jnp.bfloat16)] * 2,
        compiler_params=pltpu.CompilerParams(vmem_limit_bytes=40 * MIB),
        cost_estimate=cost(
            2 * frames * model * inner, 0, 2 * frames * (inner + model) + 2 * model * inner
        ),
        name="grad_out",
    )(place, in_hbm(act), *[in_hbm(p) for p in pieces], in_hbm(dep))


def grad_in_kernel(count, share, at, slope_ref, *refs):
    acts, branches, cuts = refs[:4], refs[4:8], refs[8 : 8 + count]
    dep, send_ref, keep_ref, act_rows, branch_rows, held = refs[8 + count :]
    tokens = acts[0].shape[0]

    @pl.when(pl.program_id(0) == 0)
    def _():
        for k in range(4):
            act_rows[k * tokens : (k + 1) * tokens] = acts[k][...]
            branch_rows[k * tokens : (k + 1) * tokens] = branches[k][...]

    cut = jnp.concatenate([c[...] for c in cuts], axis=0)
    d_hidden = (dot_turned(cut, branch_rows[...]) * slope_ref[...].astype(jnp.float32)).astype(jnp.bfloat16)
    held[...] = dot(d_hidden, act_rows[...]).astype(jnp.bfloat16).T
    store_halves(held, at[1] & 1, held.shape[0] // share // 2, share, send_ref, keep_ref)


def grad_in_of(place, slope, acts, branches, weight, groups, share, dep):
    inner, frames = slope.shape
    tokens, model = acts[0].shape
    parts = len(acts)
    width = LANES
    count = 4
    if weight.shape[0] // groups // parts == width:
        source, where = weight, lambda g, at: (g * parts + at[0], 0)
    else:
        source, where = take_rows(weight, groups, place[0], parts), lambda g, at: (g, 0)
    return pl.pallas_call(
        functools.partial(grad_in_kernel, count, share),
        grid_spec=pltpu.PrefetchScalarGridSpec(
            num_scalar_prefetch=1,
            grid=(inner // width // count,),
            in_specs=[pl.BlockSpec((count * width, frames), lambda i, at: (i, 0))]
            + [whole((tokens, model))] * (2 * parts)
            + [
                pl.BlockSpec((width, model), lambda i, at, k=k: where(i * count + k, at))
                for k in range(count)
            ]
            + [pl.BlockSpec(memory_space=pl.ANY)],
            out_specs=[pl.BlockSpec((model // 2, count * width), lambda i, at: (0, i))] * 2,
            scratch_shapes=[pltpu.VMEM((frames, model), jnp.bfloat16)] * 2
            + [pltpu.VMEM((model, count * width), jnp.bfloat16)],
        ),
        out_shape=[pltpu.HBM((model // 2, inner), jnp.bfloat16)] * 2,
        compiler_params=pltpu.CompilerParams(vmem_limit_bytes=48 * MIB),
        cost_estimate=cost(
            4 * frames * model * inner, 0, 2 * frames * (inner + 2 * model) + 4 * model * inner
        ),
        name="grad_in",
    )(place, in_hbm(slope), *[in_hbm(p) for p in (*acts, *branches)], *([in_hbm(source)] * count), in_hbm(dep))


def both_kernel(count, share, in_share, at, *refs):
    acts, branches = refs[:4], refs[4:8]
    ins, outs = refs[8 : 8 + count], refs[8 + count : 8 + 2 * count]
    dep, out_send, out_keep, in_send, in_keep, act_rows, branch_rows, out_held, in_held = refs[8 + 2 * count :]
    tokens = acts[0].shape[0]

    @pl.when(pl.program_id(0) == 0)
    def _():
        for k in range(4):
            act_rows[k * tokens : (k + 1) * tokens] = acts[k][...]
            branch_rows[k * tokens : (k + 1) * tokens] = branches[k][...]

    w_in = jnp.concatenate([c[...] for c in ins], axis=1).T
    w_out = jnp.concatenate([c[...] for c in outs], axis=0)
    mid, slope = silu_pair(dot_turned(w_in, act_rows[...]))
    d_hidden = (dot_turned(w_out, branch_rows[...]) * slope).astype(jnp.bfloat16)
    out_held[...] = dot(mid.astype(jnp.bfloat16), branch_rows[...]).astype(jnp.bfloat16)
    in_held[...] = dot(d_hidden, act_rows[...]).astype(jnp.bfloat16).T
    store_halves(out_held, at[1] & 1, out_held.shape[0] // share // 2, share, out_send, out_keep)
    store_halves(in_held, at[1] & 1, in_held.shape[0] // in_share // 2, in_share, in_send, in_keep)


def grads_of_both(place, acts, branches, w_in, w_out, groups, dep):
    tokens, model = acts[0].shape
    parts = len(acts)
    frames = parts * tokens
    inner = w_in.shape[1] // parts
    width, count = LANES, 4
    if w_in.shape[1] // groups // parts == width:
        source_in, at_in = w_in, lambda g, at: (0, g * parts + at[0])
        source_out, at_out = w_out, lambda g, at: (g * parts + at[0], 0)
    else:
        source_in, at_in = take_columns(w_in, groups, place[0], parts), lambda g, at: (0, g)
        source_out, at_out = take_rows(w_out, groups, place[0], parts), lambda g, at: (g, 0)
    step = count * width
    return pl.pallas_call(
        functools.partial(both_kernel, count, inner // groups, model // groups),
        grid_spec=pltpu.PrefetchScalarGridSpec(
            num_scalar_prefetch=1,
            grid=(inner // step,),
            in_specs=[whole((tokens, model))] * (2 * parts)
            + [pl.BlockSpec((model, width), lambda i, at, k=k: at_in(i * count + k, at)) for k in range(count)]
            + [pl.BlockSpec((width, model), lambda i, at, k=k: at_out(i * count + k, at)) for k in range(count)]
            + [pl.BlockSpec(memory_space=pl.ANY)],
            out_specs=[pl.BlockSpec((step // 2, model), lambda i, at: (i, 0))] * 2
            + [pl.BlockSpec((model // 2, step), lambda i, at: (0, i))] * 2,
            scratch_shapes=[pltpu.VMEM((frames, model), jnp.bfloat16)] * 2
            + [pltpu.VMEM((step, model), jnp.bfloat16), pltpu.VMEM((model, step), jnp.bfloat16)],
        ),
        out_shape=[pltpu.HBM((inner // 2, model), jnp.bfloat16)] * 2
        + [pltpu.HBM((model // 2, inner), jnp.bfloat16)] * 2,
        compiler_params=pltpu.CompilerParams(vmem_limit_bytes=56 * MIB),
        cost_estimate=cost(8 * frames * model * inner, 2 * frames * inner, 4 * frames * model + 8 * model * inner),
        name="grads_of_both",
    )(place, *[in_hbm(p) for p in (*acts, *branches)], *([in_hbm(source_in)] * count), *([in_hbm(source_out)] * count), in_hbm(dep))


def shards(
    features,
    lengths,
    buckets,
    gain_first,
    first_in,
    first_out,
    gain_attend,
    query_weight,
    key_weight,
    value_weight,
    output_weight,
    bias_table,
    gain_conv,
    point_in,
    depth_weight,
    batch_scale,
    batch_shift,
    point_out,
    gain_second,
    second_in,
    second_out,
    gain_final,
    cotangent,
):
    RECEIVED.clear()
    row_count, width, model = features.shape
    tokens = row_count * width
    heads, bucket_count = bias_table.shape
    head_dim = model // heads
    parts = lax.axis_size("tm")
    groups = lax.axis_size("rows")
    frames = width * parts
    half = depth_weight.shape[0] // 2
    taps = depth_weight.shape[0]
    place = lax.axis_index("tm")
    row_place = lax.axis_index("rows")
    side = place % 2
    far = place // 2
    offset = place * width
    near_heads = heads // 2
    pair = 2 * width
    places = jnp.stack([place, row_place]).astype(jnp.int32)
    info = jnp.stack([side, far, offset, lengths[0], row_place]).astype(jnp.int32)

    flat_features = features.reshape(tokens, model)
    after_first, act_first, slope_first, act_attend = first_forward(
        flat_features, gain_first, gain_attend, first_in, first_out
    )
    act_near, act_far = swap(act_attend, "tm", 1), swap(act_attend, "tm", 2)

    near_table = lax.dynamic_slice_in_dim(bias_table, side * near_heads, near_heads, 0)
    span = pair + frames
    turned = jnp.pad(buckets[::-1], (0, 1), constant_values=-1)
    window = lax.dynamic_slice_in_dim(turned, far * pair, span, 0)
    one_hot = (window[:, None] == jnp.arange(bucket_count)[None, :]).astype(jnp.float32)
    bias_lines = lax.dot_general(
        near_table, one_hot, (((1,), (1,)), ((), ())), precision=lax.Precision.HIGHEST
    )
    bias = skewed(bias_lines[:, None, :])
    key_blocks = frames // LANES
    block = jnp.arange(key_blocks)
    block = (block + far * (key_blocks // 2)) % key_blocks
    at = jnp.concatenate([frames - LANES - LANES * block, LANES * block, lengths[:1], side[None]]).astype(jnp.int32)

    query, key, value = project(info, act_attend, act_near, (query_weight, key_weight, value_weight))
    act_far, act_first, key, bias = tie(act_far, act_first, key, bias)
    act_cross = swap(act_far, "tm", 1)
    act_first_near, act_first_far = swap(act_first, "tm", 1), swap(act_first, "tm", 2)
    key_far, value_far = project(info, act_far, act_cross, (key_weight, value_weight))
    own_mixed, other_mixed, lse = attend(
        at, query, key, key_far, value, value_far, bias, near_heads, head_dim
    )
    other_mixed = swap(other_mixed, "tm", 1)

    attended, after_attend, act_conv, joined_value, gate, gated, gated_first, gated_last = mix(
        info, own_mixed, other_mixed, output_weight, after_first, gain_conv, point_in, half, act_first_far
    )
    act_first_all = [act_first, act_first_near, act_first_far, swap(act_first_far, "tm", 1)]
    up = [(i, i + 1) for i in range(parts - 1)]
    down = [(j, i) for i, j in up]
    gated_before = lax.ppermute(gated_last, "tm", up)
    gated_after = lax.ppermute(gated_first, "tm", down)
    filtered, moments = filter_frames(info, gated, gated_before, gated_after, depth_weight)
    local_count = jnp.clip(lengths[0] - offset, 0, width).astype(jnp.float32)
    count, batch_mean, spread = mesh_moments(local_count, moments[0], moments[1])
    count = count[0]
    rstd_batch = lax.rsqrt(spread / count + EPS)
    stats = jnp.stack([batch_mean, rstd_batch, batch_scale, batch_shift])
    (
        act_batch, act_second, output, branch_second, grad, d_branch_send, d_branch, d_normal, second_sums,
        batch_sums, edge_first, edge_last,
    ) = second_both(
        info, filtered, stats, after_attend, cotangent.reshape(tokens, model),
        gain_second, gain_final, point_out, second_in, second_out, half, (act_first_all[3],),
    )
    output = output.reshape(row_count, width, model)

    edge_before = lax.ppermute(edge_last, "tm", up)
    edge_after = lax.ppermute(edge_first, "tm", down)
    first_step = batch_sums + swap(batch_sums, *hops()[0])
    first_step, act_second, branch_second = tie(first_step, act_second, branch_second)
    act_second_all = spread_tm(act_second)
    branch_second_far = swap(branch_second, "tm", 2)
    branch_second_near = swap(branch_second, "tm", 1)
    batch_grads = mesh_sum(first_step, hops()[1:])
    joined_send, d_joined, grad, d_attend, conv_small = conv_back(
        info, d_normal, filtered, edge_before, edge_after, stats, batch_grads / count, depth_weight,
        gated, gated_before, gated_after, joined_value, gate, point_in, after_attend, gain_conv, grad,
        (act_second_all[2],),
    )
    d_attend_near = swap(d_attend, "tm", 1)

    held = near_heads * head_dim
    share = model // groups
    conv_send, conv_keep = cross_grads(
        info,
        [
            ((act_conv, swap(act_conv, "tm", 1)), (d_joined, swap(joined_send, "tm", 1)), model),
            ((act_batch, swap(act_batch, "tm", 1)), (d_branch, swap(d_branch_send, "tm", 1)), held),
            ((attended, swap(attended, "tm", 1)), (d_attend, d_attend_near), held),
        ],
        deps=(branch_second_near, act_second_all[1], act_second_all[3]),
    )

    branch_second_far, conv_send = tie(branch_second_far, conv_send)
    conv_got = swap(conv_send, "tm", 2)
    branch_second_all = [
        branch_second, branch_second_near, branch_second_far, swap(branch_second_far, "tm", 1)
    ]
    out_send, out_keep, in_send, in_keep = grads_of_both(
        places, act_second_all, branch_second_all, second_in, second_out, groups, conv_keep
    )
    d_attend_near, in_keep = tie(d_attend_near, in_keep)
    second_sums_of = [RowSum(out_send, out_keep, share), RowSum(in_send, in_keep, share)]

    d_query, d_key, d_value, skew_lines, far_send, far_keep = attend_back(
        at, query, key, key_far, value, value_far, d_attend, d_attend_near,
        (output_weight, key_weight, value_weight), lse, bias, near_heads, head_dim,
    )
    far_mine = add(info, (far_keep, swap(far_send, "tm", 1)), jnp.bfloat16, second_sums_of[0].terms[1])
    far_back = swap(far_mine, "tm", 2)
    conv_sum = opened(info, conv_keep, conv_got, share, far_mine)
    kept = conv_sum.terms[0]
    pair_send, pair_keep = input_back(
        info, (d_query, d_key, d_value), (0, 0, 0), (query_weight, key_weight, value_weight), width, (kept,)
    )
    attend_sum = RowSum(*cross_grads(
        info,
        [
            ((act_attend, act_near), (d_query,), held),
            ((act_attend, act_near, act_far, act_cross), (d_key,), held),
            ((act_attend, act_near, act_far, act_cross), (d_value,), held),
        ],
        split=False,
        deps=(pair_keep, second_sums_of[1].terms[1]),
    ), share)
    kept = merge(info, second_sums_of, attend_sum.terms[0])
    mid_first, slope_first_part = again(places, act_first_all, first_in, groups, kept)
    grad, branch_first, grad_gain_attend = branch_of(
        info, pair_keep, swap(pair_send, "tm", 1), far_back, after_first, gain_attend, grad,
        (mid_first, conv_sum.terms[1]),
    )
    branch_far = swap(branch_first, "tm", 2)
    grad_features, grad_gain_first = first_backward(
        info, grad, flat_features, gain_first, slope_first, first_in, first_out, ()
    )
    grad_features = grad_features.reshape(row_count, width, model)
    kept = merge(info, second_sums_of, grad_gain_first)
    branch_far, second_sums_of[-1].terms[0] = tie(branch_far, kept)
    branch_first_all = [branch_first, swap(branch_first, "tm", 1), branch_far, swap(branch_far, "tm", 1)]
    first_out_sum = RowSum(
        *grad_out_of(places, mid_first, branch_first_all, share, second_sums_of[-1].terms[0]), share
    )
    late_sums = [conv_sum, attend_sum]
    kept = merge(info, late_sums, first_out_sum.terms[0])
    table_lines = sum(jnp.pad(skew_lines[:, r], ((0, 0), (7 - r, 0)))[:, :span] for r in range(8))
    near_grad = lax.dot_general(
        table_lines, one_hot, (((1,), (0,)), ((), ())), precision=lax.Precision.HIGHEST
    )
    grad_table = lax.dynamic_update_slice_in_dim(
        jnp.zeros((heads, bucket_count), jnp.float32), near_grad, side * near_heads, 0
    )
    small = jnp.concatenate(
        [
            grad_gain_first,
            grad_gain_attend,
            second_sums,
            conv_small,
            jnp.pad(grad_table.reshape(1, -1), ((0, 0), (0, model - heads * bucket_count))),
        ],
        axis=0,
    )
    first_in_sum = RowSum(*grad_in_of(
        places, slope_first_part, act_first_all, branch_first_all, first_out, groups, share, kept,
    ), share)

    def hop(step, value, kept):
        value = value + swap(value, *step)
        return tie(value, kept)

    steps = hops()
    second_piece = joined(info, second_sums_of, first_in_sum.terms[0])
    second_pieces = spread_tm(second_piece)
    kept = merge(info, [first_out_sum], second_piece)
    kept = merge(info, late_sums, kept)
    small, attend_sum.terms[0] = hop(steps[0], small, kept)
    small, attend_sum.terms[0] = hop(steps[1], small, attend_sum.terms[0])
    kept = merge(info, [first_in_sum], attend_sum.terms[0])
    kept = merge(info, [first_out_sum], kept)
    small, first_out_sum.terms[0] = hop(steps[2], small, kept)
    for step in steps[3:-2]:
        small, first_out_sum.terms[0] = hop(step, small, first_out_sum.terms[0])
    conv_piece = joined(info, [conv_sum], first_out_sum.terms[0])
    attend_piece = joined(info, [attend_sum], conv_piece)
    conv_pieces = spread_tm(conv_piece)
    attend_got = swap(attend_piece, "tm", 2)
    kept = merge(info, [first_in_sum], attend_piece)
    if len(steps) > 4:
        small, first_in_sum.terms[0] = hop(steps[-2], small, kept)
    first_out_piece = joined(info, [first_out_sum], first_in_sum.terms[0])
    small, first_out_piece = hop(steps[-1], small, first_out_piece)
    first_out_pieces = spread_tm(first_out_piece)
    attend_piece = join(info, [[attend_piece, attend_got]], first_out_piece)
    attend_pieces = [attend_piece, swap(attend_piece, "tm", 1)]
    gains = lax.dynamic_slice_in_dim(small[:5], row_place * share, share, 1)
    grad_depth = small[5 : 5 + taps]
    grad_table = small[5 + taps, : heads * bucket_count].reshape(heads, bucket_count)

    relative = jnp.arange(parts) ^ place
    crossed = (relative % 2) * 2 + relative // 2
    quarter = model // parts

    def lay_rows(pieces):
        size = pieces[0].shape[0]
        out = jnp.zeros((parts, size, model), jnp.float32)
        for k in range(parts):
            out = lax.dynamic_update_index_in_dim(out, pieces[k].astype(jnp.float32), place ^ k, 0)
        return out.reshape(parts * size, model)

    (grad_second_in,) = lay_columns([p[:, model:] for p in second_pieces], (model,), groups, relative)
    grad_second_out = lay_rows([p[:, :model] for p in second_pieces])
    grad_point_in, grad_point_out, grad_output = lay_columns(
        conv_pieces, (2 * quarter, quarter, quarter), 1, crossed
    )
    grad_query, grad_key, grad_value = lay_columns(
        attend_pieces, (2 * quarter,) * 3, 1, jnp.stack([side, 1 - side])
    )
    first_in_pieces = spread_tm(
        joined(info, [first_in_sum], grad_second_in, grad_second_out, grad_point_out, grad_query)
    )
    grad_first_out = lay_rows(first_out_pieces)
    (grad_first_in,) = lay_columns(first_in_pieces, (model,), groups, relative)
    return (
        output,
        grad_features,
        gains[0],
        grad_first_in,
        grad_first_out,
        gains[1],
        grad_query,
        grad_key,
        grad_value,
        grad_output,
        grad_table,
        gains[4],
        grad_point_in,
        grad_depth,
        batch_grads[1],
        batch_grads[0],
        grad_point_out,
        gains[3],
        grad_second_in,
        grad_second_out,
        gains[2],
    )


def solution(mesh):
    rows3, rows2, rows1 = P("rows", "tm", None), P("rows", None), P("rows")
    in_specs = (rows3, rows1) + (P(),) * 20 + (rows3,)
    out_specs = (
        rows3, rows3, rows1, rows2, rows2, rows1, rows2, rows2, rows2, rows2, P(),
        rows1, rows2, P(), P(), P(), rows2, rows1, rows2, rows2, rows1,
    )
    return jax.shard_map(shards, mesh=mesh, in_specs=in_specs, out_specs=out_specs, check_vma=False)
```

```python
import functools

import jax
import jax.numpy as jnp
from jax import lax
from jax.experimental import pallas as pl
from jax.experimental.pallas import tpu as pltpu
from jax.sharding import PartitionSpec as P

EPS = 1e-05
NEGATIVE = -1e30
LANES = 128
MIB = 1024 * 1024
BLOCK = 1024
EFFORT = 0.0005


RECEIVED = []


def swap(value, axis, bit):
    count = lax.axis_size(axis)
    got = lax.ppermute(value, axis, [(i, i ^ bit) for i in range(count)])
    RECEIVED.append(got)
    return got


def is_received(value):
    return any(value is got for got in RECEIVED)


def hops():
    wide, deep = lax.axis_size("tm"), lax.axis_size("rows")
    found = [("tm", 1 << b) for b in range(wide.bit_length() - 1)][::-1]
    return found + [("rows", 1 << b) for b in range(deep.bit_length() - 1)]


def mesh_sum(value, steps):
    for axis, bit in steps:
        value = value + swap(value, axis, bit)
    return value


def mesh_moments(count, mean, spread):
    for axis, bit in hops():
        sent = jnp.concatenate([mean[None], spread[None], jnp.broadcast_to(count, (1, mean.shape[0]))])
        got = swap(sent, axis, bit)
        other_mean, other_spread, other_count = got[0], got[1], got[2]
        total = count + other_count
        safe = jnp.maximum(total, 1.0)
        gap = other_mean - mean
        spread = spread + other_spread + gap * gap * (count * other_count / safe)
        mean = (count * mean + other_count * other_mean) / safe
        count = total
    return (count, mean, spread)


def tie(*values):
    out = lax.optimization_barrier(values)
    RECEIVED.extend(b for a, b in zip(values, out, strict=True) if is_received(a))
    return out


def spread_tm(piece):
    far = swap(piece, "tm", 2)
    return [piece, swap(piece, "tm", 1), far, swap(far, "tm", 1)]


def silu_pair(hidden):
    sigma = 0.5 * jnp.tanh(0.5 * hidden) + 0.5
    act = hidden * sigma
    return (act, sigma + act * (1.0 - sigma))


def normed_of(values, gain):
    mean = jnp.mean(values, axis=-1, keepdims=True)
    centered = values - mean
    rstd = lax.rsqrt(jnp.mean(centered * centered, axis=-1, keepdims=True) + EPS)
    scaled = centered * rstd
    return (scaled * gain, scaled, rstd)


def normed_back(grad, values, gain):
    _, scaled, rstd = normed_of(values, gain)
    weighted = grad * gain
    inner = weighted - jnp.mean(weighted, axis=-1, keepdims=True)
    inner = inner - scaled * jnp.mean(weighted * scaled, axis=-1, keepdims=True)
    return (rstd * inner, jnp.sum(grad * scaled, axis=0, keepdims=True))


def dot(left, right):
    return jnp.dot(left, right, preferred_element_type=jnp.float32)


def dot_turned(left, right):
    return lax.dot_general(left, right, (((1,), (1,)), ((), ())), preferred_element_type=jnp.float32)


def scalars():
    return [pl.BlockSpec(memory_space=pltpu.SMEM)]


def in_hbm(value):
    if is_received(value):
        return value
    return pltpu.with_memory_space_constraint(value, pltpu.HBM)


def struct(*shape, kind=jnp.bfloat16):
    return jax.ShapeDtypeStruct(shape, kind)


class Arriving:
    def __init__(self, source, target, sem):
        self.copy = pltpu.make_async_copy(source, target, sem)
        self.target = target
        self.started = self.here = False

    def start(self):
        if not self.started:
            self.copy.start()
            self.started = True

    def get(self):
        self.start()
        if not self.here:
            self.copy.wait()
            self.here = True
        return self.target


class Leaving:
    def __init__(self, source, target, sem):
        self.ref = source
        self.target, self.sem = target, sem
        self.copy = None

    def send(self, source=None):
        self.copy = pltpu.make_async_copy(self.ref if source is None else source, self.target, self.sem)
        self.copy.start()


def flow_call(body, name, outs, scratch, info, operands, flops, mib=24, raw=(), late=(), deps=()):
    ins, results = len(operands), len(outs)

    def kernel(info, *refs):
        sources, targets = refs[:ins], refs[ins + len(deps) : ins + len(deps) + results]
        rest = refs[ins + len(deps) + results :]
        held, made = rest[:ins], rest[ins : ins + results]
        extra, sem_in, sem_out = rest[ins + results : -2], rest[-2], rest[-1]
        arriving = [
            (sources[k], held[k]) if k in raw else Arriving(sources[k], held[k], sem_in.at[k])
            for k in range(ins)
        ]
        for k in range(ins):
            if k not in raw and k not in late:
                arriving[k].start()
        leaving = [Leaving(made[k], targets[k], sem_out.at[k]) for k in range(results)]
        body(info, arriving, leaving, *extra)
        for item in leaving:
            if item.copy is None:
                item.send()
        for k in range(ins):
            if k not in raw:
                arriving[k].get()
        for item in leaving:
            item.copy.wait()

    moved = sum(o.size * o.dtype.itemsize for o in (*operands, *outs))
    return pl.pallas_call(
        kernel,
        in_specs=scalars() + [pl.BlockSpec(memory_space=pl.ANY)] * (ins + len(deps)),
        out_specs=[pl.BlockSpec(memory_space=pltpu.HBM)] * results,
        out_shape=[pltpu.HBM(o.shape, o.dtype) for o in outs],
        scratch_shapes=[pltpu.VMEM(o.shape, o.dtype) for o in (*operands, *outs)]
        + list(scratch)
        + [pltpu.SemaphoreType.DMA((ins,)), pltpu.SemaphoreType.DMA((results,))],
        compiler_params=pltpu.CompilerParams(vmem_limit_bytes=mib * MIB),
        cost_estimate=cost(flops, 0, moved),
        name=name,
    )(info, *[in_hbm(o) for o in (*operands, *deps)])


def cost(flops, transcendentals, moved):
    return pl.CostEstimate(
        flops=int(flops * EFFORT), transcendentals=int(transcendentals * EFFORT), bytes_accessed=int(moved * EFFORT)
    )


SIDE, FAR, OFFSET, LENGTH, ROW = range(5)


def row_bits():
    return lax.axis_size("rows").bit_length() - 1


def take_half(source, index, lead, size, ways=2):
    return [
        source[pl.ds(pl.multiple_of((k * ways + index) * size, size), size)] for k in range(lead)
    ]


def phases(share, far_first):
    bits = list(range(row_bits()))
    if far_first:
        return [(bit, 2 * share) for bit in bits[1:]] + [(0, share)]
    return [(bit, share) for bit in bits]


def total_of(parts):
    total = parts[0].astype(jnp.float32)
    for part in parts[1:]:
        total = total + part.astype(jnp.float32)
    return total.astype(jnp.bfloat16)


def merge_kernel(plan, info, ins, outs):
    at = 0
    for g, (count, bit, chunk) in enumerate(plan):
        held = [item.get() for item in ins[at : at + count]]
        at += count
        mine = (info[ROW] >> bit) & 1
        lead = held[0].shape[0] // chunk // 2
        for index, out in ((1 - mine, outs[2 * g]), (mine, outs[2 * g + 1])):
            parts = [take_half(h, index, lead, chunk) for h in held]
            for k in range(lead):
                out.ref[k * chunk : (k + 1) * chunk] = total_of([p[k] for p in parts])
            out.send()


def join_kernel(counts, info, ins, outs):
    begin = at = 0
    for count in counts:
        held = [item.get()[...] for item in ins[at : at + count]]
        at += count
        width = held[0].shape[1]
        outs[0].ref[:, begin : begin + width] = total_of(held)
        begin += width


class RowSum:
    def __init__(self, send, keep, share, far_first=False):
        self.left = phases(share, far_first)
        self.exchange(send, keep)

    def exchange(self, send, keep):
        bit, _ = self.left.pop(0)
        self.terms = [keep, swap(send, "rows", 1 << bit)]


def merge(info, sums, *deps):
    outs = []
    for total in sums:
        rows, columns = total.terms[0].shape
        outs += [struct(rows // 2, columns)] * 2
    plan = [(len(t.terms), *t.left[0]) for t in sums]
    made = flow_call(
        functools.partial(merge_kernel, plan), "merge",
        outs, [], info, tuple(x for t in sums for x in t.terms), 0, deps=deps,
    )
    for k, total in enumerate(sums):
        total.exchange(made[2 * k], made[2 * k + 1])
    return sums[-1].terms[0]


def joined(info, sums, *deps):
    while any(t.left for t in sums):
        merge(info, [t for t in sums if t.left])
    return join(info, [t.terms for t in sums], *deps)


def join(info, groups, *deps):
    columns = sum(g[0].shape[1] for g in groups)
    return flow_call(
        functools.partial(join_kernel, [len(g) for g in groups]), "join",
        [struct(groups[0][0].shape[0], columns)], [], info, tuple(x for g in groups for x in g), 0, deps=deps,
    )[0]


def opened(info, keep, got, share, *deps):
    rows, columns = keep.shape
    return RowSum(
        *flow_call(
            functools.partial(merge_kernel, [(2, 0, share)]), "merge",
            [struct(rows // 2, columns)] * 2, [], info, (keep, got), 0, deps=deps,
        ),
        share,
    )


def project_kernel(info, ins, outs, sem, rows):
    mine, other, *weights = ins
    side = info[SIDE]
    half = outs[0].ref.shape[1]
    lanes = pl.ds(pl.multiple_of(side * half, half), half)
    copies = [
        pltpu.make_async_copy(source.at[:, lanes], held.at[:, :half], sem.at[k])
        for k, (source, held) in enumerate(weights)
    ]
    for copy in copies:
        copy.start()
    tokens = mine.target.shape[0]
    rows[pl.ds(pl.multiple_of(side * tokens, tokens), tokens)] = mine.get()[...]
    rows[pl.ds(pl.multiple_of((1 - side) * tokens, tokens), tokens)] = other.get()[...]
    for copy, (_, held), out in zip(copies, weights, outs, strict=True):
        copy.wait()
        out.ref[...] = dot(rows[...], held[:, :half]).astype(jnp.bfloat16)
        out.send()


def project(info, mine, other, weights, deps=()):
    tokens, model = mine.shape
    pair = 2 * tokens
    return flow_call(
        project_kernel, "project",
        [struct(pair, model // 2)] * len(weights),
        [pltpu.SemaphoreType.DMA((len(weights),)), pltpu.VMEM((pair, model), jnp.bfloat16)],
        info, (mine, other, *weights), pair * model * model * len(weights),
        raw=tuple(range(2, 2 + len(weights))),
        deps=deps,
    )


def rows_of(length, first, count):
    frame = lax.broadcasted_iota(jnp.int32, (count, 1), 0) + first
    return ((frame >= 0) & (frame < length)).astype(jnp.float32)


def mix_kernel(
    info, own_ref, other_ref, weight, state_ref, gain_ref, value_w, gate_w, dep,
    attended_ref, after_ref, act_ref, value_ref, gate_ref, gated_ref, first_ref, last_ref,
):
    side = info[SIDE]
    tokens, half = own_ref.shape

    @pl.when(pl.program_id(0) == 0)
    def _():
        attended_ref[:, pl.ds(pl.multiple_of(side * half, half), half)] = own_ref[...]
        attended_ref[:, pl.ds(pl.multiple_of((1 - side) * half, half), half)] = other_ref[...]
        values = state_ref[...] + dot(attended_ref[...], weight[...])
        after_ref[...] = values
        act_ref[...] = normed_of(values, gain_ref[...])[0].astype(jnp.bfloat16)

    value = dot(act_ref[...], value_w[...])
    gate = 0.5 * jnp.tanh(0.5 * dot(act_ref[...], gate_w[...])) + 0.5
    value_ref[...] = value.astype(jnp.bfloat16)
    gate_ref[...] = gate.astype(jnp.bfloat16)
    gated_ref[...] = value * gate * rows_of(info[LENGTH], info[OFFSET], tokens)
    half = first_ref.shape[0]
    first_ref[...] = gated_ref[:half].astype(jnp.bfloat16)
    last_ref[...] = gated_ref[tokens - half :].astype(jnp.bfloat16)


def mix(info, own, other, weight, state, gain, point_in, half, dep):
    tokens, model = state.shape
    step = 512
    steps = model // step
    flat = (tokens, model)
    column = pl.BlockSpec((tokens, step), lambda i: (0, i))
    return pl.pallas_call(
        mix_kernel,
        grid=(steps,),
        in_specs=scalars() + [
            whole(own.shape), whole(own.shape), whole(weight.shape), whole(flat), whole((1, model)),
            pl.BlockSpec((model, step), lambda i: (0, i)),
            pl.BlockSpec((model, step), lambda i: (0, steps + i)),
            pl.BlockSpec(memory_space=pl.ANY),
        ],
        out_specs=[whole(flat)] * 3 + [column] * 3 + [pl.BlockSpec((half, step), lambda i: (0, i))] * 2,
        out_shape=[
            pltpu.HBM(flat, jnp.bfloat16), pltpu.HBM(flat, jnp.float32), pltpu.HBM(flat, jnp.bfloat16),
            pltpu.HBM(flat, jnp.bfloat16), pltpu.HBM(flat, jnp.bfloat16), pltpu.HBM(flat, jnp.float32),
            struct(half, model), struct(half, model),
        ],
        compiler_params=pltpu.CompilerParams(vmem_limit_bytes=32 * MIB),
        cost_estimate=cost(
            6 * tokens * model * model,
            tokens * model,
            6 * model * model + 20 * tokens * model,
        ),
        name="mix",
    )(info, in_hbm(own), other, weight, state, gain[None], point_in, point_in, in_hbm(dep))


def filter_kernel(info, ins, outs, wide):
    gated_ref, before_ref, after_ref, taps_ref = [item.get() for item in ins]
    filtered_ref, moments_ref = [item.ref for item in outs]
    tokens = gated_ref.shape[0]
    half = before_ref.shape[0]
    wide[8 : 8 + tokens] = gated_ref[...]
    wide[8 - half : 8] = before_ref[...].astype(jnp.float32)
    wide[8 + tokens : 8 + tokens + half] = after_ref[...].astype(jnp.float32)
    filtered = taps_ref[0:1] * wide[8 - half : 8 - half + tokens]
    for tap in range(1, taps_ref.shape[0]):
        filtered = filtered + taps_ref[tap : tap + 1] * wide[8 - half + tap : 8 - half + tap + tokens]
    filtered_ref[...] = filtered
    outs[0].send()
    valid = rows_of(info[LENGTH], info[OFFSET], tokens)
    count = jnp.clip(info[LENGTH] - info[OFFSET], 1, tokens).astype(jnp.float32)
    mean = jnp.sum(filtered * valid, axis=0, keepdims=True) / count
    gap = (filtered - mean) * valid
    moments_ref[0:1] = mean
    moments_ref[1:2] = jnp.sum(gap * gap, axis=0, keepdims=True)


def filter_frames(info, gated, before, later, depth):
    tokens, model = gated.shape
    return flow_call(
        filter_kernel, "filter_frames",
        [struct(tokens, model, kind=jnp.float32), struct(2, model, kind=jnp.float32)],
        [pltpu.VMEM((tokens + 16, model), jnp.float32)],
        info, (gated, before, later, depth), 10 * tokens * model,
    )


def weight_copies(pair_in, pair_out, sem, block):
    def at(i):
        lanes = pl.ds(pl.multiple_of(i * block, block), block)
        return (
            pltpu.make_async_copy(pair_in[0].at[:, lanes], pair_in[1].at[:, lanes], sem.at[0, i]),
            pltpu.make_async_copy(pair_out[0].at[lanes, :], pair_out[1].at[lanes, :], sem.at[1, i]),
        )

    return at


def second_kernel(info, ins, outs, sem, state, grad, total, slopes, low_ref):
    filtered, stats, state_in, cot, gain, final_gain, point, pair_in, pair_out = ins
    w_in, w_out = pair_in[1], pair_out[1]
    act_batch, act_out, output, branch_out, grad_out, conv_send, conv_keep, d_norm_out, sums, batch_sums, edge_first, edge_last = outs
    tokens = filtered.target.shape[0]
    steps = w_in.shape[1] // BLOCK
    valid = rows_of(info[LENGTH], info[OFFSET], tokens)
    copies = weight_copies(pair_in, pair_out, sem, BLOCK)
    filtered_ref, stats_ref = filtered.get(), stats.get()

    def normalized():
        scaled = (filtered_ref[...] - stats_ref[0:1]) * stats_ref[1:2]
        return (scaled, scaled * stats_ref[2:3] + stats_ref[3:4])

    act = silu_pair(normalized()[1])[0].astype(jnp.bfloat16)
    act_batch.ref[...] = act
    point_ref = point.get()
    for i in range(2):
        for copy in copies(i):
            copy.start()
    act_batch.send()
    values = state_in.get()[...] + dot(act, point_ref[...])
    state[...] = values
    act_ref = act_out.ref
    act_ref[...] = normed_of(values, gain.get()[...])[0].astype(jnp.bfloat16)
    act_out.send()
    cot.start()
    total[...] = jnp.zeros_like(total)

    def forward(i, carry):
        lanes = pl.ds(pl.multiple_of(i * BLOCK, BLOCK), BLOCK)
        for copy in copies(i):
            copy.wait()

        @pl.when(i + 2 < steps)
        def _():
            for copy in copies(i + 2):
                copy.start()

        mid, slope = silu_pair(dot(act_ref[...], w_in[:, lanes]))
        slopes[:, lanes] = slope.astype(jnp.bfloat16)
        total[...] += dot(mid.astype(jnp.bfloat16), w_out[lanes, :])
        return carry

    lax.fori_loop(0, steps, forward, 0)
    values = state[...] + 0.5 * total[...]
    final = final_gain.get()[...]
    normed, _, _ = normed_of(values, final)
    output.ref[...] = (normed * valid).astype(jnp.bfloat16)
    output.send()
    begin, sums.ref[0:1] = normed_back(cot.get()[...].astype(jnp.float32) * valid, values, final)
    grad[...] = begin
    branch_ref = branch_out.ref
    branch_ref[...] = (0.5 * begin).astype(jnp.bfloat16)
    branch_out.send()
    total[...] = jnp.zeros_like(total)

    def backward(i, carry):
        lanes = pl.ds(pl.multiple_of(i * BLOCK, BLOCK), BLOCK)
        part = dot_turned(branch_ref[...], w_out[lanes, :])
        part = (part * slopes[:, lanes].astype(jnp.float32)).astype(jnp.bfloat16)
        total[...] += dot_turned(part, w_in[:, lanes])
        return carry

    lax.fori_loop(0, steps, backward, 0)
    d_values, sums.ref[1:2] = normed_back(total[...], state[...], gain.get()[...])
    later = grad[...] + d_values
    grad_out.ref[...] = later
    grad_out.send()
    low = later.astype(jnp.bfloat16)
    low_ref[...] = low
    side = info[SIDE]
    half = low.shape[1] // 2
    conv_send.send(low_ref.at[:, pl.ds(pl.multiple_of((1 - side) * half, half), half)])
    conv_keep.send(low_ref.at[:, pl.ds(pl.multiple_of(side * half, half), half)])
    scaled, normal = normalized()
    d_norm = dot_turned(low, point.get()[...]) * silu_pair(normal)[1] * valid
    d_norm_out.ref[...] = d_norm
    d_norm_out.send()
    batch_sums.ref[0:1] = jnp.sum(d_norm, axis=0, keepdims=True)
    batch_sums.ref[1:2] = jnp.sum(d_norm * scaled, axis=0, keepdims=True)
    half = edge_first.ref.shape[0] // 2
    for edge, rows in ((edge_first, slice(0, half)), (edge_last, slice(tokens - half, tokens))):
        edge.ref[:half] = d_norm_out.ref[rows]
        edge.ref[half:] = filtered_ref[rows]


def second_both(info, filtered, stats, state, cotangent, gain, final_gain, point_out, w_in, w_out, half, deps):
    tokens, model = state.shape
    inner = w_in.shape[1]
    flat = (tokens, model)
    low, high = struct(*flat), struct(*flat, kind=jnp.float32)
    return flow_call(
        second_kernel, "second_both",
        [low, low, low, low, high, struct(tokens, model // 2), struct(tokens, model // 2), high,
         struct(2, model, kind=jnp.float32), struct(2, model, kind=jnp.float32),
         struct(2 * half, model, kind=jnp.float32), struct(2 * half, model, kind=jnp.float32)],
        [
            pltpu.SemaphoreType.DMA((2, inner // BLOCK)),
            pltpu.VMEM(flat, jnp.float32), pltpu.VMEM(flat, jnp.float32), pltpu.VMEM(flat, jnp.float32),
            pltpu.VMEM((tokens, inner), jnp.bfloat16), pltpu.VMEM(flat, jnp.bfloat16),
        ],
        info,
        (filtered, stats, state, cotangent, gain[None], final_gain[None], point_out, w_in, w_out),
        8 * tokens * model * inner + 4 * tokens * model * model,
        mib=48,
        raw=(7, 8),
        late=(3,),
        deps=deps,
    )


def conv_back_kernel(info, ins, outs, wide, joined_ref):
    d_norm_ref, filtered_ref, before_ref, after_ref, stats_ref, sums_ref, taps_ref = [i.get() for i in ins[:7]]
    for item in ins[8:11]:
        item.start()
    gated_ref = ins[7].get()
    value, gate, point, state, gain, grad = ins[8:]
    out_ref, low_ref, small_ref = [item.ref for item in outs[2:]]
    tokens, model = d_norm_ref.shape
    half = before_ref.shape[0] // 2

    def d_filtered(d_norm, filtered, first):
        valid = rows_of(info[LENGTH], first, d_norm.shape[0])
        scaled = (filtered - stats_ref[0:1]) * stats_ref[1:2]
        inner = d_norm - sums_ref[0:1] - scaled * sums_ref[1:2]
        return valid * (stats_ref[2:3] * stats_ref[1:2]) * inner

    offset = info[OFFSET]
    wide[8 : 8 + tokens] = d_filtered(d_norm_ref[...], filtered_ref[...], offset)
    wide[8 - half : 8] = d_filtered(before_ref[:half], before_ref[half:], offset - half)
    wide[8 + tokens : 8 + tokens + half] = d_filtered(after_ref[:half], after_ref[half:], offset + tokens)
    d_gated = jnp.zeros((tokens, model), jnp.float32)
    for tap in range(taps_ref.shape[0]):
        begin = 8 + half - tap
        shifted = wide[begin : begin + tokens]
        d_gated = d_gated + taps_ref[tap : tap + 1] * shifted
        small_ref[1 + tap : 2 + tap] = jnp.sum(shifted * gated_ref[...], axis=0, keepdims=True)
    for item in ins[11:]:
        item.start()
    d_gated = d_gated * rows_of(info[LENGTH], offset, tokens)
    gate = gate.get()[...].astype(jnp.float32)
    d_value = d_gated * gate
    joined_ref[:, :model] = d_value.astype(jnp.bfloat16)
    joined_ref[:, model:] = (d_value * value.get()[...].astype(jnp.float32) * (1.0 - gate)).astype(jnp.bfloat16)
    side = info[SIDE]
    outs[0].send(joined_ref.at[:, pl.ds(pl.multiple_of((1 - side) * model, model), model)])
    outs[1].send(joined_ref.at[:, pl.ds(pl.multiple_of(side * model, model), model)])
    d_values, small_ref[0:1] = normed_back(
        dot_turned(joined_ref[...], point.get()[...]), state.get()[...], gain.get()[...]
    )
    later = grad.get()[...] + d_values
    low_ref[...] = later.astype(jnp.bfloat16)
    outs[3].send()
    out_ref[...] = later


def conv_back(info, d_norm, filtered, before, later, stats, sums, depth, gated,
              value, gate, point_in, state, gain, grad, deps):
    tokens, model = d_norm.shape
    return flow_call(
        conv_back_kernel, "conv_back",
        [
            struct(tokens, model), struct(tokens, model),
            struct(tokens, model, kind=jnp.float32), struct(tokens, model),
            struct(1 + depth.shape[0], model, kind=jnp.float32),
        ],
        [pltpu.VMEM((tokens + 16, model), jnp.float32), pltpu.VMEM((tokens, 2 * model), jnp.bfloat16)],
        info,
        (d_norm, filtered, before, later, stats, sums, depth, gated, value,
         gate, point_in, state, gain[None], grad),
        4 * tokens * model * model,
        mib=32,
        late=tuple(range(8, 14)),
        deps=deps,
    )


def add_kernel(info, ins, outs):
    total = ins[0].get()[...].astype(jnp.float32)
    for item in ins[1:]:
        total = total + item.get()[...].astype(jnp.float32)
    outs[0].ref[...] = total.astype(outs[0].ref.dtype)


def add(info, terms, kind, *deps):
    return flow_call(
        add_kernel, "add", [struct(*terms[0].shape, kind=kind)], [], info, tuple(terms), 0, deps=deps
    )[0]


def branch_kernel(info, ins, outs):
    keep, got, far, state, gain, grad = ins
    d_input = keep.get()[...] + got.get()[...].astype(jnp.float32) + far.get()[...].astype(jnp.float32)
    d_values, outs[2].ref[...] = normed_back(d_input, state.get()[...], gain.get()[...])
    later = grad.get()[...] + d_values
    outs[1].ref[...] = (0.5 * later).astype(jnp.bfloat16)
    outs[1].send()
    outs[0].ref[...] = later


def branch_of(info, keep, got, far, state, gain, grad, deps):
    tokens, model = keep.shape
    return flow_call(
        branch_kernel, "branch",
        [struct(tokens, model, kind=jnp.float32), struct(tokens, model), struct(1, model, kind=jnp.float32)],
        [], info, (keep, got, far, state, gain[None], grad), 0, deps=deps,
    )


def input_back_kernel(count, base, info, ins, outs, sem):
    grads, weights = ins[:count], ins[count:]
    send_ref, keep_ref = outs[0].ref, outs[1].ref
    tokens = send_ref.shape[0]
    side = info[SIDE]
    half = weights[0][0].shape[1] // 2
    lanes = pl.ds(pl.multiple_of(side * half, half), half)
    copies = [
        pltpu.make_async_copy(source.at[:, lanes], held.at[:, :half], sem.at[k])
        for k, (source, held) in enumerate(weights)
    ]
    for copy in copies:
        copy.start()
    grads = [grad.get() for grad in grads]
    for copy in copies:
        copy.wait()

    def total(which):
        out = None
        for first, grad, (_, held) in zip(base, grads, weights, strict=True):
            rows = pl.ds(pl.multiple_of(first + which * tokens, LANES), tokens)
            part = dot_turned(grad[rows], held[:, :half])
            out = part if out is None else out + part
        return out

    send_ref[...] = total(1 - side).astype(jnp.bfloat16)
    outs[0].send()
    keep_ref[...] = total(side)


def input_back(info, grads, base, weights, tokens, deps=()):
    model = weights[0].shape[0]
    count = len(grads)
    return flow_call(
        functools.partial(input_back_kernel, count, base), "input_back",
        [struct(tokens, model), struct(tokens, model, kind=jnp.float32)],
        [pltpu.SemaphoreType.DMA((count,))],
        info, (*grads, *weights), 2 * tokens * model * model * count,
        mib=32, raw=tuple(range(count, 2 * count)), deps=deps,
    )


def cross_kernel(layout, split, lead, chunk, info, refs, outs, left_rows, right_rows, *held):
    far, side = info[FAR], info[SIDE]
    at = 0
    begin = 0
    for pieces, width in layout:
        lefts, right = refs[at : at + pieces], refs[at + pieces : at + pieces + (2 if width < 0 else 1)]
        at += pieces + len(right)
        tokens = lefts[0].target.shape[0]
        for k, left in enumerate(lefts):
            spot = (k // 2 * 2 + (side if k % 2 == 0 else 1 - side)) * tokens
            left_rows[pl.ds(pl.multiple_of(spot, tokens), tokens)] = left.get()[...]
        size = abs(width)
        half = size // 2 if split else size
        if len(right) == 2:
            for k, piece in enumerate(right):
                spot = (side if k == 0 else 1 - side) * tokens
                held = piece.get()
                lanes = pl.ds(0, size)
                if held.shape[1] != size:
                    lanes = pl.ds(pl.multiple_of(side * size, size), size)
                right_rows[pl.ds(pl.multiple_of(spot, tokens), tokens), :size] = held[:, lanes]
            source = right_rows
        else:
            source = right[0].get()
        count = pieces * tokens
        targets = ((1 - far, outs[0].ref), (far, outs[1].ref)) if split else ((0, held[0]),)
        for which, target in targets:
            lanes = pl.ds(pl.multiple_of(which * half, half), half)
            target[:, begin : begin + half] = lax.dot_general(
                left_rows[:count], source[:count, lanes], (((0,), (0,)), ((), ())),
                preferred_element_type=jnp.float32,
            ).astype(jnp.bfloat16)
        begin += half
    if not split:
        store_halves(held[0], info[ROW] & 1, lead, chunk, outs[0].ref, outs[1].ref)


def cross_grads(info, terms, split=True, deps=()):
    operands, layout = [], []
    total = flops = 0
    for lefts, rights, width in terms:
        operands += [*lefts, *rights]
        layout.append((len(lefts), -width if len(rights) == 2 else width))
        total += width // 2 if split else width
        tokens, model = lefts[0].shape
        flops += 2 * len(lefts) * tokens * model * width
    deepest = max(len(lefts) for lefts, *_ in terms) * tokens
    widest = max(width for *_, width in terms)
    size = model >> row_bits()
    rows = model if split else model // 2
    scratch = [pltpu.VMEM((deepest, model), jnp.bfloat16), pltpu.VMEM((deepest, widest), jnp.bfloat16)]
    if not split:
        scratch.append(pltpu.VMEM((model, total), jnp.bfloat16))
    return flow_call(
        functools.partial(cross_kernel, layout, split, model // size // 2, size), "cross_grads",
        [struct(rows, total)] * 2, scratch, info, tuple(operands), flops, mib=40, deps=deps,
    )


def first_back_kernel(info, ins, outs, sem, branch, total):
    grad, x, gain, slope, pair_in, pair_out = ins
    w_in, w_out = pair_in[1], pair_out[1]
    steps = w_in.shape[1] // BLOCK
    copies = weight_copies(pair_in, pair_out, sem, BLOCK)
    for i in range(2):
        for copy in copies(i):
            copy.start()
    grad_ref = grad.get()
    branch[...] = (0.5 * grad_ref[...]).astype(jnp.bfloat16)
    total[...] = jnp.zeros_like(total)
    slope_ref = slope.get()
    x.start()

    def backward(i, carry):
        lanes = pl.ds(pl.multiple_of(i * BLOCK, BLOCK), BLOCK)
        for copy in copies(i):
            copy.wait()

        @pl.when(i + 2 < steps)
        def _():
            for copy in copies(i + 2):
                copy.start()

        part = dot_turned(branch[...], w_out[lanes, :])
        part = (part * slope_ref[:, lanes].astype(jnp.float32)).astype(jnp.bfloat16)
        total[...] += dot_turned(part, w_in[:, lanes])
        return carry

    lax.fori_loop(0, steps, backward, 0)
    d_values, outs[1].ref[...] = normed_back(total[...], x.get()[...].astype(jnp.float32), gain.get()[...])
    outs[0].ref[...] = (grad_ref[...] + d_values).astype(jnp.bfloat16)


def first_backward(info, grad, features, gain, slope, w_in, w_out, deps):
    tokens, model = features.shape
    inner = w_in.shape[1]
    return flow_call(
        first_back_kernel, "first_backward",
        [struct(tokens, model), struct(1, model, kind=jnp.float32)],
        [pltpu.SemaphoreType.DMA((2, inner // BLOCK)), pltpu.VMEM((tokens, model), jnp.bfloat16), pltpu.VMEM((tokens, model), jnp.float32)],
        info, (grad, features, gain[None], slope, w_in, w_out), 4 * tokens * model * inner,
        mib=40, raw=(4, 5), late=(1,), deps=deps,
    )


def norm_backward(grad, scaled, rstd, gain):
    weighted = grad * gain
    inner = weighted - jnp.mean(weighted, axis=-1, keepdims=True)
    inner = inner - scaled * jnp.mean(weighted * scaled, axis=-1, keepdims=True)
    return (rstd * inner, jnp.sum(grad * scaled, axis=0))


def first_kernel(x_ref, gain_ref, next_gain_ref, w_in, w_out, state_ref, act_ref, slope_ref, next_ref, total):
    step = pl.program_id(0)

    @pl.when(step == 0)
    def _():
        values = x_ref[...].astype(jnp.float32)
        act_ref[...] = normed_of(values, gain_ref[...])[0].astype(jnp.bfloat16)
        total[...] = jnp.zeros_like(total)

    mid, slope = silu_pair(dot(act_ref[...], w_in[...]))
    slope_ref[...] = slope.astype(jnp.bfloat16)
    total[...] += dot(mid.astype(jnp.bfloat16), w_out[...])

    @pl.when(step == pl.num_programs(0) - 1)
    def _():
        values = x_ref[...].astype(jnp.float32) + 0.5 * total[...]
        state_ref[...] = values
        next_ref[...] = normed_of(values, next_gain_ref[...])[0].astype(jnp.bfloat16)


def whole(shape):
    return pl.BlockSpec(shape, lambda *_: (0,) * len(shape))


def first_forward(features, gain, next_gain, w_in, w_out):
    tokens, model = features.shape
    inner = w_in.shape[1]
    return pl.pallas_call(
        first_kernel,
        grid=(inner // BLOCK,),
        in_specs=[
            whole((tokens, model)),
            whole((1, model)),
            whole((1, model)),
            pl.BlockSpec((model, BLOCK), lambda i: (0, i)),
            pl.BlockSpec((BLOCK, model), lambda i: (i, 0)),
        ],
        out_specs=[
            whole((tokens, model)),
            whole((tokens, model)),
            pl.BlockSpec((tokens, BLOCK), lambda i: (0, i)),
            whole((tokens, model)),
        ],
        out_shape=[
            pltpu.HBM((tokens, model), jnp.float32),
            pltpu.HBM((tokens, model), jnp.bfloat16),
            pltpu.HBM((tokens, inner), jnp.bfloat16),
            pltpu.HBM((tokens, model), jnp.bfloat16),
        ],
        scratch_shapes=[pltpu.VMEM((tokens, model), jnp.float32)],
        compiler_params=pltpu.CompilerParams(vmem_limit_bytes=40 * MIB),
        cost_estimate=cost(
            4 * tokens * model * inner,
            2 * tokens * inner,
            4 * model * inner + 2 * tokens * inner,
        ),
        name="first_forward",
    )(in_hbm(features), gain[None], next_gain[None], in_hbm(w_in), in_hbm(w_out))


def take_kernel(place, source, target):
    target[...] = source[...]


def take_columns(weight, groups, place, parts):
    model, total = weight.shape
    block = total // groups // parts
    if block % LANES:
        cut = weight.reshape(model, groups, parts, block)
        return lax.dynamic_index_in_dim(cut, place, 2, keepdims=False).reshape(model, -1)
    return pl.pallas_call(
        take_kernel,
        out_shape=jax.ShapeDtypeStruct((model, total // parts), weight.dtype),
        grid_spec=pltpu.PrefetchScalarGridSpec(
            num_scalar_prefetch=1,
            grid=(groups,),
            in_specs=[pl.BlockSpec((model, block), lambda g, at: (0, g * parts + at[0]))],
            out_specs=pl.BlockSpec((model, block), lambda g, at: (0, g)),
        ),
        name="take_columns",
    )(place.reshape(1), weight)


def take_rows(weight, groups, place, parts):
    total, model = weight.shape
    cut = weight.reshape(groups, parts, total // groups // parts, model)
    return lax.dynamic_index_in_dim(cut, place, 1, keepdims=False).reshape(-1, model)


def lay_kernel(parts, widths, groups, places, *refs):
    pieces, targets = refs[:parts], refs[parts:]
    for k in range(parts):
        begin = 0
        for width, target in zip(widths, targets, strict=True):
            block = width // groups
            for g in range(groups):
                at = pl.multiple_of((g * parts + places[k]) * block, LANES)
                source = pieces[k][:, begin + g * block : begin + (g + 1) * block]
                target[:, pl.ds(at, block)] = source.astype(jnp.float32)
            begin += width


def lay_columns(pieces, widths, groups, places):
    rows = pieces[0].shape[0]
    parts = len(pieces)
    if any((width // groups) % LANES for width in widths):
        outs, begin = [], 0
        stacked = jnp.zeros((parts, *pieces[0].shape), pieces[0].dtype)
        for k in range(parts):
            stacked = lax.dynamic_update_index_in_dim(stacked, pieces[k], places[k], 0)
        for width in widths:
            cut = stacked[:, :, begin : begin + width].reshape(parts, rows, groups, width // groups)
            outs.append(cut.transpose(1, 2, 0, 3).reshape(rows, parts * width).astype(jnp.float32))
            begin += width
        return outs
    return pl.pallas_call(
        functools.partial(lay_kernel, parts, widths, groups),
        out_shape=[jax.ShapeDtypeStruct((rows, parts * width), jnp.float32) for width in widths],
        grid_spec=pltpu.PrefetchScalarGridSpec(
            num_scalar_prefetch=1,
            grid=(1,),
            in_specs=[pl.BlockSpec(p.shape, lambda i, at: (0, 0)) for p in pieces],
            out_specs=[pl.BlockSpec((rows, parts * width), lambda i, at: (0, 0)) for width in widths],
        ),
        compiler_params=pltpu.CompilerParams(vmem_limit_bytes=24 * MIB),
        name="lay_columns",
    )(places, *pieces)


def skew_kernel(line, out):
    length = line.shape[-1]
    width = out.shape[-1]
    spread = jnp.broadcast_to(line[0], (LANES, length))
    rolled = pltpu.roll(spread, length - (LANES - 1), 1, stride=1, stride_axis=0)
    out[0] = rolled[:, :width]


def skewed(lines):
    heads, _, length = lines.shape
    width = length - LANES
    return pl.pallas_call(
        skew_kernel,
        out_shape=pltpu.HBM((heads, LANES, width), jnp.float32),
        grid=(heads,),
        in_specs=[pl.BlockSpec((1, 1, length), lambda h: (h, 0, 0))],
        out_specs=pl.BlockSpec((1, LANES, width), lambda h: (h, 0, 0)),
        name="bias_rows",
    )(lines)


def attend_kernel(
    scale, at, q_ref, k_pair, k_far, v_pair, v_far, bias_ref, own_ref, other_ref, lse_ref,
    k_ref, vt_ref, s_ref, p_ref, out_ref,
):
    tile = q_ref.shape[0]
    blocks = k_ref.shape[0] // LANES
    pair = k_pair.shape[0]
    length = at[blocks * 2]

    @pl.when(pl.program_id(1) == 0)
    def _():
        k_ref[:pair] = k_pair[...]
        k_ref[pair:] = k_far[...]
        vt_ref[:, :pair] = v_pair[...].T
        vt_ref[:, pair:] = v_far[...].T

    begin = pl.program_id(1) * tile
    s_ref[...] = lax.dot_general(
        k_ref[...], q_ref[...], (((1,), (1,)), ((), ())), preferred_element_type=jnp.float32
    )
    frame = lax.broadcasted_iota(jnp.int32, (LANES, tile), 0)
    top = jnp.full((1, tile), NEGATIVE, jnp.float32)
    for b in range(blocks):
        lanes = pl.ds(pl.multiple_of(at[b] + begin, LANES), tile)
        s = s_ref[b * LANES : (b + 1) * LANES] * scale + bias_ref[0, :, lanes]
        s = jnp.where(frame < length - at[blocks + b], s, NEGATIVE)
        s_ref[b * LANES : (b + 1) * LANES] = s
        top = jnp.maximum(top, jnp.max(s, axis=0, keepdims=True))
    total = jnp.zeros((1, tile), jnp.float32)
    for b in range(blocks):
        p = jnp.exp(s_ref[b * LANES : (b + 1) * LANES] - top)
        total = total + jnp.sum(p, axis=0, keepdims=True)
        p_ref[b * LANES : (b + 1) * LANES] = p.astype(jnp.bfloat16)
    mixed = jnp.dot(vt_ref[...], p_ref[...], preferred_element_type=jnp.float32) / total
    out_ref[...] = mixed.T.astype(jnp.bfloat16)
    half = tile // 2
    side = at[blocks * 2 + 1]
    own_ref[...] = out_ref[pl.ds(pl.multiple_of(side * half, half), half)]
    other_ref[...] = out_ref[pl.ds(pl.multiple_of((1 - side) * half, half), half)]
    lse_ref[0] = top + jnp.log(total)


def attend(at, query, key, key_far, value, value_far, bias, heads, head_dim):
    queries, keys = query.shape[0], 2 * key.shape[0]
    tile = queries
    width = bias.shape[-1]
    grid_spec = pltpu.PrefetchScalarGridSpec(
        num_scalar_prefetch=1,
        grid=(heads, queries // tile),
        in_specs=[
            pl.BlockSpec((tile, head_dim), lambda h, i, at: (i, h)),
            pl.BlockSpec((keys // 2, head_dim), lambda h, i, at: (0, h)),
            pl.BlockSpec((keys // 2, head_dim), lambda h, i, at: (0, h)),
            pl.BlockSpec((keys // 2, head_dim), lambda h, i, at: (0, h)),
            pl.BlockSpec((keys // 2, head_dim), lambda h, i, at: (0, h)),
            pl.BlockSpec((1, LANES, width), lambda h, i, at: (h, 0, 0)),
        ],
        out_specs=[
            pl.BlockSpec((tile // 2, head_dim), lambda h, i, at: (0, h)),
            pl.BlockSpec((tile // 2, head_dim), lambda h, i, at: (0, h)),
            pl.BlockSpec((1, 1, tile), lambda h, i, at: (h, 0, i)),
        ],
        scratch_shapes=[
            pltpu.VMEM((keys, head_dim), jnp.bfloat16),
            pltpu.VMEM((head_dim, keys), jnp.bfloat16),
            pltpu.VMEM((keys, tile), jnp.float32),
            pltpu.VMEM((keys, tile), jnp.bfloat16),
            pltpu.VMEM((tile, head_dim), jnp.bfloat16),
        ],
    )
    return pl.pallas_call(
        functools.partial(attend_kernel, head_dim ** (-0.5)),
        out_shape=[
            pltpu.HBM((queries // 2, heads * head_dim), jnp.bfloat16),
            pltpu.HBM((queries // 2, heads * head_dim), jnp.bfloat16),
            pltpu.HBM((heads, 1, queries), jnp.float32),
        ],
        grid_spec=grid_spec,
        compiler_params=pltpu.CompilerParams(vmem_limit_bytes=24 * MIB),
        cost_estimate=cost(
            4 * heads * queries * keys * head_dim,
            heads * queries * keys,
            4 * heads * LANES * width + 4 * heads * head_dim * (queries + keys),
        ),
        name="attend",
    )(at, *[in_hbm(x) for x in (query, key, key_far, value, value_far, bias)])


def attend_back_kernel(
    scale, at, q_ref, k_pair, k_far, v_pair, v_far, da_own, da_near, wo_ref, wk_ref, wv_ref, lse_ref, bias_ref,
    dq_ref, dk_ref, dv_ref, line_ref, send_ref, far_ref,
    do_ref, all_dk, all_dv, k_ref, v_ref, kt_ref, s_ref, dp_ref, p_ref, ds_ref, skew_ref,
):
    tile = q_ref.shape[0]
    blocks = k_ref.shape[0] // LANES
    length = at[blocks * 2]
    pair = k_pair.shape[0]

    side = at[blocks * 2 + 1]
    own = da_own.shape[0]
    mine = pl.ds(pl.multiple_of(side * own, own), own)
    other = pl.ds(pl.multiple_of((1 - side) * own, own), own)
    do_ref[mine] = dot_turned(da_own[...], wo_ref[...]).astype(jnp.bfloat16)
    do_ref[other] = dot_turned(da_near[...], wo_ref[...]).astype(jnp.bfloat16)
    k_ref[:pair] = k_pair[...]
    k_ref[pair:] = k_far[...]
    v_ref[:pair] = v_pair[...]
    v_ref[pair:] = v_far[...]
    kt_ref[...] = k_ref[...].T
    skew_ref[...] = jnp.zeros_like(skew_ref)
    s_ref[...] = lax.dot_general(
        k_ref[...], q_ref[...], (((1,), (1,)), ((), ())), preferred_element_type=jnp.float32
    )
    dp_ref[...] = lax.dot_general(
        v_ref[...], do_ref[...], (((1,), (1,)), ((), ())), preferred_element_type=jnp.float32
    )
    frame = lax.broadcasted_iota(jnp.int32, (LANES, tile), 0)
    lse = lse_ref[0]
    delta = jnp.zeros((1, tile), jnp.float32)
    for b in range(blocks):
        rows = slice(b * LANES, (b + 1) * LANES)
        lanes = pl.ds(pl.multiple_of(at[b], LANES), tile)
        s = s_ref[rows] * scale + bias_ref[0, :, lanes]
        s = jnp.where(frame < length - at[blocks + b], s, NEGATIVE)
        p = jnp.exp(s - lse)
        s_ref[rows] = p
        p_ref[rows] = p.astype(jnp.bfloat16)
        delta = delta + jnp.sum(p * dp_ref[rows], axis=0, keepdims=True)
    for b in range(blocks):
        rows = slice(b * LANES, (b + 1) * LANES)
        lanes = pl.ds(pl.multiple_of(at[b], LANES), tile)
        ds = (s_ref[rows] * (dp_ref[rows] - delta)).astype(jnp.bfloat16)
        ds_ref[rows] = ds
        skew_ref[:, lanes] += ds.astype(jnp.float32)
    dv = jnp.dot(p_ref[...], do_ref[...], preferred_element_type=jnp.float32).astype(jnp.bfloat16)
    dk = jnp.dot(ds_ref[...], q_ref[...], preferred_element_type=jnp.float32) * scale
    dk = dk.astype(jnp.bfloat16)
    dq = jnp.dot(kt_ref[...], ds_ref[...], preferred_element_type=jnp.float32) * scale
    dq_ref[...] = dq.T.astype(jnp.bfloat16)
    dk_ref[...] = dk
    dv_ref[...] = dv
    head = pl.program_id(0)
    all_dk[head] = dk[pair:]
    all_dv[head] = dv[pair:]
    lines = jnp.concatenate([skew_ref[...], jnp.zeros((LANES, LANES), jnp.float32)], axis=1)
    count = LANES // 2
    while count >= 8:
        lines = lines[count:] + pltpu.roll(lines[:count], count, 1)
        count //= 2
    line_ref[0] = lines

    @pl.when(head == pl.num_programs(0) - 1)
    def _():
        def total(rows):
            heads = all_dk.shape[0]
            d_key = jnp.concatenate([all_dk[h, rows] for h in range(heads)], axis=1)
            d_value = jnp.concatenate([all_dv[h, rows] for h in range(heads)], axis=1)
            return dot_turned(d_key, wk_ref[...]) + dot_turned(d_value, wv_ref[...])

        send_ref[...] = total(other).astype(jnp.bfloat16)
        far_ref[...] = total(mine)


def attend_back(at, query, key, key_far, value, value_far, own, near, weights, lse, bias, heads, head_dim):
    queries, keys = query.shape[0], 2 * key.shape[0]
    tokens, model = own.shape
    width = bias.shape[-1]
    blocks = keys // LANES
    column = lambda h, at: (0, h)
    half = pl.BlockSpec((keys // 2, head_dim), column)
    low = jnp.bfloat16
    wo, wk, wv = weights
    grid_spec = pltpu.PrefetchScalarGridSpec(
        num_scalar_prefetch=1,
        grid=(heads,),
        in_specs=[
            pl.BlockSpec((queries, head_dim), column), half, half, half, half,
            whole((tokens, model)), whole((tokens, model)),
            pl.BlockSpec((head_dim, model), lambda h, at: (at[2 * blocks + 1] * heads + h, 0)),
            pl.BlockSpec((model, model // 2), lambda h, at: (0, at[2 * blocks + 1])),
            pl.BlockSpec((model, model // 2), lambda h, at: (0, at[2 * blocks + 1])),
            pl.BlockSpec((1, 1, queries), lambda h, at: (h, 0, 0)),
            pl.BlockSpec((1, LANES, width), lambda h, at: (h, 0, 0)),
        ],
        out_specs=[
            pl.BlockSpec((queries, head_dim), column),
            pl.BlockSpec((keys, head_dim), column),
            pl.BlockSpec((keys, head_dim), column),
            pl.BlockSpec((1, 8, width + LANES), lambda h, at: (h, 0, 0)),
            whole((tokens, model)),
            whole((tokens, model)),
        ],
        scratch_shapes=[
            pltpu.VMEM((queries, head_dim), low),
            pltpu.VMEM((heads, keys // 2, head_dim), low),
            pltpu.VMEM((heads, keys // 2, head_dim), low),
            pltpu.VMEM((keys, head_dim), low),
            pltpu.VMEM((keys, head_dim), low),
            pltpu.VMEM((head_dim, keys), low),
            pltpu.VMEM((keys, queries), jnp.float32),
            pltpu.VMEM((keys, queries), jnp.float32),
            pltpu.VMEM((keys, queries), low),
            pltpu.VMEM((keys, queries), low),
            pltpu.VMEM((LANES, width), jnp.float32),
        ],
    )
    return pl.pallas_call(
        functools.partial(attend_back_kernel, head_dim ** (-0.5)),
        out_shape=[
            pltpu.HBM((queries, heads * head_dim), low),
            pltpu.HBM((keys, heads * head_dim), low),
            pltpu.HBM((keys, heads * head_dim), low),
            pltpu.HBM((heads, 8, width + LANES), jnp.float32),
            pltpu.HBM((tokens, model), low),
            pltpu.HBM((tokens, model), jnp.float32),
        ],
        grid_spec=grid_spec,
        compiler_params=pltpu.CompilerParams(vmem_limit_bytes=48 * MIB),
        cost_estimate=cost(
            10 * heads * queries * keys * head_dim,
            heads * queries * keys,
            4 * heads * LANES * width + 8 * heads * head_dim * (queries + keys),
        ),
        name="attend_back",
    )(
        at, *[in_hbm(x) for x in (query, key, key_far, value, value_far, own, near, wo, wk, wv, lse, bias)]
    )


def again_kernel(count, at, *refs):
    pieces, cuts = refs[:4], refs[4 : 4 + count]
    act_ref, slope_ref, rows = refs[5 + count :]
    tokens = pieces[0].shape[0]

    @pl.when(pl.program_id(0) == 0)
    def _():
        for k in range(4):
            rows[k * tokens : (k + 1) * tokens] = pieces[k][...]

    for k in range(count):
        block = cuts[k].shape[1]
        mid, slope = silu_pair(dot_turned(cuts[k][...].T, rows[...]))
        act_ref[k * block : (k + 1) * block] = mid.astype(jnp.bfloat16)
        slope_ref[k * block : (k + 1) * block] = slope.astype(jnp.bfloat16)


def column_cuts(weight, groups, parts, width):
    block = weight.shape[1] // groups // parts
    if block == width:
        return weight, lambda g, at: (0, g * parts + at[0])
    return None, lambda g, at: (0, g)


def again(place, pieces, weight, groups, dep):
    parts = len(pieces)
    tokens, model = pieces[0].shape
    inner = weight.shape[1] // parts
    width = LANES
    source, where = column_cuts(weight, groups, parts, width)
    if source is None:
        source = take_columns(weight, groups, place[0], parts)
    count = 2
    cut = inner // width // count
    return pl.pallas_call(
        functools.partial(again_kernel, count),
        grid_spec=pltpu.PrefetchScalarGridSpec(
            num_scalar_prefetch=1,
            grid=(cut,),
            in_specs=[whole((tokens, model))] * parts
            + [
                pl.BlockSpec((model, width), lambda i, at, k=k: where(i * count + k, at))
                for k in range(count)
            ]
            + [pl.BlockSpec(memory_space=pl.ANY)],
            out_specs=[pl.BlockSpec((count * width, parts * tokens), lambda i, at: (i, 0))] * 2,
            scratch_shapes=[pltpu.VMEM((parts * tokens, model), jnp.bfloat16)],
        ),
        out_shape=[pltpu.HBM((inner, parts * tokens), jnp.bfloat16)] * 2,
        compiler_params=pltpu.CompilerParams(vmem_limit_bytes=40 * MIB),
        cost_estimate=cost(
            2 * parts * tokens * model * inner,
            2 * parts * tokens * inner,
            2 * parts * tokens * (2 * inner + model) + 2 * model * inner,
        ),
        name="again",
    )(place[:1], *[in_hbm(p) for p in pieces], *([in_hbm(source)] * count), in_hbm(dep))


def store_halves(held, mine, lead, size, send_ref, keep_ref):
    for index, target in ((1 - mine, send_ref), (mine, keep_ref)):
        for k, part in enumerate(take_half(held, index, lead, size)):
            target[k * size : (k + 1) * size] = part


def grad_out_kernel(share, at, act_ref, *refs):
    pieces, dep, send_ref, keep_ref, rows, held = refs[:4], *refs[4:]
    tokens = pieces[0].shape[0]

    @pl.when(pl.program_id(0) == 0)
    def _():
        for k in range(4):
            rows[k * tokens : (k + 1) * tokens] = pieces[k][...]

    held[...] = dot(act_ref[...], rows[...]).astype(jnp.bfloat16)
    store_halves(held, at[1] & 1, held.shape[0] // share // 2, share, send_ref, keep_ref)


def grad_out_of(place, act, pieces, share, dep):
    inner, frames = act.shape
    tokens, model = pieces[0].shape
    step = 512
    return pl.pallas_call(
        functools.partial(grad_out_kernel, share),
        grid_spec=pltpu.PrefetchScalarGridSpec(
            num_scalar_prefetch=1,
            grid=(inner // step,),
            in_specs=[pl.BlockSpec((step, frames), lambda i, at: (i, 0))]
            + [whole((tokens, model))] * len(pieces)
            + [pl.BlockSpec(memory_space=pl.ANY)],
            out_specs=[pl.BlockSpec((step // 2, model), lambda i, at: (i, 0))] * 2,
            scratch_shapes=[
                pltpu.VMEM((frames, model), jnp.bfloat16), pltpu.VMEM((step, model), jnp.bfloat16)
            ],
        ),
        out_shape=[pltpu.HBM((inner // 2, model), jnp.bfloat16)] * 2,
        compiler_params=pltpu.CompilerParams(vmem_limit_bytes=40 * MIB),
        cost_estimate=cost(
            2 * frames * model * inner, 0, 2 * frames * (inner + model) + 2 * model * inner
        ),
        name="grad_out",
    )(place, in_hbm(act), *[in_hbm(p) for p in pieces], in_hbm(dep))


def grad_in_kernel(count, share, at, slope_ref, *refs):
    acts, branches, cuts = refs[:4], refs[4:8], refs[8 : 8 + count]
    dep, send_ref, keep_ref, act_rows, branch_rows, held = refs[8 + count :]
    tokens = acts[0].shape[0]

    @pl.when(pl.program_id(0) == 0)
    def _():
        for k in range(4):
            act_rows[k * tokens : (k + 1) * tokens] = acts[k][...]
            branch_rows[k * tokens : (k + 1) * tokens] = branches[k][...]

    cut = jnp.concatenate([c[...] for c in cuts], axis=0)
    d_hidden = (dot_turned(cut, branch_rows[...]) * slope_ref[...].astype(jnp.float32)).astype(jnp.bfloat16)
    held[...] = dot(d_hidden, act_rows[...]).astype(jnp.bfloat16).T
    store_halves(held, at[1] & 1, held.shape[0] // share // 2, share, send_ref, keep_ref)


def grad_in_of(place, slope, acts, branches, weight, groups, share, dep):
    inner, frames = slope.shape
    tokens, model = acts[0].shape
    parts = len(acts)
    width = LANES
    count = 4
    if weight.shape[0] // groups // parts == width:
        source, where = weight, lambda g, at: (g * parts + at[0], 0)
    else:
        source, where = take_rows(weight, groups, place[0], parts), lambda g, at: (g, 0)
    return pl.pallas_call(
        functools.partial(grad_in_kernel, count, share),
        grid_spec=pltpu.PrefetchScalarGridSpec(
            num_scalar_prefetch=1,
            grid=(inner // width // count,),
            in_specs=[pl.BlockSpec((count * width, frames), lambda i, at: (i, 0))]
            + [whole((tokens, model))] * (2 * parts)
            + [
                pl.BlockSpec((width, model), lambda i, at, k=k: where(i * count + k, at))
                for k in range(count)
            ]
            + [pl.BlockSpec(memory_space=pl.ANY)],
            out_specs=[pl.BlockSpec((model // 2, count * width), lambda i, at: (0, i))] * 2,
            scratch_shapes=[pltpu.VMEM((frames, model), jnp.bfloat16)] * 2
            + [pltpu.VMEM((model, count * width), jnp.bfloat16)],
        ),
        out_shape=[pltpu.HBM((model // 2, inner), jnp.bfloat16)] * 2,
        compiler_params=pltpu.CompilerParams(vmem_limit_bytes=48 * MIB),
        cost_estimate=cost(
            4 * frames * model * inner, 0, 2 * frames * (inner + 2 * model) + 4 * model * inner
        ),
        name="grad_in",
    )(place, in_hbm(slope), *[in_hbm(p) for p in (*acts, *branches)], *([in_hbm(source)] * count), in_hbm(dep))


def both_kernel(count, share, in_share, at, *refs):
    acts, branches = refs[:4], refs[4:8]
    ins, outs = refs[8 : 8 + count], refs[8 + count : 8 + 2 * count]
    dep, out_send, out_keep, in_send, in_keep, act_rows, branch_rows, out_held, in_held = refs[8 + 2 * count :]
    tokens = acts[0].shape[0]

    @pl.when(pl.program_id(0) == 0)
    def _():
        for k in range(4):
            act_rows[k * tokens : (k + 1) * tokens] = acts[k][...]
            branch_rows[k * tokens : (k + 1) * tokens] = branches[k][...]

    w_in = jnp.concatenate([c[...] for c in ins], axis=1).T
    w_out = jnp.concatenate([c[...] for c in outs], axis=0)
    mid, slope = silu_pair(dot_turned(w_in, act_rows[...]))
    d_hidden = (dot_turned(w_out, branch_rows[...]) * slope).astype(jnp.bfloat16)
    out_held[...] = dot(mid.astype(jnp.bfloat16), branch_rows[...]).astype(jnp.bfloat16)
    in_held[...] = dot(d_hidden, act_rows[...]).astype(jnp.bfloat16).T
    store_halves(out_held, at[1] & 1, out_held.shape[0] // share // 2, share, out_send, out_keep)
    store_halves(in_held, (at[1] >> 1) & 1, in_held.shape[0] // in_share // 2, in_share, in_send, in_keep)


def grads_of_both(place, acts, branches, w_in, w_out, groups, dep):
    tokens, model = acts[0].shape
    parts = len(acts)
    frames = parts * tokens
    inner = w_in.shape[1] // parts
    width, count = LANES, 4
    if w_in.shape[1] // groups // parts == width:
        source_in, at_in = w_in, lambda g, at: (0, g * parts + at[0])
        source_out, at_out = w_out, lambda g, at: (g * parts + at[0], 0)
    else:
        source_in, at_in = take_columns(w_in, groups, place[0], parts), lambda g, at: (0, g)
        source_out, at_out = take_rows(w_out, groups, place[0], parts), lambda g, at: (g, 0)
    step = count * width
    return pl.pallas_call(
        functools.partial(both_kernel, count, inner // groups, 2 * model // groups),
        grid_spec=pltpu.PrefetchScalarGridSpec(
            num_scalar_prefetch=1,
            grid=(inner // step,),
            in_specs=[whole((tokens, model))] * (2 * parts)
            + [pl.BlockSpec((model, width), lambda i, at, k=k: at_in(i * count + k, at)) for k in range(count)]
            + [pl.BlockSpec((width, model), lambda i, at, k=k: at_out(i * count + k, at)) for k in range(count)]
            + [pl.BlockSpec(memory_space=pl.ANY)],
            out_specs=[pl.BlockSpec((step // 2, model), lambda i, at: (i, 0))] * 2
            + [pl.BlockSpec((model // 2, step), lambda i, at: (0, i))] * 2,
            scratch_shapes=[pltpu.VMEM((frames, model), jnp.bfloat16)] * 2
            + [pltpu.VMEM((step, model), jnp.bfloat16), pltpu.VMEM((model, step), jnp.bfloat16)],
        ),
        out_shape=[pltpu.HBM((inner // 2, model), jnp.bfloat16)] * 2
        + [pltpu.HBM((model // 2, inner), jnp.bfloat16)] * 2,
        compiler_params=pltpu.CompilerParams(vmem_limit_bytes=56 * MIB),
        cost_estimate=cost(8 * frames * model * inner, 2 * frames * inner, 4 * frames * model + 8 * model * inner),
        name="grads_of_both",
    )(place, *[in_hbm(p) for p in (*acts, *branches)], *([in_hbm(source_in)] * count), *([in_hbm(source_out)] * count), in_hbm(dep))


def shards(
    features,
    lengths,
    buckets,
    gain_first,
    first_in,
    first_out,
    gain_attend,
    query_weight,
    key_weight,
    value_weight,
    output_weight,
    bias_table,
    gain_conv,
    point_in,
    depth_weight,
    batch_scale,
    batch_shift,
    point_out,
    gain_second,
    second_in,
    second_out,
    gain_final,
    cotangent,
):
    RECEIVED.clear()
    row_count, width, model = features.shape
    tokens = row_count * width
    heads, bucket_count = bias_table.shape
    head_dim = model // heads
    parts = lax.axis_size("tm")
    groups = lax.axis_size("rows")
    frames = width * parts
    half = depth_weight.shape[0] // 2
    taps = depth_weight.shape[0]
    place = lax.axis_index("tm")
    row_place = lax.axis_index("rows")
    side = place % 2
    far = place // 2
    offset = place * width
    near_heads = heads // 2
    pair = 2 * width
    places = jnp.stack([place, row_place]).astype(jnp.int32)
    info = jnp.stack([side, far, offset, lengths[0], row_place]).astype(jnp.int32)

    flat_features = features.reshape(tokens, model)
    after_first, act_first, slope_first, act_attend = first_forward(
        flat_features, gain_first, gain_attend, first_in, first_out
    )
    act_near, act_far = swap(act_attend, "tm", 1), swap(act_attend, "tm", 2)

    near_table = lax.dynamic_slice_in_dim(bias_table, side * near_heads, near_heads, 0)
    span = pair + frames
    turned = jnp.pad(buckets[::-1], (0, 1), constant_values=-1)
    window = lax.dynamic_slice_in_dim(turned, far * pair, span, 0)
    one_hot = (window[:, None] == jnp.arange(bucket_count)[None, :]).astype(jnp.float32)
    bias_lines = lax.dot_general(
        near_table, one_hot, (((1,), (1,)), ((), ())), precision=lax.Precision.HIGHEST
    )
    bias = skewed(bias_lines[:, None, :])
    key_blocks = frames // LANES
    block = jnp.arange(key_blocks)
    block = (block + far * (key_blocks // 2)) % key_blocks
    at = jnp.concatenate([frames - LANES - LANES * block, LANES * block, lengths[:1], side[None]]).astype(jnp.int32)

    query, key, value = project(info, act_attend, act_near, (query_weight, key_weight, value_weight))
    act_far, act_first, key, bias = tie(act_far, act_first, key, bias)
    act_cross = swap(act_far, "tm", 1)
    act_first_near, act_first_far = swap(act_first, "tm", 1), swap(act_first, "tm", 2)
    key_far, value_far = project(info, act_far, act_cross, (key_weight, value_weight))
    own_mixed, other_mixed, lse = attend(
        at, query, key, key_far, value, value_far, bias, near_heads, head_dim
    )
    other_mixed = swap(other_mixed, "tm", 1)

    attended, after_attend, act_conv, joined_value, gate, gated, gated_first, gated_last = mix(
        info, own_mixed, other_mixed, output_weight, after_first, gain_conv, point_in, half, act_first_far
    )
    act_first_all = [act_first, act_first_near, act_first_far, swap(act_first_far, "tm", 1)]
    up = [(i, i + 1) for i in range(parts - 1)]
    down = [(j, i) for i, j in up]
    gated_before = lax.ppermute(gated_last, "tm", up)
    gated_after = lax.ppermute(gated_first, "tm", down)
    filtered, moments = filter_frames(info, gated, gated_before, gated_after, depth_weight)
    local_count = jnp.clip(lengths[0] - offset, 0, width).astype(jnp.float32)
    count, batch_mean, spread = mesh_moments(local_count, moments[0], moments[1])
    count = count[0]
    rstd_batch = lax.rsqrt(spread / count + EPS)
    stats = jnp.stack([batch_mean, rstd_batch, batch_scale, batch_shift])
    (
        act_batch, act_second, output, branch_second, grad, d_branch_send, d_branch, d_normal, second_sums,
        batch_sums, edge_first, edge_last,
    ) = second_both(
        info, filtered, stats, after_attend, cotangent.reshape(tokens, model),
        gain_second, gain_final, point_out, second_in, second_out, half, (act_first_all[3],),
    )
    output = output.reshape(row_count, width, model)

    edge_before = lax.ppermute(edge_last, "tm", up)
    edge_after = lax.ppermute(edge_first, "tm", down)
    first_step = batch_sums + swap(batch_sums, *hops()[0])
    first_step, act_second, branch_second = tie(first_step, act_second, branch_second)
    act_second_all = spread_tm(act_second)
    branch_second_far = swap(branch_second, "tm", 2)
    branch_second_near = swap(branch_second, "tm", 1)
    batch_grads = mesh_sum(first_step, hops()[1:])
    joined_send, d_joined, grad, d_attend, conv_small = conv_back(
        info, d_normal, filtered, edge_before, edge_after, stats, batch_grads / count, depth_weight,
        gated, joined_value, gate, point_in, after_attend, gain_conv, grad,
        (act_second_all[2],),
    )
    d_attend_near = swap(d_attend, "tm", 1)

    held = near_heads * head_dim
    share = model // groups
    conv_send, conv_keep = cross_grads(
        info,
        [
            ((act_conv, swap(act_conv, "tm", 1)), (d_joined, swap(joined_send, "tm", 1)), model),
            ((act_batch, swap(act_batch, "tm", 1)), (d_branch, swap(d_branch_send, "tm", 1)), held),
            ((attended, swap(attended, "tm", 1)), (d_attend, d_attend_near), held),
        ],
        deps=(branch_second_near, act_second_all[1], act_second_all[3]),
    )

    branch_second_far, conv_send = tie(branch_second_far, conv_send)
    conv_got = swap(conv_send, "tm", 2)
    branch_second_all = [
        branch_second, branch_second_near, branch_second_far, swap(branch_second_far, "tm", 1)
    ]
    out_send, out_keep, in_send, in_keep = grads_of_both(
        places, act_second_all, branch_second_all, second_in, second_out, groups, conv_keep
    )
    d_attend_near, in_keep = tie(d_attend_near, in_keep)
    second_sums_of = [RowSum(out_send, out_keep, share), RowSum(in_send, in_keep, share, True)]

    d_query, d_key, d_value, skew_lines, far_send, far_keep = attend_back(
        at, query, key, key_far, value, value_far, d_attend, d_attend_near,
        (output_weight, key_weight, value_weight), lse, bias, near_heads, head_dim,
    )
    far_mine = add(info, (far_keep, swap(far_send, "tm", 1)), jnp.bfloat16, second_sums_of[0].terms[1],
                   second_sums_of[1].terms[1])
    far_back = swap(far_mine, "tm", 2)
    conv_sum = opened(info, conv_keep, conv_got, share, far_mine)
    kept = merge(info, second_sums_of, conv_sum.terms[0])
    pair_send, pair_keep = input_back(
        info, (d_query, d_key, d_value), (0, 0, 0), (query_weight, key_weight, value_weight), width, (kept,)
    )
    attend_sum = RowSum(*cross_grads(
        info,
        [
            ((act_attend, act_near), (d_query,), held),
            ((act_attend, act_near, act_far, act_cross), (d_key,), held),
            ((act_attend, act_near, act_far, act_cross), (d_value,), held),
        ],
        split=False,
        deps=(pair_keep,),
    ), share)
    grad, branch_first, grad_gain_attend = branch_of(
        info, pair_keep, swap(pair_send, "tm", 1), far_back, after_first, gain_attend, grad,
        (attend_sum.terms[0], conv_sum.terms[1], second_sums_of[0].terms[1]),
    )
    branch_far = swap(branch_first, "tm", 2)
    grad_features, grad_gain_first = first_backward(
        info, grad, flat_features, gain_first, slope_first, first_in, first_out, ()
    )
    grad_features = grad_features.reshape(row_count, width, model)
    mid_first, slope_first_part = again(places, act_first_all, first_in, groups, grad_gain_first)
    kept = merge(info, [*second_sums_of, conv_sum], mid_first)
    branch_far, conv_sum.terms[0] = tie(branch_far, kept)
    branch_first_all = [branch_first, swap(branch_first, "tm", 1), branch_far, swap(branch_far, "tm", 1)]
    first_out_sum = RowSum(
        *grad_out_of(places, mid_first, branch_first_all, share, conv_sum.terms[0]), share
    )
    late_sums = [conv_sum, attend_sum]
    kept = merge(info, late_sums, first_out_sum.terms[0], *[t.terms[1] for t in second_sums_of])
    second_piece = joined(info, second_sums_of, kept)
    second_pieces = spread_tm(second_piece)
    kept = second_piece
    table_lines = sum(jnp.pad(skew_lines[:, r], ((0, 0), (7 - r, 0)))[:, :span] for r in range(8))
    near_grad = lax.dot_general(
        table_lines, one_hot, (((1,), (0,)), ((), ())), precision=lax.Precision.HIGHEST
    )
    grad_table = lax.dynamic_update_slice_in_dim(
        jnp.zeros((heads, bucket_count), jnp.float32), near_grad, side * near_heads, 0
    )
    small = jnp.concatenate(
        [
            grad_gain_first,
            grad_gain_attend,
            second_sums,
            conv_small,
            jnp.pad(grad_table.reshape(1, -1), ((0, 0), (0, model - heads * bucket_count))),
        ],
        axis=0,
    )
    first_in_sum = RowSum(*grad_in_of(
        places, slope_first_part, act_first_all, branch_first_all, first_out, groups, share, kept,
    ), share)

    def hop(step, value, kept):
        value = value + swap(value, *step)
        return tie(value, kept)

    steps = hops()
    kept = merge(info, [first_out_sum, attend_sum], first_in_sum.terms[0])
    conv_piece = joined(info, [conv_sum], kept)
    conv_pieces = spread_tm(conv_piece)
    small, first_in_sum.terms[0] = hop(steps[0], small, first_in_sum.terms[0])
    kept = merge(info, [first_in_sum], conv_piece)
    kept = merge(info, [first_out_sum], kept)
    small, first_out_sum.terms[0] = hop(steps[1], small, kept)
    for step in steps[2:-1]:
        small, first_out_sum.terms[0] = hop(step, small, first_out_sum.terms[0])
    kept = merge(info, [first_in_sum], first_out_sum.terms[0])
    attend_piece = joined(info, [attend_sum], kept)
    attend_got = swap(attend_piece, "tm", 2)
    first_out_piece = joined(info, [first_out_sum], attend_piece)
    first_out_pieces = spread_tm(first_out_piece)
    attend_piece = join(info, [[attend_piece, attend_got]], first_out_piece)
    small, attend_piece = hop(steps[-1], small, attend_piece)
    attend_pieces = [attend_piece, swap(attend_piece, "tm", 1)]
    gains = lax.dynamic_slice_in_dim(small[:5], row_place * share, share, 1)
    grad_depth = small[5 : 5 + taps]
    grad_table = small[5 + taps, : heads * bucket_count].reshape(heads, bucket_count)

    relative = jnp.arange(parts) ^ place
    crossed = (relative % 2) * 2 + relative // 2
    quarter = model // parts

    def lay_rows(pieces):
        size = pieces[0].shape[0]
        out = jnp.zeros((parts, size, model), jnp.float32)
        for k in range(parts):
            out = lax.dynamic_update_index_in_dim(out, pieces[k].astype(jnp.float32), place ^ k, 0)
        return out.reshape(parts * size, model)

    (grad_second_in,) = lay_columns([p[:, model:] for p in second_pieces], (model,), groups, relative)
    grad_second_out = lay_rows([p[:, :model] for p in second_pieces])
    grad_point_in, grad_point_out, grad_output = lay_columns(
        conv_pieces, (2 * quarter, quarter, quarter), 1, crossed
    )
    grad_query, grad_key, grad_value = lay_columns(
        attend_pieces, (2 * quarter,) * 3, 1, jnp.stack([side, 1 - side])
    )
    first_in_pieces = spread_tm(
        joined(info, [first_in_sum], grad_second_in, grad_second_out, grad_point_out, grad_query)
    )
    grad_first_out = lay_rows(first_out_pieces)
    (grad_first_in,) = lay_columns(first_in_pieces, (model,), groups, relative)
    return (
        output,
        grad_features,
        gains[0],
        grad_first_in,
        grad_first_out,
        gains[1],
        grad_query,
        grad_key,
        grad_value,
        grad_output,
        grad_table,
        gains[4],
        grad_point_in,
        grad_depth,
        batch_grads[1],
        batch_grads[0],
        grad_point_out,
        gains[3],
        grad_second_in,
        grad_second_out,
        gains[2],
    )


def solution(mesh):
    rows3, rows2, rows1 = P("rows", "tm", None), P("rows", None), P("rows")
    in_specs = (rows3, rows1) + (P(),) * 20 + (rows3,)
    out_specs = (
        rows3, rows3, rows1, rows2, rows2, rows1, rows2, rows2, rows2, rows2, P(),
        rows1, rows2, P(), P(), P(), rows2, rows1, rows2, rows2, rows1,
    )
    return jax.shard_map(shards, mesh=mesh, in_specs=in_specs, out_specs=out_specs, check_vma=False)
```

```python
import functools

import jax
import jax.numpy as jnp
from jax import lax
from jax.experimental import pallas as pl
from jax.experimental.pallas import tpu as pltpu
from jax.sharding import PartitionSpec as P

EPS = 1e-05
NEGATIVE = -1e30
LANES = 128
LOG2E = 1.4426950408889634
MIB = 1024 * 1024
BLOCK = 1024
EFFORT = 0.0005


RECEIVED = []


def swap(value, axis, bit):
    count = lax.axis_size(axis)
    got = lax.ppermute(value, axis, [(i, i ^ bit) for i in range(count)])
    RECEIVED.append(got)
    return got


def is_received(value):
    return any(value is got for got in RECEIVED)


def hops():
    wide, deep = lax.axis_size("tm"), lax.axis_size("rows")
    found = [("tm", 1 << b) for b in range(wide.bit_length() - 1)][::-1]
    return found + [("rows", 1 << b) for b in range(deep.bit_length() - 1)]


def mesh_sum(value, steps):
    for axis, bit in steps:
        value = value + swap(value, axis, bit)
    return value


def mesh_moments(count, mean, spread):
    for axis, bit in hops():
        sent = jnp.concatenate([mean[None], spread[None], jnp.broadcast_to(count, (1, mean.shape[0]))])
        got = swap(sent, axis, bit)
        other_mean, other_spread, other_count = got[0], got[1], got[2]
        total = count + other_count
        safe = jnp.maximum(total, 1.0)
        gap = other_mean - mean
        spread = spread + other_spread + gap * gap * (count * other_count / safe)
        mean = (count * mean + other_count * other_mean) / safe
        count = total
    return (count, mean, spread)


def tie(*values):
    out = lax.optimization_barrier(values)
    RECEIVED.extend(b for a, b in zip(values, out, strict=True) if is_received(a))
    return out


def spread_tm(piece):
    far = swap(piece, "tm", 2)
    return [piece, swap(piece, "tm", 1), far, swap(far, "tm", 1)]


def silu_pair(hidden):
    sigma = 0.5 * jnp.tanh(0.5 * hidden) + 0.5
    act = hidden * sigma
    return (act, sigma + act * (1.0 - sigma))


def normed_of(values, gain):
    mean = jnp.mean(values, axis=-1, keepdims=True)
    centered = values - mean
    rstd = lax.rsqrt(jnp.mean(centered * centered, axis=-1, keepdims=True) + EPS)
    scaled = centered * rstd
    return (scaled * gain, scaled, rstd)


def normed_back(grad, values, gain):
    _, scaled, rstd = normed_of(values, gain)
    weighted = grad * gain
    inner = weighted - jnp.mean(weighted, axis=-1, keepdims=True)
    inner = inner - scaled * jnp.mean(weighted * scaled, axis=-1, keepdims=True)
    return (rstd * inner, jnp.sum(grad * scaled, axis=0, keepdims=True))


def dot(left, right):
    return jnp.dot(left, right, preferred_element_type=jnp.float32)


def dot_turned(left, right):
    return lax.dot_general(left, right, (((1,), (1,)), ((), ())), preferred_element_type=jnp.float32)


def scalars():
    return [pl.BlockSpec(memory_space=pltpu.SMEM)]


def in_hbm(value):
    if is_received(value):
        return value
    return pltpu.with_memory_space_constraint(value, pltpu.HBM)


def struct(*shape, kind=jnp.bfloat16):
    return jax.ShapeDtypeStruct(shape, kind)


class Arriving:
    def __init__(self, source, target, sem):
        self.copy = pltpu.make_async_copy(source, target, sem)
        self.target = target
        self.started = self.here = False

    def start(self):
        if not self.started:
            self.copy.start()
            self.started = True

    def get(self):
        self.start()
        if not self.here:
            self.copy.wait()
            self.here = True
        return self.target


class Leaving:
    def __init__(self, source, target, sem):
        self.ref = source
        self.target, self.sem = target, sem
        self.copy = None

    def send(self, source=None):
        self.copy = pltpu.make_async_copy(self.ref if source is None else source, self.target, self.sem)
        self.copy.start()


def flow_call(body, name, outs, scratch, info, operands, flops, mib=24, raw=(), late=(), deps=()):
    ins, results = len(operands), len(outs)

    def kernel(info, *refs):
        sources, targets = refs[:ins], refs[ins + len(deps) : ins + len(deps) + results]
        rest = refs[ins + len(deps) + results :]
        held, made = rest[:ins], rest[ins : ins + results]
        extra, sem_in, sem_out = rest[ins + results : -2], rest[-2], rest[-1]
        arriving = [
            (sources[k], held[k]) if k in raw else Arriving(sources[k], held[k], sem_in.at[k])
            for k in range(ins)
        ]
        for k in range(ins):
            if k not in raw and k not in late:
                arriving[k].start()
        leaving = [Leaving(made[k], targets[k], sem_out.at[k]) for k in range(results)]
        body(info, arriving, leaving, *extra)
        for item in leaving:
            if item.copy is None:
                item.send()
        for k in range(ins):
            if k not in raw:
                arriving[k].get()
        for item in leaving:
            item.copy.wait()

    moved = sum(o.size * o.dtype.itemsize for o in (*operands, *outs))
    return pl.pallas_call(
        kernel,
        in_specs=scalars() + [pl.BlockSpec(memory_space=pl.ANY)] * (ins + len(deps)),
        out_specs=[pl.BlockSpec(memory_space=pltpu.HBM)] * results,
        out_shape=[pltpu.HBM(o.shape, o.dtype) for o in outs],
        scratch_shapes=[pltpu.VMEM(o.shape, o.dtype) for o in (*operands, *outs)]
        + list(scratch)
        + [pltpu.SemaphoreType.DMA((ins,)), pltpu.SemaphoreType.DMA((results,))],
        compiler_params=pltpu.CompilerParams(vmem_limit_bytes=mib * MIB),
        cost_estimate=cost(flops, 0, moved),
        name=name,
    )(info, *[in_hbm(o) for o in (*operands, *deps)])


def cost(flops, transcendentals, moved):
    return pl.CostEstimate(
        flops=int(flops * EFFORT), transcendentals=int(transcendentals * EFFORT), bytes_accessed=int(moved * EFFORT)
    )


SIDE, FAR, OFFSET, LENGTH, ROW = range(5)


def row_bits():
    return lax.axis_size("rows").bit_length() - 1


def take_half(source, index, lead, size, ways=2):
    return [
        source[pl.ds(pl.multiple_of((k * ways + index) * size, size), size)] for k in range(lead)
    ]


def phases(share, far_first):
    bits = list(range(row_bits()))
    if far_first:
        return [(bit, 2 * share) for bit in bits[1:]] + [(0, share)]
    return [(bit, share) for bit in bits]


def total_of(parts):
    total = parts[0].astype(jnp.float32)
    for part in parts[1:]:
        total = total + part.astype(jnp.float32)
    return total.astype(jnp.bfloat16)


def merge_kernel(plan, info, ins, outs):
    at = 0
    for g, (count, bit, chunk) in enumerate(plan):
        held = [item.get() for item in ins[at : at + count]]
        at += count
        mine = (info[ROW] >> bit) & 1
        lead = held[0].shape[0] // chunk // 2
        for index, out in ((1 - mine, outs[2 * g]), (mine, outs[2 * g + 1])):
            parts = [take_half(h, index, lead, chunk) for h in held]
            for k in range(lead):
                out.ref[k * chunk : (k + 1) * chunk] = total_of([p[k] for p in parts])
            out.send()


def join_kernel(counts, info, ins, outs):
    begin = at = 0
    for count in counts:
        held = [item.get()[...] for item in ins[at : at + count]]
        at += count
        width = held[0].shape[1]
        outs[0].ref[:, begin : begin + width] = total_of(held)
        begin += width


class RowSum:
    def __init__(self, send, keep, share, far_first=False):
        self.left = phases(share, far_first)
        self.exchange(send, keep)

    def exchange(self, send, keep):
        bit, _ = self.left.pop(0)
        self.terms = [keep, swap(send, "rows", 1 << bit)]


def merge(info, sums, *deps):
    outs = []
    for total in sums:
        rows, columns = total.terms[0].shape
        outs += [struct(rows // 2, columns)] * 2
    plan = [(len(t.terms), *t.left[0]) for t in sums]
    made = flow_call(
        functools.partial(merge_kernel, plan), "merge",
        outs, [], info, tuple(x for t in sums for x in t.terms), 0, deps=deps,
    )
    for k, total in enumerate(sums):
        total.exchange(made[2 * k], made[2 * k + 1])
    return sums[-1].terms[0]


def joined(info, sums, *deps):
    while any(t.left for t in sums):
        merge(info, [t for t in sums if t.left])
    return join(info, [t.terms for t in sums], *deps)


def join(info, groups, *deps):
    columns = sum(g[0].shape[1] for g in groups)
    return flow_call(
        functools.partial(join_kernel, [len(g) for g in groups]), "join",
        [struct(groups[0][0].shape[0], columns)], [], info, tuple(x for g in groups for x in g), 0, deps=deps,
    )[0]


def opened(info, keep, got, share, *deps):
    rows, columns = keep.shape
    return RowSum(
        *flow_call(
            functools.partial(merge_kernel, [(2, 0, share)]), "merge",
            [struct(rows // 2, columns)] * 2, [], info, (keep, got), 0, deps=deps,
        ),
        share,
    )


def project_kernel(info, ins, outs, sem, rows):
    mine, other, *weights = ins
    side = info[SIDE]
    half = outs[0].ref.shape[1]
    lanes = pl.ds(pl.multiple_of(side * half, half), half)
    copies = [
        pltpu.make_async_copy(source.at[:, lanes], held.at[:, :half], sem.at[k])
        for k, (source, held) in enumerate(weights)
    ]
    for copy in copies:
        copy.start()
    tokens = mine.target.shape[0]
    rows[pl.ds(pl.multiple_of(side * tokens, tokens), tokens)] = mine.get()[...]
    rows[pl.ds(pl.multiple_of((1 - side) * tokens, tokens), tokens)] = other.get()[...]
    for copy, (_, held), out in zip(copies, weights, outs, strict=True):
        copy.wait()
        out.ref[...] = dot(rows[...], held[:, :half]).astype(jnp.bfloat16)
        out.send()


def project(info, mine, other, weights, deps=()):
    tokens, model = mine.shape
    pair = 2 * tokens
    return flow_call(
        project_kernel, "project",
        [struct(pair, model // 2)] * len(weights),
        [pltpu.SemaphoreType.DMA((len(weights),)), pltpu.VMEM((pair, model), jnp.bfloat16)],
        info, (mine, other, *weights), pair * model * model * len(weights),
        raw=tuple(range(2, 2 + len(weights))),
        deps=deps,
    )


def rows_of(length, first, count):
    frame = lax.broadcasted_iota(jnp.int32, (count, 1), 0) + first
    return ((frame >= 0) & (frame < length)).astype(jnp.float32)


def mix_kernel(
    info, own_ref, other_ref, weight, state_ref, gain_ref, value_w, gate_w, dep,
    attended_ref, after_ref, act_ref, value_ref, gate_ref, gated_ref, first_ref, last_ref,
):
    side = info[SIDE]
    tokens, half = own_ref.shape

    @pl.when(pl.program_id(0) == 0)
    def _():
        attended_ref[:, pl.ds(pl.multiple_of(side * half, half), half)] = own_ref[...]
        attended_ref[:, pl.ds(pl.multiple_of((1 - side) * half, half), half)] = other_ref[...]
        values = state_ref[...] + dot(attended_ref[...], weight[...])
        after_ref[...] = values
        act_ref[...] = normed_of(values, gain_ref[...])[0].astype(jnp.bfloat16)

    value = dot(act_ref[...], value_w[...])
    gate = 0.5 * jnp.tanh(0.5 * dot(act_ref[...], gate_w[...])) + 0.5
    value_ref[...] = value.astype(jnp.bfloat16)
    gate_ref[...] = gate.astype(jnp.bfloat16)
    gated_ref[...] = value * gate * rows_of(info[LENGTH], info[OFFSET], tokens)
    half = first_ref.shape[0]
    first_ref[...] = gated_ref[:half].astype(jnp.bfloat16)
    last_ref[...] = gated_ref[tokens - half :].astype(jnp.bfloat16)


def mix(info, own, other, weight, state, gain, point_in, half, dep):
    tokens, model = state.shape
    step = 512
    steps = model // step
    flat = (tokens, model)
    column = pl.BlockSpec((tokens, step), lambda i: (0, i))
    return pl.pallas_call(
        mix_kernel,
        grid=(steps,),
        in_specs=scalars() + [
            whole(own.shape), whole(own.shape), whole(weight.shape), whole(flat), whole((1, model)),
            pl.BlockSpec((model, step), lambda i: (0, i)),
            pl.BlockSpec((model, step), lambda i: (0, steps + i)),
            pl.BlockSpec(memory_space=pl.ANY),
        ],
        out_specs=[whole(flat)] * 3 + [column] * 3 + [pl.BlockSpec((half, step), lambda i: (0, i))] * 2,
        out_shape=[
            pltpu.HBM(flat, jnp.bfloat16), pltpu.HBM(flat, jnp.float32), pltpu.HBM(flat, jnp.bfloat16),
            pltpu.HBM(flat, jnp.bfloat16), pltpu.HBM(flat, jnp.bfloat16), pltpu.HBM(flat, jnp.float32),
            struct(half, model), struct(half, model),
        ],
        compiler_params=pltpu.CompilerParams(vmem_limit_bytes=32 * MIB),
        cost_estimate=cost(
            6 * tokens * model * model,
            tokens * model,
            6 * model * model + 20 * tokens * model,
        ),
        name="mix",
    )(info, in_hbm(own), other, weight, state, gain[None], point_in, point_in, in_hbm(dep))


def filter_kernel(info, ins, outs, wide):
    gated_ref, before_ref, after_ref, taps_ref = [item.get() for item in ins]
    filtered_ref, moments_ref = [item.ref for item in outs]
    tokens = gated_ref.shape[0]
    half = before_ref.shape[0]
    wide[8 : 8 + tokens] = gated_ref[...]
    wide[8 - half : 8] = before_ref[...].astype(jnp.float32)
    wide[8 + tokens : 8 + tokens + half] = after_ref[...].astype(jnp.float32)
    filtered = taps_ref[0:1] * wide[8 - half : 8 - half + tokens]
    for tap in range(1, taps_ref.shape[0]):
        filtered = filtered + taps_ref[tap : tap + 1] * wide[8 - half + tap : 8 - half + tap + tokens]
    filtered_ref[...] = filtered
    outs[0].send()
    valid = rows_of(info[LENGTH], info[OFFSET], tokens)
    count = jnp.clip(info[LENGTH] - info[OFFSET], 1, tokens).astype(jnp.float32)
    mean = jnp.sum(filtered * valid, axis=0, keepdims=True) / count
    gap = (filtered - mean) * valid
    moments_ref[0:1] = mean
    moments_ref[1:2] = jnp.sum(gap * gap, axis=0, keepdims=True)


def filter_frames(info, gated, before, later, depth):
    tokens, model = gated.shape
    return flow_call(
        filter_kernel, "filter_frames",
        [struct(tokens, model, kind=jnp.float32), struct(2, model, kind=jnp.float32)],
        [pltpu.VMEM((tokens + 16, model), jnp.float32)],
        info, (gated, before, later, depth), 10 * tokens * model,
    )


def weight_copies(pair_in, pair_out, sem, block):
    def at(i):
        lanes = pl.ds(pl.multiple_of(i * block, block), block)
        return (
            pltpu.make_async_copy(pair_in[0].at[:, lanes], pair_in[1].at[:, lanes], sem.at[0, i]),
            pltpu.make_async_copy(pair_out[0].at[lanes, :], pair_out[1].at[lanes, :], sem.at[1, i]),
        )

    return at


def second_kernel(info, ins, outs, sem, state, grad, total, slopes, low_ref):
    filtered, stats, state_in, cot, gain, final_gain, point, pair_in, pair_out = ins
    w_in, w_out = pair_in[1], pair_out[1]
    act_batch, act_out, output, branch_out, grad_out, conv_send, conv_keep, d_norm_out, sums, batch_sums, edge_first, edge_last = outs
    tokens = filtered.target.shape[0]
    steps = w_in.shape[1] // BLOCK
    valid = rows_of(info[LENGTH], info[OFFSET], tokens)
    copies = weight_copies(pair_in, pair_out, sem, BLOCK)
    filtered_ref, stats_ref = filtered.get(), stats.get()

    def normalized():
        scaled = (filtered_ref[...] - stats_ref[0:1]) * stats_ref[1:2]
        return (scaled, scaled * stats_ref[2:3] + stats_ref[3:4])

    act = silu_pair(normalized()[1])[0].astype(jnp.bfloat16)
    act_batch.ref[...] = act
    point_ref = point.get()
    for i in range(2):
        for copy in copies(i):
            copy.start()
    act_batch.send()
    values = state_in.get()[...] + dot(act, point_ref[...])
    state[...] = values
    act_ref = act_out.ref
    act_ref[...] = normed_of(values, gain.get()[...])[0].astype(jnp.bfloat16)
    act_out.send()
    cot.start()
    total[...] = jnp.zeros_like(total)

    def forward(i, carry):
        lanes = pl.ds(pl.multiple_of(i * BLOCK, BLOCK), BLOCK)
        for copy in copies(i):
            copy.wait()

        @pl.when(i + 2 < steps)
        def _():
            for copy in copies(i + 2):
                copy.start()

        mid, slope = silu_pair(dot(act_ref[...], w_in[:, lanes]))
        slopes[:, lanes] = slope.astype(jnp.bfloat16)
        total[...] += dot(mid.astype(jnp.bfloat16), w_out[lanes, :])
        return carry

    lax.fori_loop(0, steps, forward, 0)
    values = state[...] + 0.5 * total[...]
    final = final_gain.get()[...]
    normed, _, _ = normed_of(values, final)
    output.ref[...] = (normed * valid).astype(jnp.bfloat16)
    output.send()
    begin, sums.ref[0:1] = normed_back(cot.get()[...].astype(jnp.float32) * valid, values, final)
    grad[...] = begin
    branch_ref = branch_out.ref
    branch_ref[...] = (0.5 * begin).astype(jnp.bfloat16)
    branch_out.send()
    total[...] = jnp.zeros_like(total)

    def backward(i, carry):
        lanes = pl.ds(pl.multiple_of(i * BLOCK, BLOCK), BLOCK)
        part = dot_turned(branch_ref[...], w_out[lanes, :])
        part = (part * slopes[:, lanes].astype(jnp.float32)).astype(jnp.bfloat16)
        total[...] += dot_turned(part, w_in[:, lanes])
        return carry

    lax.fori_loop(0, steps, backward, 0)
    d_values, sums.ref[1:2] = normed_back(total[...], state[...], gain.get()[...])
    later = grad[...] + d_values
    grad_out.ref[...] = later
    grad_out.send()
    low = later.astype(jnp.bfloat16)
    low_ref[...] = low
    side = info[SIDE]
    half = low.shape[1] // 2
    conv_send.send(low_ref.at[:, pl.ds(pl.multiple_of((1 - side) * half, half), half)])
    conv_keep.send(low_ref.at[:, pl.ds(pl.multiple_of(side * half, half), half)])
    scaled, normal = normalized()
    d_norm = dot_turned(low, point.get()[...]) * silu_pair(normal)[1] * valid
    d_norm_out.ref[...] = d_norm
    d_norm_out.send()
    batch_sums.ref[0:1] = jnp.sum(d_norm, axis=0, keepdims=True)
    batch_sums.ref[1:2] = jnp.sum(d_norm * scaled, axis=0, keepdims=True)
    half = edge_first.ref.shape[0] // 2
    for edge, rows in ((edge_first, slice(0, half)), (edge_last, slice(tokens - half, tokens))):
        edge.ref[:half] = d_norm_out.ref[rows]
        edge.ref[half:] = filtered_ref[rows]


def second_both(info, filtered, stats, state, cotangent, gain, final_gain, point_out, w_in, w_out, half, deps):
    tokens, model = state.shape
    inner = w_in.shape[1]
    flat = (tokens, model)
    low, high = struct(*flat), struct(*flat, kind=jnp.float32)
    return flow_call(
        second_kernel, "second_both",
        [low, low, low, low, high, struct(tokens, model // 2), struct(tokens, model // 2), high,
         struct(2, model, kind=jnp.float32), struct(2, model, kind=jnp.float32),
         struct(2 * half, model, kind=jnp.float32), struct(2 * half, model, kind=jnp.float32)],
        [
            pltpu.SemaphoreType.DMA((2, inner // BLOCK)),
            pltpu.VMEM(flat, jnp.float32), pltpu.VMEM(flat, jnp.float32), pltpu.VMEM(flat, jnp.float32),
            pltpu.VMEM((tokens, inner), jnp.bfloat16), pltpu.VMEM(flat, jnp.bfloat16),
        ],
        info,
        (filtered, stats, state, cotangent, gain[None], final_gain[None], point_out, w_in, w_out),
        8 * tokens * model * inner + 4 * tokens * model * model,
        mib=48,
        raw=(7, 8),
        late=(3,),
        deps=deps,
    )


def conv_back_kernel(info, ins, outs, wide, joined_ref):
    d_norm_ref, filtered_ref, before_ref, after_ref, stats_ref, sums_ref, taps_ref = [i.get() for i in ins[:7]]
    for item in ins[8:11]:
        item.start()
    gated_ref = ins[7].get()
    value, gate, point, state, gain, grad = ins[8:]
    out_ref, low_ref, small_ref = [item.ref for item in outs[2:]]
    tokens, model = d_norm_ref.shape
    half = before_ref.shape[0] // 2

    def d_filtered(d_norm, filtered, first):
        valid = rows_of(info[LENGTH], first, d_norm.shape[0])
        scaled = (filtered - stats_ref[0:1]) * stats_ref[1:2]
        inner = d_norm - sums_ref[0:1] - scaled * sums_ref[1:2]
        return valid * (stats_ref[2:3] * stats_ref[1:2]) * inner

    offset = info[OFFSET]
    wide[8 : 8 + tokens] = d_filtered(d_norm_ref[...], filtered_ref[...], offset)
    wide[8 - half : 8] = d_filtered(before_ref[:half], before_ref[half:], offset - half)
    wide[8 + tokens : 8 + tokens + half] = d_filtered(after_ref[:half], after_ref[half:], offset + tokens)
    d_gated = jnp.zeros((tokens, model), jnp.float32)
    for tap in range(taps_ref.shape[0]):
        begin = 8 + half - tap
        shifted = wide[begin : begin + tokens]
        d_gated = d_gated + taps_ref[tap : tap + 1] * shifted
        small_ref[1 + tap : 2 + tap] = jnp.sum(shifted * gated_ref[...], axis=0, keepdims=True)
    for item in ins[11:]:
        item.start()
    d_gated = d_gated * rows_of(info[LENGTH], offset, tokens)
    gate = gate.get()[...].astype(jnp.float32)
    d_value = d_gated * gate
    joined_ref[:, :model] = d_value.astype(jnp.bfloat16)
    joined_ref[:, model:] = (d_value * value.get()[...].astype(jnp.float32) * (1.0 - gate)).astype(jnp.bfloat16)
    side = info[SIDE]
    outs[0].send(joined_ref.at[:, pl.ds(pl.multiple_of((1 - side) * model, model), model)])
    outs[1].send(joined_ref.at[:, pl.ds(pl.multiple_of(side * model, model), model)])
    d_values, small_ref[0:1] = normed_back(
        dot_turned(joined_ref[...], point.get()[...]), state.get()[...], gain.get()[...]
    )
    later = grad.get()[...] + d_values
    low_ref[...] = later.astype(jnp.bfloat16)
    outs[3].send()
    out_ref[...] = later


def conv_back(info, d_norm, filtered, before, later, stats, sums, depth, gated,
              value, gate, point_in, state, gain, grad, deps):
    tokens, model = d_norm.shape
    return flow_call(
        conv_back_kernel, "conv_back",
        [
            struct(tokens, model), struct(tokens, model),
            struct(tokens, model, kind=jnp.float32), struct(tokens, model),
            struct(1 + depth.shape[0], model, kind=jnp.float32),
        ],
        [pltpu.VMEM((tokens + 16, model), jnp.float32), pltpu.VMEM((tokens, 2 * model), jnp.bfloat16)],
        info,
        (d_norm, filtered, before, later, stats, sums, depth, gated, value,
         gate, point_in, state, gain[None], grad),
        4 * tokens * model * model,
        mib=32,
        late=tuple(range(8, 14)),
        deps=deps,
    )


def add_kernel(info, ins, outs):
    total = ins[0].get()[...].astype(jnp.float32)
    for item in ins[1:]:
        total = total + item.get()[...].astype(jnp.float32)
    outs[0].ref[...] = total.astype(outs[0].ref.dtype)


def add(info, terms, kind, *deps):
    return flow_call(
        add_kernel, "add", [struct(*terms[0].shape, kind=kind)], [], info, tuple(terms), 0, deps=deps
    )[0]


def branch_kernel(info, ins, outs):
    keep, got, far, state, gain, grad = ins
    d_input = keep.get()[...] + got.get()[...].astype(jnp.float32) + far.get()[...].astype(jnp.float32)
    d_values, outs[2].ref[...] = normed_back(d_input, state.get()[...], gain.get()[...])
    later = grad.get()[...] + d_values
    outs[1].ref[...] = (0.5 * later).astype(jnp.bfloat16)
    outs[1].send()
    outs[0].ref[...] = later


def branch_of(info, keep, got, far, state, gain, grad, deps):
    tokens, model = keep.shape
    return flow_call(
        branch_kernel, "branch",
        [struct(tokens, model, kind=jnp.float32), struct(tokens, model), struct(1, model, kind=jnp.float32)],
        [], info, (keep, got, far, state, gain[None], grad), 0, deps=deps,
    )


def input_back_kernel(count, base, info, ins, outs, sem):
    grads, weights = ins[:count], ins[count:]
    send_ref, keep_ref = outs[0].ref, outs[1].ref
    tokens = send_ref.shape[0]
    side = info[SIDE]
    half = weights[0][0].shape[1] // 2
    lanes = pl.ds(pl.multiple_of(side * half, half), half)
    copies = [
        pltpu.make_async_copy(source.at[:, lanes], held.at[:, :half], sem.at[k])
        for k, (source, held) in enumerate(weights)
    ]
    for copy in copies:
        copy.start()
    grads = [grad.get() for grad in grads]
    for copy in copies:
        copy.wait()

    def total(which):
        out = None
        for first, grad, (_, held) in zip(base, grads, weights, strict=True):
            rows = pl.ds(pl.multiple_of(first + which * tokens, LANES), tokens)
            part = dot_turned(grad[rows], held[:, :half])
            out = part if out is None else out + part
        return out

    send_ref[...] = total(1 - side).astype(jnp.bfloat16)
    outs[0].send()
    keep_ref[...] = total(side)


def input_back(info, grads, base, weights, tokens, deps=()):
    model = weights[0].shape[0]
    count = len(grads)
    return flow_call(
        functools.partial(input_back_kernel, count, base), "input_back",
        [struct(tokens, model), struct(tokens, model, kind=jnp.float32)],
        [pltpu.SemaphoreType.DMA((count,))],
        info, (*grads, *weights), 2 * tokens * model * model * count,
        mib=32, raw=tuple(range(count, 2 * count)), deps=deps,
    )


def cross_kernel(layout, split, lead, chunk, info, refs, outs, left_rows, right_rows, *held):
    far, side = info[FAR], info[SIDE]
    at = 0
    begin = 0
    for pieces, width in layout:
        lefts, right = refs[at : at + pieces], refs[at + pieces : at + pieces + (2 if width < 0 else 1)]
        at += pieces + len(right)
        tokens = lefts[0].target.shape[0]
        for k, left in enumerate(lefts):
            spot = (k // 2 * 2 + (side if k % 2 == 0 else 1 - side)) * tokens
            left_rows[pl.ds(pl.multiple_of(spot, tokens), tokens)] = left.get()[...]
        size = abs(width)
        half = size // 2 if split else size
        if len(right) == 2:
            for k, piece in enumerate(right):
                spot = (side if k == 0 else 1 - side) * tokens
                held = piece.get()
                lanes = pl.ds(0, size)
                if held.shape[1] != size:
                    lanes = pl.ds(pl.multiple_of(side * size, size), size)
                right_rows[pl.ds(pl.multiple_of(spot, tokens), tokens), :size] = held[:, lanes]
            source = right_rows
        else:
            source = right[0].get()
        count = pieces * tokens
        targets = ((1 - far, outs[0].ref), (far, outs[1].ref)) if split else ((0, held[0]),)
        for which, target in targets:
            lanes = pl.ds(pl.multiple_of(which * half, half), half)
            target[:, begin : begin + half] = lax.dot_general(
                left_rows[:count], source[:count, lanes], (((0,), (0,)), ((), ())),
                preferred_element_type=jnp.float32,
            ).astype(jnp.bfloat16)
        begin += half
    if not split:
        store_halves(held[0], info[ROW] & 1, lead, chunk, outs[0].ref, outs[1].ref)


def cross_grads(info, terms, split=True, deps=()):
    operands, layout = [], []
    total = flops = 0
    for lefts, rights, width in terms:
        operands += [*lefts, *rights]
        layout.append((len(lefts), -width if len(rights) == 2 else width))
        total += width // 2 if split else width
        tokens, model = lefts[0].shape
        flops += 2 * len(lefts) * tokens * model * width
    deepest = max(len(lefts) for lefts, *_ in terms) * tokens
    widest = max(width for *_, width in terms)
    size = model >> row_bits()
    rows = model if split else model // 2
    scratch = [pltpu.VMEM((deepest, model), jnp.bfloat16), pltpu.VMEM((deepest, widest), jnp.bfloat16)]
    if not split:
        scratch.append(pltpu.VMEM((model, total), jnp.bfloat16))
    return flow_call(
        functools.partial(cross_kernel, layout, split, model // size // 2, size), "cross_grads",
        [struct(rows, total)] * 2, scratch, info, tuple(operands), flops, mib=40, deps=deps,
    )


def first_back_kernel(info, ins, outs, sem, branch, total):
    grad, x, gain, slope, pair_in, pair_out = ins
    w_in, w_out = pair_in[1], pair_out[1]
    steps = w_in.shape[1] // BLOCK
    copies = weight_copies(pair_in, pair_out, sem, BLOCK)
    for i in range(2):
        for copy in copies(i):
            copy.start()
    grad_ref = grad.get()
    branch[...] = (0.5 * grad_ref[...]).astype(jnp.bfloat16)
    total[...] = jnp.zeros_like(total)
    slope_ref = slope.get()
    x.start()

    def backward(i, carry):
        lanes = pl.ds(pl.multiple_of(i * BLOCK, BLOCK), BLOCK)
        for copy in copies(i):
            copy.wait()

        @pl.when(i + 2 < steps)
        def _():
            for copy in copies(i + 2):
                copy.start()

        part = dot_turned(branch[...], w_out[lanes, :])
        part = (part * slope_ref[:, lanes].astype(jnp.float32)).astype(jnp.bfloat16)
        total[...] += dot_turned(part, w_in[:, lanes])
        return carry

    lax.fori_loop(0, steps, backward, 0)
    d_values, outs[1].ref[...] = normed_back(total[...], x.get()[...].astype(jnp.float32), gain.get()[...])
    outs[0].ref[...] = (grad_ref[...] + d_values).astype(jnp.bfloat16)


def first_backward(info, grad, features, gain, slope, w_in, w_out, deps):
    tokens, model = features.shape
    inner = w_in.shape[1]
    return flow_call(
        first_back_kernel, "first_backward",
        [struct(tokens, model), struct(1, model, kind=jnp.float32)],
        [pltpu.SemaphoreType.DMA((2, inner // BLOCK)), pltpu.VMEM((tokens, model), jnp.bfloat16), pltpu.VMEM((tokens, model), jnp.float32)],
        info, (grad, features, gain[None], slope, w_in, w_out), 4 * tokens * model * inner,
        mib=40, raw=(4, 5), late=(1,), deps=deps,
    )


def norm_backward(grad, scaled, rstd, gain):
    weighted = grad * gain
    inner = weighted - jnp.mean(weighted, axis=-1, keepdims=True)
    inner = inner - scaled * jnp.mean(weighted * scaled, axis=-1, keepdims=True)
    return (rstd * inner, jnp.sum(grad * scaled, axis=0))


def first_kernel(x_ref, gain_ref, next_gain_ref, w_in, w_out, state_ref, act_ref, slope_ref, next_ref, total):
    step = pl.program_id(0)

    @pl.when(step == 0)
    def _():
        values = x_ref[...].astype(jnp.float32)
        act_ref[...] = normed_of(values, gain_ref[...])[0].astype(jnp.bfloat16)
        total[...] = jnp.zeros_like(total)

    mid, slope = silu_pair(dot(act_ref[...], w_in[...]))
    slope_ref[...] = slope.astype(jnp.bfloat16)
    total[...] += dot(mid.astype(jnp.bfloat16), w_out[...])

    @pl.when(step == pl.num_programs(0) - 1)
    def _():
        values = x_ref[...].astype(jnp.float32) + 0.5 * total[...]
        state_ref[...] = values
        next_ref[...] = normed_of(values, next_gain_ref[...])[0].astype(jnp.bfloat16)


def whole(shape):
    return pl.BlockSpec(shape, lambda *_: (0,) * len(shape))


def first_forward(features, gain, next_gain, w_in, w_out):
    tokens, model = features.shape
    inner = w_in.shape[1]
    return pl.pallas_call(
        first_kernel,
        grid=(inner // BLOCK,),
        in_specs=[
            whole((tokens, model)),
            whole((1, model)),
            whole((1, model)),
            pl.BlockSpec((model, BLOCK), lambda i: (0, i)),
            pl.BlockSpec((BLOCK, model), lambda i: (i, 0)),
        ],
        out_specs=[
            whole((tokens, model)),
            whole((tokens, model)),
            pl.BlockSpec((tokens, BLOCK), lambda i: (0, i)),
            whole((tokens, model)),
        ],
        out_shape=[
            pltpu.HBM((tokens, model), jnp.float32),
            pltpu.HBM((tokens, model), jnp.bfloat16),
            pltpu.HBM((tokens, inner), jnp.bfloat16),
            pltpu.HBM((tokens, model), jnp.bfloat16),
        ],
        scratch_shapes=[pltpu.VMEM((tokens, model), jnp.float32)],
        compiler_params=pltpu.CompilerParams(vmem_limit_bytes=40 * MIB),
        cost_estimate=cost(
            4 * tokens * model * inner,
            2 * tokens * inner,
            4 * model * inner + 2 * tokens * inner,
        ),
        name="first_forward",
    )(in_hbm(features), gain[None], next_gain[None], in_hbm(w_in), in_hbm(w_out))


def take_kernel(place, source, target):
    target[...] = source[...]


def take_columns(weight, groups, place, parts):
    model, total = weight.shape
    block = total // groups // parts
    if block % LANES:
        cut = weight.reshape(model, groups, parts, block)
        return lax.dynamic_index_in_dim(cut, place, 2, keepdims=False).reshape(model, -1)
    return pl.pallas_call(
        take_kernel,
        out_shape=jax.ShapeDtypeStruct((model, total // parts), weight.dtype),
        grid_spec=pltpu.PrefetchScalarGridSpec(
            num_scalar_prefetch=1,
            grid=(groups,),
            in_specs=[pl.BlockSpec((model, block), lambda g, at: (0, g * parts + at[0]))],
            out_specs=pl.BlockSpec((model, block), lambda g, at: (0, g)),
        ),
        name="take_columns",
    )(place.reshape(1), weight)


def take_rows(weight, groups, place, parts):
    total, model = weight.shape
    cut = weight.reshape(groups, parts, total // groups // parts, model)
    return lax.dynamic_index_in_dim(cut, place, 1, keepdims=False).reshape(-1, model)


def lay_kernel(parts, widths, groups, places, *refs):
    pieces, targets = refs[:parts], refs[parts:]
    for k in range(parts):
        begin = 0
        for width, target in zip(widths, targets, strict=True):
            block = width // groups
            for g in range(groups):
                at = pl.multiple_of((g * parts + places[k]) * block, LANES)
                source = pieces[k][:, begin + g * block : begin + (g + 1) * block]
                target[:, pl.ds(at, block)] = source.astype(jnp.float32)
            begin += width


def lay_columns(pieces, widths, groups, places):
    rows = pieces[0].shape[0]
    parts = len(pieces)
    if any((width // groups) % LANES for width in widths):
        outs, begin = [], 0
        stacked = jnp.zeros((parts, *pieces[0].shape), pieces[0].dtype)
        for k in range(parts):
            stacked = lax.dynamic_update_index_in_dim(stacked, pieces[k], places[k], 0)
        for width in widths:
            cut = stacked[:, :, begin : begin + width].reshape(parts, rows, groups, width // groups)
            outs.append(cut.transpose(1, 2, 0, 3).reshape(rows, parts * width).astype(jnp.float32))
            begin += width
        return outs
    return pl.pallas_call(
        functools.partial(lay_kernel, parts, widths, groups),
        out_shape=[jax.ShapeDtypeStruct((rows, parts * width), jnp.float32) for width in widths],
        grid_spec=pltpu.PrefetchScalarGridSpec(
            num_scalar_prefetch=1,
            grid=(1,),
            in_specs=[pl.BlockSpec(p.shape, lambda i, at: (0, 0)) for p in pieces],
            out_specs=[pl.BlockSpec((rows, parts * width), lambda i, at: (0, 0)) for width in widths],
        ),
        compiler_params=pltpu.CompilerParams(vmem_limit_bytes=24 * MIB),
        name="lay_columns",
    )(places, *pieces)


def skew_kernel(line, out):
    length = line.shape[-1]
    width = out.shape[-1]
    spread = jnp.broadcast_to(line[0], (LANES, length))
    rolled = pltpu.roll(spread, length - (LANES - 1), 1, stride=1, stride_axis=0)
    out[0] = rolled[:, :width]


def skewed(lines):
    heads, _, length = lines.shape
    width = length - LANES
    return pl.pallas_call(
        skew_kernel,
        out_shape=pltpu.HBM((heads, LANES, width), jnp.float32),
        grid=(heads,),
        in_specs=[pl.BlockSpec((1, 1, length), lambda h: (h, 0, 0))],
        out_specs=pl.BlockSpec((1, LANES, width), lambda h: (h, 0, 0)),
        name="bias_rows",
    )(lines)


def attend_kernel(
    scale, at, q_ref, k_pair, k_far, v_pair, v_far, bias_ref, own_ref, other_ref, lse_ref,
    k_ref, vt_ref, s_ref, p_ref, out_ref,
):
    tile = q_ref.shape[0]
    blocks = k_ref.shape[0] // LANES
    pair = k_pair.shape[0]
    length = at[blocks * 2]

    @pl.when(pl.program_id(1) == 0)
    def _():
        k_ref[:pair] = k_pair[...]
        k_ref[pair:] = k_far[...]
        vt_ref[:, :pair] = v_pair[...].T
        vt_ref[:, pair:] = v_far[...].T

    begin = pl.program_id(1) * tile
    s_ref[...] = lax.dot_general(
        k_ref[...], q_ref[...], (((1,), (1,)), ((), ())), preferred_element_type=jnp.float32
    )
    frame = lax.broadcasted_iota(jnp.int32, (LANES, tile), 0)
    top = jnp.full((1, tile), NEGATIVE, jnp.float32)
    for b in range(blocks):
        lanes = pl.ds(pl.multiple_of(at[b] + begin, LANES), tile)
        s = s_ref[b * LANES : (b + 1) * LANES] * (scale * LOG2E) + bias_ref[0, :, lanes]
        s = jnp.where(frame < length - at[blocks + b], s, NEGATIVE)
        s_ref[b * LANES : (b + 1) * LANES] = s
        top = jnp.maximum(top, jnp.max(s, axis=0, keepdims=True))
    total = jnp.zeros((1, tile), jnp.float32)
    for b in range(blocks):
        p = jnp.exp2(s_ref[b * LANES : (b + 1) * LANES] - top)
        total = total + jnp.sum(p, axis=0, keepdims=True)
        p_ref[b * LANES : (b + 1) * LANES] = p.astype(jnp.bfloat16)
    mixed = jnp.dot(vt_ref[...], p_ref[...], preferred_element_type=jnp.float32) / total
    out_ref[...] = mixed.T.astype(jnp.bfloat16)
    half = tile // 2
    side = at[blocks * 2 + 1]
    own_ref[...] = out_ref[pl.ds(pl.multiple_of(side * half, half), half)]
    other_ref[...] = out_ref[pl.ds(pl.multiple_of((1 - side) * half, half), half)]
    lse_ref[0] = top + jnp.log(total) * LOG2E


def attend(at, query, key, key_far, value, value_far, bias, heads, head_dim):
    queries, keys = query.shape[0], 2 * key.shape[0]
    tile = queries
    width = bias.shape[-1]
    grid_spec = pltpu.PrefetchScalarGridSpec(
        num_scalar_prefetch=1,
        grid=(heads, queries // tile),
        in_specs=[
            pl.BlockSpec((tile, head_dim), lambda h, i, at: (i, h)),
            pl.BlockSpec((keys // 2, head_dim), lambda h, i, at: (0, h)),
            pl.BlockSpec((keys // 2, head_dim), lambda h, i, at: (0, h)),
            pl.BlockSpec((keys // 2, head_dim), lambda h, i, at: (0, h)),
            pl.BlockSpec((keys // 2, head_dim), lambda h, i, at: (0, h)),
            pl.BlockSpec((1, LANES, width), lambda h, i, at: (h, 0, 0)),
        ],
        out_specs=[
            pl.BlockSpec((tile // 2, head_dim), lambda h, i, at: (0, h)),
            pl.BlockSpec((tile // 2, head_dim), lambda h, i, at: (0, h)),
            pl.BlockSpec((1, 1, tile), lambda h, i, at: (h, 0, i)),
        ],
        scratch_shapes=[
            pltpu.VMEM((keys, head_dim), jnp.bfloat16),
            pltpu.VMEM((head_dim, keys), jnp.bfloat16),
            pltpu.VMEM((keys, tile), jnp.float32),
            pltpu.VMEM((keys, tile), jnp.bfloat16),
            pltpu.VMEM((tile, head_dim), jnp.bfloat16),
        ],
    )
    return pl.pallas_call(
        functools.partial(attend_kernel, head_dim ** (-0.5)),
        out_shape=[
            pltpu.HBM((queries // 2, heads * head_dim), jnp.bfloat16),
            pltpu.HBM((queries // 2, heads * head_dim), jnp.bfloat16),
            pltpu.HBM((heads, 1, queries), jnp.float32),
        ],
        grid_spec=grid_spec,
        compiler_params=pltpu.CompilerParams(vmem_limit_bytes=24 * MIB),
        cost_estimate=cost(
            4 * heads * queries * keys * head_dim,
            heads * queries * keys,
            4 * heads * LANES * width + 4 * heads * head_dim * (queries + keys),
        ),
        name="attend",
    )(at, *[in_hbm(x) for x in (query, key, key_far, value, value_far, bias)])


def attend_back_kernel(
    scale, at, q_ref, k_pair, k_far, v_pair, v_far, da_own, da_near, wo_ref, wk_ref, wv_ref, lse_ref, bias_ref,
    dq_ref, dk_ref, dv_ref, line_ref, send_ref, far_ref,
    do_ref, all_dk, all_dv, k_ref, v_ref, kt_ref, s_ref, dp_ref, p_ref, ds_ref, skew_ref,
):
    tile = q_ref.shape[0]
    blocks = k_ref.shape[0] // LANES
    length = at[blocks * 2]
    pair = k_pair.shape[0]

    side = at[blocks * 2 + 1]
    own = da_own.shape[0]
    mine = pl.ds(pl.multiple_of(side * own, own), own)
    other = pl.ds(pl.multiple_of((1 - side) * own, own), own)
    do_ref[mine] = dot_turned(da_own[...], wo_ref[...]).astype(jnp.bfloat16)
    do_ref[other] = dot_turned(da_near[...], wo_ref[...]).astype(jnp.bfloat16)
    k_ref[:pair] = k_pair[...]
    k_ref[pair:] = k_far[...]
    v_ref[:pair] = v_pair[...]
    v_ref[pair:] = v_far[...]
    kt_ref[...] = k_ref[...].T
    skew_ref[...] = jnp.zeros_like(skew_ref)
    s_ref[...] = lax.dot_general(
        k_ref[...], q_ref[...], (((1,), (1,)), ((), ())), preferred_element_type=jnp.float32
    )
    dp_ref[...] = lax.dot_general(
        v_ref[...], do_ref[...], (((1,), (1,)), ((), ())), preferred_element_type=jnp.float32
    )
    frame = lax.broadcasted_iota(jnp.int32, (LANES, tile), 0)
    lse = lse_ref[0]
    delta = jnp.zeros((1, tile), jnp.float32)
    for b in range(blocks):
        rows = slice(b * LANES, (b + 1) * LANES)
        lanes = pl.ds(pl.multiple_of(at[b], LANES), tile)
        s = s_ref[rows] * (scale * LOG2E) + bias_ref[0, :, lanes]
        s = jnp.where(frame < length - at[blocks + b], s, NEGATIVE)
        p = jnp.exp2(s - lse)
        s_ref[rows] = p
        p_ref[rows] = p.astype(jnp.bfloat16)
        delta = delta + jnp.sum(p * dp_ref[rows], axis=0, keepdims=True)
    for b in range(blocks):
        rows = slice(b * LANES, (b + 1) * LANES)
        lanes = pl.ds(pl.multiple_of(at[b], LANES), tile)
        ds = (s_ref[rows] * (dp_ref[rows] - delta)).astype(jnp.bfloat16)
        ds_ref[rows] = ds
        skew_ref[:, lanes] += ds.astype(jnp.float32)
    dv = jnp.dot(p_ref[...], do_ref[...], preferred_element_type=jnp.float32).astype(jnp.bfloat16)
    dk = jnp.dot(ds_ref[...], q_ref[...], preferred_element_type=jnp.float32) * scale
    dk = dk.astype(jnp.bfloat16)
    dq = jnp.dot(kt_ref[...], ds_ref[...], preferred_element_type=jnp.float32) * scale
    dq_ref[...] = dq.T.astype(jnp.bfloat16)
    dk_ref[...] = dk
    dv_ref[...] = dv
    head = pl.program_id(0)
    all_dk[head] = dk[pair:]
    all_dv[head] = dv[pair:]
    lines = jnp.concatenate([skew_ref[...], jnp.zeros((LANES, LANES), jnp.float32)], axis=1)
    count = LANES // 2
    while count >= 8:
        lines = lines[count:] + pltpu.roll(lines[:count], count, 1)
        count //= 2
    line_ref[0] = lines

    @pl.when(head == pl.num_programs(0) - 1)
    def _():
        def total(rows):
            heads = all_dk.shape[0]
            d_key = jnp.concatenate([all_dk[h, rows] for h in range(heads)], axis=1)
            d_value = jnp.concatenate([all_dv[h, rows] for h in range(heads)], axis=1)
            return dot_turned(d_key, wk_ref[...]) + dot_turned(d_value, wv_ref[...])

        send_ref[...] = total(other).astype(jnp.bfloat16)
        far_ref[...] = total(mine)


def attend_back(at, query, key, key_far, value, value_far, own, near, weights, lse, bias, heads, head_dim):
    queries, keys = query.shape[0], 2 * key.shape[0]
    tokens, model = own.shape
    width = bias.shape[-1]
    blocks = keys // LANES
    column = lambda h, at: (0, h)
    half = pl.BlockSpec((keys // 2, head_dim), column)
    low = jnp.bfloat16
    wo, wk, wv = weights
    grid_spec = pltpu.PrefetchScalarGridSpec(
        num_scalar_prefetch=1,
        grid=(heads,),
        in_specs=[
            pl.BlockSpec((queries, head_dim), column), half, half, half, half,
            whole((tokens, model)), whole((tokens, model)),
            pl.BlockSpec((head_dim, model), lambda h, at: (at[2 * blocks + 1] * heads + h, 0)),
            pl.BlockSpec((model, model // 2), lambda h, at: (0, at[2 * blocks + 1])),
            pl.BlockSpec((model, model // 2), lambda h, at: (0, at[2 * blocks + 1])),
            pl.BlockSpec((1, 1, queries), lambda h, at: (h, 0, 0)),
            pl.BlockSpec((1, LANES, width), lambda h, at: (h, 0, 0)),
        ],
        out_specs=[
            pl.BlockSpec((queries, head_dim), column),
            pl.BlockSpec((keys, head_dim), column),
            pl.BlockSpec((keys, head_dim), column),
            pl.BlockSpec((1, 8, width + LANES), lambda h, at: (h, 0, 0)),
            whole((tokens, model)),
            whole((tokens, model)),
        ],
        scratch_shapes=[
            pltpu.VMEM((queries, head_dim), low),
            pltpu.VMEM((heads, keys // 2, head_dim), low),
            pltpu.VMEM((heads, keys // 2, head_dim), low),
            pltpu.VMEM((keys, head_dim), low),
            pltpu.VMEM((keys, head_dim), low),
            pltpu.VMEM((head_dim, keys), low),
            pltpu.VMEM((keys, queries), jnp.float32),
            pltpu.VMEM((keys, queries), jnp.float32),
            pltpu.VMEM((keys, queries), low),
            pltpu.VMEM((keys, queries), low),
            pltpu.VMEM((LANES, width), jnp.float32),
        ],
    )
    return pl.pallas_call(
        functools.partial(attend_back_kernel, head_dim ** (-0.5)),
        out_shape=[
            pltpu.HBM((queries, heads * head_dim), low),
            pltpu.HBM((keys, heads * head_dim), low),
            pltpu.HBM((keys, heads * head_dim), low),
            pltpu.HBM((heads, 8, width + LANES), jnp.float32),
            pltpu.HBM((tokens, model), low),
            pltpu.HBM((tokens, model), jnp.float32),
        ],
        grid_spec=grid_spec,
        compiler_params=pltpu.CompilerParams(vmem_limit_bytes=48 * MIB),
        cost_estimate=cost(
            10 * heads * queries * keys * head_dim,
            heads * queries * keys,
            4 * heads * LANES * width + 8 * heads * head_dim * (queries + keys),
        ),
        name="attend_back",
    )(
        at, *[in_hbm(x) for x in (query, key, key_far, value, value_far, own, near, wo, wk, wv, lse, bias)]
    )


def again_kernel(count, at, *refs):
    pieces, cuts = refs[:4], refs[4 : 4 + count]
    act_ref, slope_ref, rows = refs[5 + count :]
    tokens = pieces[0].shape[0]

    @pl.when(pl.program_id(0) == 0)
    def _():
        for k in range(4):
            rows[k * tokens : (k + 1) * tokens] = pieces[k][...]

    for k in range(count):
        block = cuts[k].shape[1]
        mid, slope = silu_pair(dot_turned(cuts[k][...].T, rows[...]))
        act_ref[k * block : (k + 1) * block] = mid.astype(jnp.bfloat16)
        slope_ref[k * block : (k + 1) * block] = slope.astype(jnp.bfloat16)


def column_cuts(weight, groups, parts, width):
    block = weight.shape[1] // groups // parts
    if block == width:
        return weight, lambda g, at: (0, g * parts + at[0])
    return None, lambda g, at: (0, g)


def again(place, pieces, weight, groups, dep):
    parts = len(pieces)
    tokens, model = pieces[0].shape
    inner = weight.shape[1] // parts
    width = LANES
    source, where = column_cuts(weight, groups, parts, width)
    if source is None:
        source = take_columns(weight, groups, place[0], parts)
    count = 2
    cut = inner // width // count
    return pl.pallas_call(
        functools.partial(again_kernel, count),
        grid_spec=pltpu.PrefetchScalarGridSpec(
            num_scalar_prefetch=1,
            grid=(cut,),
            in_specs=[whole((tokens, model))] * parts
            + [
                pl.BlockSpec((model, width), lambda i, at, k=k: where(i * count + k, at))
                for k in range(count)
            ]
            + [pl.BlockSpec(memory_space=pl.ANY)],
            out_specs=[pl.BlockSpec((count * width, parts * tokens), lambda i, at: (i, 0))] * 2,
            scratch_shapes=[pltpu.VMEM((parts * tokens, model), jnp.bfloat16)],
        ),
        out_shape=[pltpu.HBM((inner, parts * tokens), jnp.bfloat16)] * 2,
        compiler_params=pltpu.CompilerParams(vmem_limit_bytes=40 * MIB),
        cost_estimate=cost(
            2 * parts * tokens * model * inner,
            2 * parts * tokens * inner,
            2 * parts * tokens * (2 * inner + model) + 2 * model * inner,
        ),
        name="again",
    )(place[:1], *[in_hbm(p) for p in pieces], *([in_hbm(source)] * count), in_hbm(dep))


def store_halves(held, mine, lead, size, send_ref, keep_ref):
    for index, target in ((1 - mine, send_ref), (mine, keep_ref)):
        for k, part in enumerate(take_half(held, index, lead, size)):
            target[k * size : (k + 1) * size] = part


def grad_out_kernel(share, at, act_ref, *refs):
    pieces, dep, send_ref, keep_ref, rows, held = refs[:4], *refs[4:]
    tokens = pieces[0].shape[0]

    @pl.when(pl.program_id(0) == 0)
    def _():
        for k in range(4):
            rows[k * tokens : (k + 1) * tokens] = pieces[k][...]

    held[...] = dot(act_ref[...], rows[...]).astype(jnp.bfloat16)
    store_halves(held, at[1] & 1, held.shape[0] // share // 2, share, send_ref, keep_ref)


def grad_out_of(place, act, pieces, share, dep):
    inner, frames = act.shape
    tokens, model = pieces[0].shape
    step = 512
    return pl.pallas_call(
        functools.partial(grad_out_kernel, share),
        grid_spec=pltpu.PrefetchScalarGridSpec(
            num_scalar_prefetch=1,
            grid=(inner // step,),
            in_specs=[pl.BlockSpec((step, frames), lambda i, at: (i, 0))]
            + [whole((tokens, model))] * len(pieces)
            + [pl.BlockSpec(memory_space=pl.ANY)],
            out_specs=[pl.BlockSpec((step // 2, model), lambda i, at: (i, 0))] * 2,
            scratch_shapes=[
                pltpu.VMEM((frames, model), jnp.bfloat16), pltpu.VMEM((step, model), jnp.bfloat16)
            ],
        ),
        out_shape=[pltpu.HBM((inner // 2, model), jnp.bfloat16)] * 2,
        compiler_params=pltpu.CompilerParams(vmem_limit_bytes=40 * MIB),
        cost_estimate=cost(
            2 * frames * model * inner, 0, 2 * frames * (inner + model) + 2 * model * inner
        ),
        name="grad_out",
    )(place, in_hbm(act), *[in_hbm(p) for p in pieces], in_hbm(dep))


def grad_in_kernel(count, share, at, slope_ref, *refs):
    acts, branches, cuts = refs[:4], refs[4:8], refs[8 : 8 + count]
    dep, send_ref, keep_ref, act_rows, branch_rows, held = refs[8 + count :]
    tokens = acts[0].shape[0]

    @pl.when(pl.program_id(0) == 0)
    def _():
        for k in range(4):
            act_rows[k * tokens : (k + 1) * tokens] = acts[k][...]
            branch_rows[k * tokens : (k + 1) * tokens] = branches[k][...]

    cut = jnp.concatenate([c[...] for c in cuts], axis=0)
    d_hidden = (dot_turned(cut, branch_rows[...]) * slope_ref[...].astype(jnp.float32)).astype(jnp.bfloat16)
    held[...] = dot(d_hidden, act_rows[...]).astype(jnp.bfloat16).T
    store_halves(held, at[1] & 1, held.shape[0] // share // 2, share, send_ref, keep_ref)


def grad_in_of(place, slope, acts, branches, weight, groups, share, dep):
    inner, frames = slope.shape
    tokens, model = acts[0].shape
    parts = len(acts)
    width = LANES
    count = 4
    if weight.shape[0] // groups // parts == width:
        source, where = weight, lambda g, at: (g * parts + at[0], 0)
    else:
        source, where = take_rows(weight, groups, place[0], parts), lambda g, at: (g, 0)
    return pl.pallas_call(
        functools.partial(grad_in_kernel, count, share),
        grid_spec=pltpu.PrefetchScalarGridSpec(
            num_scalar_prefetch=1,
            grid=(inner // width // count,),
            in_specs=[pl.BlockSpec((count * width, frames), lambda i, at: (i, 0))]
            + [whole((tokens, model))] * (2 * parts)
            + [
                pl.BlockSpec((width, model), lambda i, at, k=k: where(i * count + k, at))
                for k in range(count)
            ]
            + [pl.BlockSpec(memory_space=pl.ANY)],
            out_specs=[pl.BlockSpec((model // 2, count * width), lambda i, at: (0, i))] * 2,
            scratch_shapes=[pltpu.VMEM((frames, model), jnp.bfloat16)] * 2
            + [pltpu.VMEM((model, count * width), jnp.bfloat16)],
        ),
        out_shape=[pltpu.HBM((model // 2, inner), jnp.bfloat16)] * 2,
        compiler_params=pltpu.CompilerParams(vmem_limit_bytes=48 * MIB),
        cost_estimate=cost(
            4 * frames * model * inner, 0, 2 * frames * (inner + 2 * model) + 4 * model * inner
        ),
        name="grad_in",
    )(place, in_hbm(slope), *[in_hbm(p) for p in (*acts, *branches)], *([in_hbm(source)] * count), in_hbm(dep))


def both_kernel(count, share, in_share, at, *refs):
    acts, branches = refs[:4], refs[4:8]
    ins, outs = refs[8 : 8 + count], refs[8 + count : 8 + 2 * count]
    dep, out_send, out_keep, in_send, in_keep, act_rows, branch_rows, out_held, in_held = refs[8 + 2 * count :]
    tokens = acts[0].shape[0]

    @pl.when(pl.program_id(0) == 0)
    def _():
        for k in range(4):
            act_rows[k * tokens : (k + 1) * tokens] = acts[k][...]
            branch_rows[k * tokens : (k + 1) * tokens] = branches[k][...]

    w_in = jnp.concatenate([c[...] for c in ins], axis=1).T
    w_out = jnp.concatenate([c[...] for c in outs], axis=0)
    mid, slope = silu_pair(dot_turned(w_in, act_rows[...]))
    d_hidden = (dot_turned(w_out, branch_rows[...]) * slope).astype(jnp.bfloat16)
    out_held[...] = dot(mid.astype(jnp.bfloat16), branch_rows[...]).astype(jnp.bfloat16)
    in_held[...] = dot(d_hidden, act_rows[...]).astype(jnp.bfloat16).T
    store_halves(out_held, at[1] & 1, out_held.shape[0] // share // 2, share, out_send, out_keep)
    store_halves(in_held, (at[1] >> 1) & 1, in_held.shape[0] // in_share // 2, in_share, in_send, in_keep)


def grads_of_both(place, acts, branches, w_in, w_out, groups, dep):
    tokens, model = acts[0].shape
    parts = len(acts)
    frames = parts * tokens
    inner = w_in.shape[1] // parts
    width, count = LANES, 4
    if w_in.shape[1] // groups // parts == width:
        source_in, at_in = w_in, lambda g, at: (0, g * parts + at[0])
        source_out, at_out = w_out, lambda g, at: (g * parts + at[0], 0)
    else:
        source_in, at_in = take_columns(w_in, groups, place[0], parts), lambda g, at: (0, g)
        source_out, at_out = take_rows(w_out, groups, place[0], parts), lambda g, at: (g, 0)
    step = count * width
    return pl.pallas_call(
        functools.partial(both_kernel, count, inner // groups, 2 * model // groups),
        grid_spec=pltpu.PrefetchScalarGridSpec(
            num_scalar_prefetch=1,
            grid=(inner // step,),
            in_specs=[whole((tokens, model))] * (2 * parts)
            + [pl.BlockSpec((model, width), lambda i, at, k=k: at_in(i * count + k, at)) for k in range(count)]
            + [pl.BlockSpec((width, model), lambda i, at, k=k: at_out(i * count + k, at)) for k in range(count)]
            + [pl.BlockSpec(memory_space=pl.ANY)],
            out_specs=[pl.BlockSpec((step // 2, model), lambda i, at: (i, 0))] * 2
            + [pl.BlockSpec((model // 2, step), lambda i, at: (0, i))] * 2,
            scratch_shapes=[pltpu.VMEM((frames, model), jnp.bfloat16)] * 2
            + [pltpu.VMEM((step, model), jnp.bfloat16), pltpu.VMEM((model, step), jnp.bfloat16)],
        ),
        out_shape=[pltpu.HBM((inner // 2, model), jnp.bfloat16)] * 2
        + [pltpu.HBM((model // 2, inner), jnp.bfloat16)] * 2,
        compiler_params=pltpu.CompilerParams(vmem_limit_bytes=56 * MIB),
        cost_estimate=cost(8 * frames * model * inner, 2 * frames * inner, 4 * frames * model + 8 * model * inner),
        name="grads_of_both",
    )(place, *[in_hbm(p) for p in (*acts, *branches)], *([in_hbm(source_in)] * count), *([in_hbm(source_out)] * count), in_hbm(dep))


def shards(
    features,
    lengths,
    buckets,
    gain_first,
    first_in,
    first_out,
    gain_attend,
    query_weight,
    key_weight,
    value_weight,
    output_weight,
    bias_table,
    gain_conv,
    point_in,
    depth_weight,
    batch_scale,
    batch_shift,
    point_out,
    gain_second,
    second_in,
    second_out,
    gain_final,
    cotangent,
):
    RECEIVED.clear()
    row_count, width, model = features.shape
    tokens = row_count * width
    heads, bucket_count = bias_table.shape
    head_dim = model // heads
    parts = lax.axis_size("tm")
    groups = lax.axis_size("rows")
    frames = width * parts
    half = depth_weight.shape[0] // 2
    taps = depth_weight.shape[0]
    place = lax.axis_index("tm")
    row_place = lax.axis_index("rows")
    side = place % 2
    far = place // 2
    offset = place * width
    near_heads = heads // 2
    pair = 2 * width
    places = jnp.stack([place, row_place]).astype(jnp.int32)
    info = jnp.stack([side, far, offset, lengths[0], row_place]).astype(jnp.int32)

    flat_features = features.reshape(tokens, model)
    after_first, act_first, slope_first, act_attend = first_forward(
        flat_features, gain_first, gain_attend, first_in, first_out
    )
    act_near, act_far = swap(act_attend, "tm", 1), swap(act_attend, "tm", 2)

    near_table = lax.dynamic_slice_in_dim(bias_table, side * near_heads, near_heads, 0)
    span = pair + frames
    turned = jnp.pad(buckets[::-1], (0, 1), constant_values=-1)
    window = lax.dynamic_slice_in_dim(turned, far * pair, span, 0)
    one_hot = (window[:, None] == jnp.arange(bucket_count)[None, :]).astype(jnp.float32)
    bias_lines = lax.dot_general(
        near_table, one_hot, (((1,), (1,)), ((), ())), precision=lax.Precision.HIGHEST
    )
    bias = skewed((bias_lines * LOG2E)[:, None, :])
    key_blocks = frames // LANES
    block = jnp.arange(key_blocks)
    block = (block + far * (key_blocks // 2)) % key_blocks
    at = jnp.concatenate([frames - LANES - LANES * block, LANES * block, lengths[:1], side[None]]).astype(jnp.int32)

    query, key, value = project(info, act_attend, act_near, (query_weight, key_weight, value_weight))
    act_far, act_first, key, bias = tie(act_far, act_first, key, bias)
    act_cross = swap(act_far, "tm", 1)
    act_first_near, act_first_far = swap(act_first, "tm", 1), swap(act_first, "tm", 2)
    key_far, value_far = project(info, act_far, act_cross, (key_weight, value_weight))
    own_mixed, other_mixed, lse = attend(
        at, query, key, key_far, value, value_far, bias, near_heads, head_dim
    )
    other_mixed = swap(other_mixed, "tm", 1)

    attended, after_attend, act_conv, joined_value, gate, gated, gated_first, gated_last = mix(
        info, own_mixed, other_mixed, output_weight, after_first, gain_conv, point_in, half, act_first_far
    )
    act_first_all = [act_first, act_first_near, act_first_far, swap(act_first_far, "tm", 1)]
    up = [(i, i + 1) for i in range(parts - 1)]
    down = [(j, i) for i, j in up]
    gated_before = lax.ppermute(gated_last, "tm", up)
    gated_after = lax.ppermute(gated_first, "tm", down)
    filtered, moments = filter_frames(info, gated, gated_before, gated_after, depth_weight)
    local_count = jnp.clip(lengths[0] - offset, 0, width).astype(jnp.float32)
    count, batch_mean, spread = mesh_moments(local_count, moments[0], moments[1])
    count = count[0]
    rstd_batch = lax.rsqrt(spread / count + EPS)
    stats = jnp.stack([batch_mean, rstd_batch, batch_scale, batch_shift])
    (
        act_batch, act_second, output, branch_second, grad, d_branch_send, d_branch, d_normal, second_sums,
        batch_sums, edge_first, edge_last,
    ) = second_both(
        info, filtered, stats, after_attend, cotangent.reshape(tokens, model),
        gain_second, gain_final, point_out, second_in, second_out, half, (act_first_all[3],),
    )
    output = output.reshape(row_count, width, model)

    edge_before = lax.ppermute(edge_last, "tm", up)
    edge_after = lax.ppermute(edge_first, "tm", down)
    first_step = batch_sums + swap(batch_sums, *hops()[0])
    first_step, act_second, branch_second = tie(first_step, act_second, branch_second)
    act_second_all = spread_tm(act_second)
    branch_second_far = swap(branch_second, "tm", 2)
    branch_second_near = swap(branch_second, "tm", 1)
    batch_grads = mesh_sum(first_step, hops()[1:])
    joined_send, d_joined, grad, d_attend, conv_small = conv_back(
        info, d_normal, filtered, edge_before, edge_after, stats, batch_grads / count, depth_weight,
        gated, joined_value, gate, point_in, after_attend, gain_conv, grad,
        (act_second_all[2],),
    )
    d_attend_near = swap(d_attend, "tm", 1)

    held = near_heads * head_dim
    share = model // groups
    conv_send, conv_keep = cross_grads(
        info,
        [
            ((act_conv, swap(act_conv, "tm", 1)), (d_joined, swap(joined_send, "tm", 1)), model),
            ((act_batch, swap(act_batch, "tm", 1)), (d_branch, swap(d_branch_send, "tm", 1)), held),
            ((attended, swap(attended, "tm", 1)), (d_attend, d_attend_near), held),
        ],
        deps=(branch_second_near, act_second_all[1], act_second_all[3]),
    )

    branch_second_far, conv_send = tie(branch_second_far, conv_send)
    conv_got = swap(conv_send, "tm", 2)
    branch_second_all = [
        branch_second, branch_second_near, branch_second_far, swap(branch_second_far, "tm", 1)
    ]
    out_send, out_keep, in_send, in_keep = grads_of_both(
        places, act_second_all, branch_second_all, second_in, second_out, groups, conv_keep
    )
    d_attend_near, in_keep = tie(d_attend_near, in_keep)
    second_sums_of = [RowSum(out_send, out_keep, share), RowSum(in_send, in_keep, share, True)]

    d_query, d_key, d_value, skew_lines, far_send, far_keep = attend_back(
        at, query, key, key_far, value, value_far, d_attend, d_attend_near,
        (output_weight, key_weight, value_weight), lse, bias, near_heads, head_dim,
    )
    far_mine = add(info, (far_keep, swap(far_send, "tm", 1)), jnp.bfloat16, second_sums_of[0].terms[1],
                   second_sums_of[1].terms[1])
    far_back = swap(far_mine, "tm", 2)
    conv_sum = opened(info, conv_keep, conv_got, share, far_mine)
    kept = merge(info, second_sums_of, conv_sum.terms[0])
    pair_send, pair_keep = input_back(
        info, (d_query, d_key, d_value), (0, 0, 0), (query_weight, key_weight, value_weight), width, (kept,)
    )
    attend_sum = RowSum(*cross_grads(
        info,
        [
            ((act_attend, act_near), (d_query,), held),
            ((act_attend, act_near, act_far, act_cross), (d_key,), held),
            ((act_attend, act_near, act_far, act_cross), (d_value,), held),
        ],
        split=False,
        deps=(pair_keep,),
    ), share)
    grad, branch_first, grad_gain_attend = branch_of(
        info, pair_keep, swap(pair_send, "tm", 1), far_back, after_first, gain_attend, grad,
        (attend_sum.terms[0], conv_sum.terms[1], second_sums_of[0].terms[1]),
    )
    branch_far = swap(branch_first, "tm", 2)
    grad_features, grad_gain_first = first_backward(
        info, grad, flat_features, gain_first, slope_first, first_in, first_out, ()
    )
    grad_features = grad_features.reshape(row_count, width, model)
    mid_first, slope_first_part = again(places, act_first_all, first_in, groups, grad_gain_first)
    kept = merge(info, [*second_sums_of, conv_sum], mid_first)
    branch_far, conv_sum.terms[0] = tie(branch_far, kept)
    branch_first_all = [branch_first, swap(branch_first, "tm", 1), branch_far, swap(branch_far, "tm", 1)]
    first_out_sum = RowSum(
        *grad_out_of(places, mid_first, branch_first_all, share, conv_sum.terms[0]), share
    )
    late_sums = [conv_sum, attend_sum]
    kept = merge(info, late_sums, first_out_sum.terms[0], *[t.terms[1] for t in second_sums_of])
    second_piece = joined(info, second_sums_of, kept)
    second_pieces = spread_tm(second_piece)
    kept = second_piece
    table_lines = sum(jnp.pad(skew_lines[:, r], ((0, 0), (7 - r, 0)))[:, :span] for r in range(8))
    near_grad = lax.dot_general(
        table_lines, one_hot, (((1,), (0,)), ((), ())), precision=lax.Precision.HIGHEST
    )
    grad_table = lax.dynamic_update_slice_in_dim(
        jnp.zeros((heads, bucket_count), jnp.float32), near_grad, side * near_heads, 0
    )
    small = jnp.concatenate(
        [
            grad_gain_first,
            grad_gain_attend,
            second_sums,
            conv_small,
            jnp.pad(grad_table.reshape(1, -1), ((0, 0), (0, model - heads * bucket_count))),
        ],
        axis=0,
    )
    first_in_sum = RowSum(*grad_in_of(
        places, slope_first_part, act_first_all, branch_first_all, first_out, groups, share, kept,
    ), share)

    def hop(step, value, kept):
        value = value + swap(value, *step)
        return tie(value, kept)

    steps = hops()
    kept = merge(info, [first_out_sum, attend_sum], first_in_sum.terms[0])
    conv_piece = joined(info, [conv_sum], kept)
    conv_pieces = spread_tm(conv_piece)
    small, first_in_sum.terms[0] = hop(steps[0], small, first_in_sum.terms[0])
    kept = merge(info, [first_in_sum], conv_piece)
    kept = merge(info, [first_out_sum], kept)
    small, first_out_sum.terms[0] = hop(steps[1], small, kept)
    for step in steps[2:-1]:
        small, first_out_sum.terms[0] = hop(step, small, first_out_sum.terms[0])
    kept = merge(info, [first_in_sum], first_out_sum.terms[0])
    attend_piece = joined(info, [attend_sum], kept)
    attend_got = swap(attend_piece, "tm", 2)
    first_out_piece = joined(info, [first_out_sum], attend_piece)
    first_out_pieces = spread_tm(first_out_piece)
    attend_piece = join(info, [[attend_piece, attend_got]], first_out_piece)
    small, attend_piece = hop(steps[-1], small, attend_piece)
    attend_pieces = [attend_piece, swap(attend_piece, "tm", 1)]
    gains = lax.dynamic_slice_in_dim(small[:5], row_place * share, share, 1)
    grad_depth = small[5 : 5 + taps]
    grad_table = small[5 + taps, : heads * bucket_count].reshape(heads, bucket_count)

    relative = jnp.arange(parts) ^ place
    crossed = (relative % 2) * 2 + relative // 2
    quarter = model // parts

    def lay_rows(pieces):
        size = pieces[0].shape[0]
        out = jnp.zeros((parts, size, model), jnp.float32)
        for k in range(parts):
            out = lax.dynamic_update_index_in_dim(out, pieces[k].astype(jnp.float32), place ^ k, 0)
        return out.reshape(parts * size, model)

    (grad_second_in,) = lay_columns([p[:, model:] for p in second_pieces], (model,), groups, relative)
    grad_second_out = lay_rows([p[:, :model] for p in second_pieces])
    grad_point_in, grad_point_out, grad_output = lay_columns(
        conv_pieces, (2 * quarter, quarter, quarter), 1, crossed
    )
    grad_query, grad_key, grad_value = lay_columns(
        attend_pieces, (2 * quarter,) * 3, 1, jnp.stack([side, 1 - side])
    )
    first_in_pieces = spread_tm(
        joined(info, [first_in_sum], grad_second_in, grad_second_out, grad_point_out, grad_query)
    )
    grad_first_out = lay_rows(first_out_pieces)
    (grad_first_in,) = lay_columns(first_in_pieces, (model,), groups, relative)
    return (
        output,
        grad_features,
        gains[0],
        grad_first_in,
        grad_first_out,
        gains[1],
        grad_query,
        grad_key,
        grad_value,
        grad_output,
        grad_table,
        gains[4],
        grad_point_in,
        grad_depth,
        batch_grads[1],
        batch_grads[0],
        grad_point_out,
        gains[3],
        grad_second_in,
        grad_second_out,
        gains[2],
    )


def solution(mesh):
    rows3, rows2, rows1 = P("rows", "tm", None), P("rows", None), P("rows")
    in_specs = (rows3, rows1) + (P(),) * 20 + (rows3,)
    out_specs = (
        rows3, rows3, rows1, rows2, rows2, rows1, rows2, rows2, rows2, rows2, P(),
        rows1, rows2, P(), P(), P(), rows2, rows1, rows2, rows2, rows1,
    )
    return jax.shard_map(shards, mesh=mesh, in_specs=in_specs, out_specs=out_specs, check_vma=False)
```
